512 devices in a mesh: elem: 32 (over x, y), four: 16 (over z, core).
Axes of the slice: x: 4, y: 8, z: 8, core: 2. Of those that a mesh axis runs over, the one named last changes fastest.
Arguments:
- adjoint_velocity: float32 [3, 2, 11, 1441792], P(None, None, None, ('elem', 'four')), may hold values from -6 to 6
- base_flow: bfloat16 [3, 2, 11, 1441792], P(None, None, None, ('elem', 'four')), may hold values from -6 to 6
- column_widths: float32 [512], P('elem'), may hold values from 0.03 to 0.65
- row_heights: float32 [2], replicated, may hold values from 0.06 to 0.18
- base_phase: int32 [1], replicated, may hold values from 0 to 255
Outputs:
- adjoint_next: float32 [3, 2, 11, 1441792], P(None, None, None, ('elem', 'four'))
The draws below stay inside these ranges and needn't reach their ends.
All inputs are finite; a program needn't handle non-finite values.
Results may differ from the reference program's by a relative error of at most 0.0003.
Values sent between devices are 32-bit elements; how exact they have to be, the bound alone decides.
No kernel may reach another device: no remote copies, remote signals or barrier semaphores. Data moves between devices by JAX's collectives and lax.ppermute only.
A program may use at most 128 MiB of HBM per device.

```python
import math
import jax
import jax.numpy as jnp
import numpy as np
from jax import lax

Q = 11
PLANES = 256
EX_DEV = 16
EY = 2
ITERS = 3
EX = 512
XN = 5632
N_ELEM = 32


def draw_column_widths(key, part):
    position = jnp.arange(EX, dtype=jnp.float32) / max(EX - 1, 1)
    rough = jax.random.uniform(key, (EX,), jnp.float32, 0.75, 1.35)
    return 0.06 * jnp.power(3.0, position) * rough


def block_scale(key, shape, split, low, top_value):
    factor_of = 1.0
    for dim, blocks in split:
        draws = jax.random.uniform(jax.random.fold_in(jax.random.fold_in(key, 6), dim), (blocks,), jnp.float32, low / len(split), top_value / len(split))
        factor_of = factor_of * jnp.repeat(jnp.exp(draws), shape[dim] // blocks).reshape((-1,) + (1,) * (len(shape) - 1 - dim))
    return factor_of


def bell_draw(rng, dims, width, most, cuts=(), kind=jnp.bfloat16):
    factor_of = block_scale(rng, dims, cuts, -0.22, 0.18) if cuts else 1.0
    array = jax.random.normal(rng, dims, jnp.float32) * width * factor_of
    return jnp.minimum(jnp.maximum(array, -most), most).astype(kind)


def setup_inputs(seed: int = 0) -> dict:
    seeds = jax.random.split(jax.random.key(seed), 6)
    adjoint_velocity = bell_draw(seeds[0], (3, EY, Q, N_ELEM * PLANES * EX_DEV * Q), 1.0, 6.0, ((3, 512),), jnp.float32)
    base_flow = bell_draw(seeds[1], (3, EY, Q, XN * PLANES), 1.0, 6.0, ((3, 512),))
    column_widths = draw_column_widths(jax.random.fold_in(seeds[5], 71), 0)
    row_heights = jnp.clip(jnp.exp(jax.random.uniform(seeds[3], (EY,), jnp.float32, math.log(0.06), math.log(0.18))), 0.06, 0.18)
    base_phase = jax.random.randint(seeds[4], (1,), 0, PLANES).astype(jnp.int32)
    return dict(adjoint_velocity=adjoint_velocity, base_flow=base_flow, column_widths=column_widths, row_heights=row_heights, base_phase=base_phase)


NU = 0.005
DT = 0.01
SIGMA = 1.0 / (NU * DT)
HIGHEST = lax.Precision.HIGHEST

def legendre_values(points, node_count):
    table_rows = np.zeros((points.shape[0], node_count))
    table_rows[:, 0] = 1.0
    table_rows[:, 1] = points
    for degree_now in range(2, node_count):
        table_rows[:, degree_now] = ((2 * degree_now - 1) * points * table_rows[:, degree_now - 1] - (degree_now - 1) * table_rows[:, degree_now - 2]) / degree_now
    return table_rows

def gll_tables(node_count):
    degree = node_count - 1
    points = np.cos(np.pi * np.arange(node_count) / degree)
    for newton_step in range(60):
        legendre = legendre_values(points, node_count)
        points = points - (points * legendre[:, degree] - legendre[:, degree - 1]) / (node_count * legendre[:, degree])
    legendre = legendre_values(points, node_count)
    weights = 2.0 / (degree * node_count * legendre[:, degree] ** 2)
    points = points[::-1]
    weights = weights[::-1]
    end_values = legendre[::-1, degree]
    derivative = np.zeros((node_count, node_count))
    for row_index in range(node_count):
        for column in range(node_count):
            if row_index != column:
                derivative[row_index, column] = end_values[row_index] / (end_values[column] * (points[row_index] - points[column]))
    derivative[0, 0] = -degree * node_count / 4.0
    derivative[degree, degree] = degree * node_count / 4.0
    return (jnp.asarray(derivative.astype(np.float32)), jnp.asarray(weights.astype(np.float32)))

def fourier_table(plane_count):
    positions = np.arange(plane_count)
    basis_rows = np.zeros((plane_count, plane_count))
    basis_rows[0] = 1.0 / np.sqrt(plane_count)
    basis_rows[1] = np.cos(np.pi * positions) / np.sqrt(plane_count)
    for wave_index in range(1, plane_count // 2):
        basis_rows[2 * wave_index] = np.sqrt(2.0 / plane_count) * np.cos(2.0 * np.pi * wave_index * positions / plane_count)
        basis_rows[2 * wave_index + 1] = np.sqrt(2.0 / plane_count) * np.sin(2.0 * np.pi * wave_index * positions / plane_count)
    wave_counts = np.arange(plane_count) // 2
    wave_counts[1] = plane_count // 2
    wave_counts[0] = 0
    wavenumbers = 2.0 * np.pi * wave_counts / (plane_count / 64.0)
    rotate = np.zeros((plane_count, plane_count))
    for wave_index in range(1, plane_count // 2):
        rotate[2 * wave_index, 2 * wave_index + 1] = wavenumbers[2 * wave_index]
        rotate[2 * wave_index + 1, 2 * wave_index] = -wavenumbers[2 * wave_index]
    span_slope = basis_rows.T @ rotate @ basis_rows
    return (jnp.asarray(basis_rows.astype(np.float32)), jnp.asarray(wavenumbers.astype(np.float32)), jnp.asarray(span_slope.astype(np.float32)))

def slope_width(values, widths, derivative):
    node_count = derivative.shape[0]
    shaped = values.reshape(values.shape[:-1] + (widths.shape[0], node_count))
    turned = jnp.einsum('km,...xm->...xk', derivative, shaped, precision=HIGHEST)
    return (turned * (2.0 / widths)[:, None]).reshape(values.shape)

def slope_height(values, heights, derivative):
    turned = jnp.einsum('km,...ympx->...ykpx', derivative, values, precision=HIGHEST)
    return turned * (2.0 / heights).reshape(-1, 1, 1, 1)

def slope_span(values, span_slope):
    return jnp.einsum('zw,...wx->...zx', span_slope, values, precision=HIGHEST)

def gradients(values, widths, heights, derivative, span_slope):
    return (slope_width(values, widths, derivative), slope_height(values, heights, derivative), slope_span(values, span_slope))

def advect(line_values, slopes, base_now, base_slopes):
    pieces = []
    for component in range(3):
        summed = base_now[0] * slopes[0][component] + base_now[1] * slopes[1][component] + base_now[2] * slopes[2][component]
        summed = summed - (line_values[0] * base_slopes[component][0] + line_values[1] * base_slopes[component][1] + line_values[2] * base_slopes[component][2])
        pieces.append(summed)
    return jnp.stack(pieces)

def to_lines(basis_rows, coeffs):
    return jnp.einsum('jz,...jx->...zx', basis_rows, coeffs, precision=HIGHEST)

def to_coeffs(basis_rows, line_values):
    return jnp.einsum('jz,...zx->...jx', basis_rows, line_values, precision=HIGHEST)

def mass_factor(widths, heights, weights):
    node_count = weights.shape[0]
    width_b = widths.reshape(1, 1, 1, -1, 1)
    height_b = heights.reshape(-1, 1, 1, 1, 1)
    return width_b * height_b * 0.25 * weights.reshape(1, node_count, 1, 1, 1) * weights.reshape(1, 1, 1, 1, node_count)

def local_operator(values, widths, heights, weights, derivative, wave_sq):
    node_count = derivative.shape[0]
    column_count = widths.shape[0]
    shaped = values.reshape(values.shape[:-1] + (column_count, node_count))
    height_b = heights.reshape(-1, 1, 1, 1, 1)
    width_b = widths.reshape(1, 1, 1, column_count, 1)
    weight_y = weights.reshape(1, node_count, 1, 1, 1)
    weight_x = weights.reshape(1, 1, 1, 1, node_count)
    along_x = jnp.einsum('km,...xm->...xk', derivative, shaped, precision=HIGHEST) * weight_x
    back_x = jnp.einsum('km,...xk->...xm', derivative, along_x, precision=HIGHEST)
    along_y = jnp.einsum('km,...ympxq->...ykpxq', derivative, shaped, precision=HIGHEST) * weight_y
    back_y = jnp.einsum('km,...ykpxq->...ympxq', derivative, along_y, precision=HIGHEST)
    wave_b = wave_sq.reshape(1, 1, -1, 1, 1)
    summed = height_b / width_b * weight_y * back_x + width_b / height_b * weight_x * back_y
    summed = summed + (wave_b + SIGMA) * (width_b * height_b * 0.25) * weight_y * weight_x * shaped
    return summed.reshape(values.shape)

def assemble(values, left_ghost, right_ghost, node_count):
    shaped = values.reshape(values.shape[:-1] + (values.shape[-1] // node_count, node_count))
    first_col = shaped[..., 0]
    last_col = shaped[..., node_count - 1]
    from_left = jnp.concatenate([left_ghost[..., None], last_col[..., :-1]], axis=-1)
    from_right = jnp.concatenate([first_col[..., 1:], right_ghost[..., None]], axis=-1)
    shaped = jnp.concatenate([(first_col + from_left)[..., None], shaped[..., 1:node_count - 1], (last_col + from_right)[..., None]], axis=-1)
    joined = shaped.reshape(values.shape)
    first_row = joined[..., :, 0, :, :]
    last_row = joined[..., :, node_count - 1, :, :]
    shared = last_row[..., :-1, :, :] + first_row[..., 1:, :, :]
    new_first = jnp.concatenate([first_row[..., :1, :, :], shared], axis=-3)
    new_last = jnp.concatenate([shared, last_row[..., -1:, :, :]], axis=-3)
    return jnp.concatenate([new_first[..., :, None, :, :], joined[..., :, 1:node_count - 1, :, :], new_last[..., :, None, :, :]], axis=-3)

def inner_product(left, right, weight):
    return lax.optimization_barrier(jnp.sum(left * right * weight, axis=(-4, -3, -1), keepdims=True))

def reference(adjoint_velocity, base_flow, column_widths, row_heights, base_phase):
    part_nodes = EX_DEV * Q
    packed = adjoint_velocity.reshape(3, EY, Q, N_ELEM, PLANES, part_nodes)
    adjoint_full = jnp.transpose(packed, (0, 1, 2, 4, 3, 5)).reshape(3, EY, Q, PLANES, XN)
    base_full = jnp.transpose(base_flow.reshape(3, EY, Q, XN, PLANES), (0, 1, 2, 4, 3))
    basis_rows, wavenumbers, span_slope = fourier_table(PLANES)
    derivative, weights = gll_tables(Q)
    rolled = jnp.roll(base_full, base_phase[0], axis=3)
    zero_index = jnp.zeros((), jnp.int32)

    def column_step(column_index, accumulated):
        offset = (column_index * Q).astype(jnp.int32)
        coeffs = lax.dynamic_slice_in_dim(adjoint_full, offset, Q, axis=4)
        base_now = lax.dynamic_slice_in_dim(rolled, offset, Q, axis=4).astype(jnp.float32)
        width_here = lax.dynamic_slice_in_dim(column_widths, column_index.astype(jnp.int32), 1)
        line_values = to_lines(basis_rows, coeffs)
        slopes = gradients(line_values, width_here, row_heights, derivative, span_slope)
        base_slopes = gradients(base_now, width_here, row_heights, derivative, span_slope)
        returned = to_coeffs(basis_rows, advect(line_values, slopes, base_now, base_slopes))
        source = SIGMA * coeffs + returned / NU
        shaped = source.reshape(source.shape[:-1] + (1, Q))
        local_part = (mass_factor(width_here, row_heights, weights) * shaped).reshape(source.shape)
        return lax.dynamic_update_slice_in_dim(accumulated, local_part, offset, axis=4)
    local_side = lax.fori_loop(0, EX, column_step, jnp.zeros(adjoint_full.shape, jnp.float32))
    ghost = jnp.zeros(local_side.shape[:-1], jnp.float32)
    right_full = assemble(local_side, ghost, ghost, Q)
    node_x = jnp.arange(EX * Q, dtype=jnp.int32)
    place_x = node_x % Q
    column_x = node_x // Q
    shared_x = (place_x == 0) & (column_x > 0) | (place_x == Q - 1) & (column_x < EX - 1)
    node_y = jnp.arange(EY * Q, dtype=jnp.int32)
    place_y = node_y % Q
    row_y = node_y // Q
    shared_y = (place_y == 0) & (row_y > 0) | (place_y == Q - 1) & (row_y < EY - 1)
    mult_x = 1.0 + shared_x.astype(jnp.float32)
    mult_y = 1.0 + shared_y.astype(jnp.float32)
    weight = (1.0 / (mult_y[:, None] * mult_x[None, :])).reshape(EY, Q, 1, EX * Q)
    blocks = PLANES // 16
    wave_sq_all = wavenumbers * wavenumbers
    ghost_block = jnp.zeros((EY, Q, 16), jnp.float32)

    def helmholtz(values, wave_sq):
        return assemble(local_operator(values, column_widths, row_heights, weights, derivative, wave_sq), ghost_block, ghost_block, Q)

    def solve_block(job_index):
        component = (job_index // blocks).astype(jnp.int32)
        block_index = (job_index % blocks).astype(jnp.int32)
        right_side = lax.dynamic_slice(right_full, (component, zero_index, zero_index, block_index * 16, zero_index), (1, EY, Q, 16, EX * Q))[0]
        wave_sq = lax.dynamic_slice_in_dim(wave_sq_all, block_index * 16, 16)
        solution = jnp.zeros_like(right_side)
        residual = right_side
        direction = right_side
        norm_now = inner_product(residual, residual, weight)
        for iteration in range(ITERS):
            image_vec = helmholtz(direction, wave_sq)
            step_size = norm_now / inner_product(direction, image_vec, weight)
            solution = solution + step_size * direction
            residual = residual - step_size * image_vec
            norm_next = inner_product(residual, residual, weight)
            direction = residual + norm_next / norm_now * direction
            norm_now = norm_next
        return solution
    solved = lax.map(solve_block, jnp.arange(3 * blocks, dtype=jnp.int32))
    solved = solved.reshape(3, blocks, EY, Q, 16, EX * Q)
    solved = jnp.transpose(solved, (0, 2, 3, 1, 4, 5)).reshape(3, EY, Q, PLANES, N_ELEM, part_nodes)
    return jnp.transpose(solved, (0, 1, 2, 4, 3, 5)).reshape(3, EY, Q, N_ELEM * PLANES * part_nodes)
```

```python
import jax
import jax.numpy as jnp
import numpy as np
from jax import lax
from jax.experimental import pallas as pl
from jax.experimental.pallas import tpu as pltpu
from jax.sharding import PartitionSpec as P

Q = 11
PLANES = 256
PEERS = 16
LOCAL = 16
COLUMNS = 16
GHOST = 3
ROWS = 21
NODES = Q * Q
LANES = 128
NU = 0.005
DT = 0.01
SIGMA = 1.0 / (NU * DT)
HIGHEST = lax.Precision.HIGHEST
F32 = jnp.float32
BF16 = jnp.bfloat16


def legendre_values(points, node_count):
    table_rows = np.zeros((points.shape[0], node_count))
    table_rows[:, 0] = 1.0
    table_rows[:, 1] = points
    for degree_now in range(2, node_count):
        table_rows[:, degree_now] = (
            (2 * degree_now - 1) * points * table_rows[:, degree_now - 1]
            - (degree_now - 1) * table_rows[:, degree_now - 2]
        ) / degree_now
    return table_rows


def gll_tables(node_count):
    degree = node_count - 1
    points = np.cos(np.pi * np.arange(node_count) / degree)
    for newton_step in range(60):
        legendre = legendre_values(points, node_count)
        points = points - (points * legendre[:, degree] - legendre[:, degree - 1]) / (
            node_count * legendre[:, degree]
        )
    legendre = legendre_values(points, node_count)
    weights = 2.0 / (degree * node_count * legendre[:, degree] ** 2)
    points = points[::-1]
    weights = weights[::-1]
    end_values = legendre[::-1, degree]
    derivative = np.zeros((node_count, node_count))
    for row_index in range(node_count):
        for column in range(node_count):
            if row_index != column:
                derivative[row_index, column] = end_values[row_index] / (
                    end_values[column] * (points[row_index] - points[column])
                )
    derivative[0, 0] = -degree * node_count / 4.0
    derivative[degree, degree] = degree * node_count / 4.0
    return derivative, weights


def fourier_table(plane_count):
    positions = np.arange(plane_count)
    basis_rows = np.zeros((plane_count, plane_count))
    basis_rows[0] = 1.0 / np.sqrt(plane_count)
    basis_rows[1] = np.cos(np.pi * positions) / np.sqrt(plane_count)
    for wave_index in range(1, plane_count // 2):
        angle = 2.0 * np.pi * wave_index * positions / plane_count
        basis_rows[2 * wave_index] = np.sqrt(2.0 / plane_count) * np.cos(angle)
        basis_rows[2 * wave_index + 1] = np.sqrt(2.0 / plane_count) * np.sin(angle)
    wave_counts = np.arange(plane_count) // 2
    wave_counts[1] = plane_count // 2
    wave_counts[0] = 0
    wavenumbers = 2.0 * np.pi * wave_counts / (plane_count / 64.0)
    rotate = np.zeros((plane_count, plane_count))
    for wave_index in range(1, plane_count // 2):
        rotate[2 * wave_index, 2 * wave_index + 1] = wavenumbers[2 * wave_index]
        rotate[2 * wave_index + 1, 2 * wave_index] = -wavenumbers[2 * wave_index]
    return basis_rows, rotate.T @ basis_rows, basis_rows.T @ rotate @ basis_rows


def halves(array):
    high = np.asarray(array, np.float32).astype(jnp.bfloat16)
    low = (np.asarray(array, np.float64) - high.astype(np.float64)).astype(jnp.bfloat16)
    return high, low


def split(value):
    high = value.astype(BF16)
    return high, (value - high.astype(F32)).astype(BF16)


def dot(left, right):
    return jnp.dot(left, right, preferred_element_type=F32)


def dot_full(left, right):
    return jnp.dot(left, right, precision=HIGHEST, preferred_element_type=F32)


def lane_ids(shape):
    return lax.broadcasted_iota(jnp.int32, shape, len(shape) - 1)


def turn(value, shift):
    shift = shift % LANES
    return value if shift == 0 else pltpu.roll(value, shift, value.ndim - 1)


def block_transpose(arrays, count):
    lane = lane_ids(arrays[0].shape)
    turned = [turn(array, Q * k) for k, array in enumerate(arrays)]
    results = []
    for place in range(count):
        distance = (lane - Q * place) & (LANES - 1)
        chosen = turned[0]
        for k in range(1, len(turned)):
            chosen = jnp.where(distance >= Q * k, turned[k], chosen)
        chosen = jnp.where(distance < NODES, chosen, 0.0)
        results.append(turn(chosen, -Q * place))
    return results


def pack_body(in_ref, out_ref, scr0, scr1):
    lane = lane_ids((Q, LANES))
    scratches = (scr0, scr1)
    for j in range(LOCAL):
        for t in range(2):
            offset = j * COLUMNS * Q + NODES * t
            tile, shift = offset // LANES, offset % LANES
            first = in_ref[0, 0, :, tile * LANES : (tile + 1) * LANES]
            if shift and tile + 1 < COLUMNS * Q * LOCAL // LANES:
                second = in_ref[0, 0, :, (tile + 1) * LANES : (tile + 2) * LANES]
                first = jnp.where(lane >= shift, first, second)
            scratches[t][j * 16 : j * 16 + Q, :] = turn(first, -shift)
    for t in range(2):
        rows = [scratches[t][pl.ds(qy, LOCAL, stride=16), :] for qy in range(Q)]
        for place, value in enumerate(block_transpose(rows, Q if t == 0 else COLUMNS - Q)):
            out_ref[Q * t + place, 0, 0] = value


def pack(adjoint):
    return pl.pallas_call(
        pack_body,
        grid=(6,),
        in_specs=[pl.BlockSpec((1, 1, Q, COLUMNS * Q * LOCAL), lambda i: (i // 2, i % 2, 0, 0))],
        out_specs=pl.BlockSpec((PEERS, 1, 1, LOCAL, LANES), lambda i: (0, i // 2, i % 2, 0, 0)),
        out_shape=jax.ShapeDtypeStruct((PEERS, 3, 2, LOCAL, LANES), F32),
        scratch_shapes=[pltpu.VMEM((256, LANES), F32)] * 2,
        name="pack",
    )(adjoint)


def base_body(ints, widths, heights, base_ref, table_ref, stack_ref, dzh_ref, dzl_ref,
              field_ref, fgh_ref, fgl_ref, fh_ref, fl_ref, scr):
    step = pl.program_id(0)

    @pl.when(step == 0)
    def _():
        scr[...] = jnp.zeros_like(scr)
        rows = pltpu.roll(table_ref[...], (PLANES - ints[1]) % PLANES, 0)
        for k in range(2):
            high, low = split(rows[:, k * PLANES : (k + 1) * PLANES])
            fgh_ref[k * PLANES : (k + 1) * PLANES, :] = high
            fgl_ref[k * PLANES : (k + 1) * PLANES, :] = low
        high, low = split(jnp.transpose(rows[:, :PLANES]))
        fh_ref[...] = high
        fl_ref[...] = low

    for qx in range(Q):
        part = base_ref[0, 0, :, qx * PLANES : (qx + 1) * PLANES]
        scr[qx * 16 : qx * 16 + Q, :] = part
        scr[176 + qx * 16 : 176 + qx * 16 + Q, :] = part
    mixed = lax.dot_general(
        scr[...], stack_ref[...], (((0,), (0,)), ((), ())), preferred_element_type=F32
    )
    plain = mixed[:, :LANES]
    field_ref[0, 0, 0] = plain
    field_ref[1, 0, 0] = mixed[:, LANES : 2 * LANES] * (2.0 / widths[ints[0]])
    field_ref[2, 0, 0] = mixed[:, 2 * LANES :] * (2.0 / heights[step % 2])
    exact = plain.astype(BF16)
    field_ref[3, 0, 0] = dot(dzh_ref[...], exact) + dot(dzl_ref[...], exact)


def base_stage(ints, widths, heights, base, table, stack, dz_high, dz_low):
    smem = pl.BlockSpec(memory_space=pltpu.SMEM)

    def whole(shape):
        return pl.BlockSpec(shape, lambda i: (0,) * len(shape))

    return pl.pallas_call(
        base_body,
        grid=(6,),
        in_specs=[
            smem, smem, smem,
            pl.BlockSpec((1, 1, Q, Q * PLANES), lambda i: (i // 2, i % 2, 0, 0)),
            whole(table.shape), whole(stack.shape), whole(dz_high.shape), whole(dz_low.shape),
        ],
        out_specs=[
            pl.BlockSpec((4, 1, 1, PLANES, LANES), lambda i: (0, i // 2, i % 2, 0, 0)),
            whole((2 * PLANES, PLANES)), whole((2 * PLANES, PLANES)),
            whole((PLANES, PLANES)), whole((PLANES, PLANES)),
        ],
        out_shape=[
            jax.ShapeDtypeStruct((4, 3, 2, PLANES, LANES), F32),
            jax.ShapeDtypeStruct((2 * PLANES, PLANES), BF16),
            jax.ShapeDtypeStruct((2 * PLANES, PLANES), BF16),
            jax.ShapeDtypeStruct((PLANES, PLANES), BF16),
            jax.ShapeDtypeStruct((PLANES, PLANES), BF16),
        ],
        scratch_shapes=[pltpu.VMEM((352, PLANES), BF16)],
        name="base_stage",
    )(ints, widths, heights, base, table, stack, dz_high, dz_low)


def lines_body(ints, widths, heights, in_ref, field_ref, fgh_ref, fgl_ref, fh_ref, fl_ref,
               dh_ref, dl_ref, mass_ref, out_ref):
    ey = pl.program_id(0)
    width, height = widths[ints[0]], heights[ey]
    coeffs = [in_ref[:, c, 0].reshape(PLANES, LANES) for c in range(3)]
    high, low = split(jnp.concatenate(coeffs, axis=1))
    both = dot(fgh_ref[...], high) + dot(fgh_ref[...], low) + dot(fgl_ref[...], high)
    lines = [both[:PLANES, c * LANES : (c + 1) * LANES] for c in range(3)]
    slopes = [None, None, [both[PLANES:, c * LANES : (c + 1) * LANES] for c in range(3)]]
    high, low = split(jnp.concatenate(lines, axis=0))
    plane = dot(high, dh_ref[...]) + dot(low, dh_ref[...]) + dot(high, dl_ref[...])
    per_c = [plane[c * PLANES : (c + 1) * PLANES] for c in range(3)]
    slopes[0] = [part[:, :LANES] * (2.0 / width) for part in per_c]
    slopes[1] = [part[:, LANES:] * (2.0 / height) for part in per_c]
    pieces = []
    for c in range(3):
        total = field_ref[0, 0, 0] * slopes[0][c]
        for d in range(1, 3):
            total = total + field_ref[0, d, 0] * slopes[d][c]
        for d in range(3):
            total = total - lines[d] * field_ref[1 + c, d, 0]
        pieces.append(total)
    high, low = split(jnp.concatenate(pieces, axis=1))
    hat = dot(fh_ref[...], high) + dot(fh_ref[...], low) + dot(fl_ref[...], high)
    mass = mass_ref[...] * (width * height * 0.25)
    lane = lane_ids((PLANES, LANES))
    for c in range(3):
        source = SIGMA * coeffs[c] + hat[:, c * LANES : (c + 1) * LANES] * (1.0 / NU)
        value = jnp.where(lane < NODES, mass * source, width)
        out_ref[:, c, 0] = value.reshape(PEERS, LOCAL, LANES)


def lines_stage(ints, widths, heights, arrived, fields, tables, d_high, d_low, mass):
    smem = pl.BlockSpec(memory_space=pltpu.SMEM)

    def whole(array):
        return pl.BlockSpec(array.shape, lambda i: (0,) * array.ndim)

    block = pl.BlockSpec((PEERS, 3, 1, LOCAL, LANES), lambda i: (0, 0, i, 0, 0))
    return pl.pallas_call(
        lines_body,
        grid=(2,),
        in_specs=[
            smem, smem, smem, block,
            pl.BlockSpec((4, 3, 1, PLANES, LANES), lambda i: (0, 0, i, 0, 0)),
        ] + [whole(a) for a in tables] + [whole(d_high), whole(d_low), whole(mass)],
        out_specs=block,
        out_shape=jax.ShapeDtypeStruct((PEERS, 3, 2, LOCAL, LANES), F32),
        name="lines_stage",
    )(ints, widths, heights, arrived, fields, *tables, d_high, d_low, mass)


def krylov_body(stiff_y, weights, ints, heights, own_ref, left_ref, right_ref, kb_ref, join_ref, wx_ref,
                v0_ref, v1_ref, v2_ref, mom_ref, loc, kxs, kbs, vec, prod, tmp):
    comp = pl.program_id(0)
    column_refs = (
        [left_ref.at[k] for k in range(GHOST)]
        + [own_ref.at[k] for k in range(COLUMNS)]
        + [right_ref.at[k] for k in range(GHOST)]
    )

    @pl.when(comp == 0)
    def _():
        lane = lane_ids((8, LANES))
        for t in range(2):
            here = jnp.zeros((8, LANES), F32)
            for place in range(Q):
                width = column_refs[Q * t + place][0, 0, 0:8, NODES : NODES + 1]
                inside = (lane >= Q * place) & (lane < Q * place + Q)
                here = jnp.where(inside, width, here)
            vec[0, :, t * LANES : (t + 1) * LANES] = here
        here = vec[0]
        inverse = jnp.where(here > 0.0, 1.0 / jnp.where(here > 0.0, here, 1.0), 0.0)
        line = lane_ids((8, 2 * LANES))
        own = ((line >= GHOST * Q) & (line < NODES)) | (
            (line >= LANES) & (line < LANES + (Q - GHOST) * Q)
        )
        own = own.astype(F32)
        mass_x = here * wx_ref[...]
        vec[1] = dot_full(mass_x, join_ref[...])
        vec[2] = mass_x * own
        place = jnp.where(line >= LANES, line - LANES, line)
        place = place - Q * ((place * 5958) >> 16)
        edge = (place == 0) | (place == Q - 1)
        left_end = (line == GHOST * Q) & (pltpu.roll(here, 1, 1) == 0.0)
        right_end = (line == LANES + (Q - GHOST) * Q - 1) & (
            pltpu.roll(here, 2 * LANES - 1, 1) == 0.0
        )
        shared = edge & jnp.logical_not(left_end | right_end)
        vec[3] = own * jnp.where(shared, 0.5, 1.0)
        scaled = kb_ref[...] * inverse[0:1]
        kxs[...] = dot_full(scaled, join_ref[...])
        kbs[...] = scaled * own[0:1]

    for t in range(2):
        before = None
        for ey in range(2):
            chunks = [column_refs[Q * t + place][0, ey] for place in range(Q)]
            placed = block_transpose(chunks, Q)
            for qy in range(Q):
                value = placed[qy]
                y = qy + (Q - 1) * ey
                if ey == 0 and qy == Q - 1:
                    before = value
                    continue
                if ey == 1 and qy == 0:
                    value = value + before
                loc[y * LOCAL : (y + 1) * LOCAL, t * LANES : (t + 1) * LANES] = value

    h0, h1 = heights[0], heights[1]
    inv0, inv1 = 1.0 / h0, 1.0 / h1
    mass_y = []
    for y in range(ROWS):
        if y < Q - 1:
            mass_y.append(h0 * weights[y])
        elif y == Q - 1:
            mass_y.append(h0 * weights[y] + h1 * weights[0])
        else:
            mass_y.append(h1 * weights[y - Q + 1])

    def products(source_ref, body):
        for half in range(2):
            plane = ints[0] * LOCAL + half * 8 + lax.broadcasted_iota(jnp.int32, (8, LANES), 0)
            kappa = jnp.where(plane == 1, PLANES // 2, plane >> 1).astype(F32)
            beta = kappa * (2.0 * np.pi / (PLANES / 64.0))
            lam = (beta * beta + SIGMA) * 0.25
            for t in range(2):
                rows = [pl.ds(y * LOCAL + half * 8, 8) for y in range(ROWS)]
                lanes = pl.ds(t * LANES, LANES)
                values = [source_ref[r, lanes] for r in rows]
                for y in range(ROWS):
                    total = (lam * mass_y[y]) * values[y]
                    if y <= Q - 1:
                        inner = stiff_y[y][0] * values[0]
                        for m in range(1, Q):
                            inner = inner + stiff_y[y][m] * values[m]
                        total = total + inv0 * inner
                    if y >= Q - 1:
                        inner = stiff_y[y - Q + 1][0] * values[Q - 1]
                        for m in range(1, Q):
                            inner = inner + stiff_y[y - Q + 1][m] * values[Q - 1 + m]
                        total = total + inv1 * inner
                    body(half, t, y, rows[y], lanes, values[y], total)

    first, second, third = v0_ref.at[0], v1_ref.at[0], v2_ref.at[0]
    first[...] = dot_full(loc[...], join_ref[...])
    sums = {}

    def add(key, half, t, value):
        key = (key, half, t)
        sums[key] = value if key not in sums else sums[key] + value

    def step(target, low_key, previous):
        def body(half, t, y, r, lanes, value, total):
            image = mass_y[y] * tmp[r, lanes] + vec[1, :, lanes] * total
            target[r, lanes] = image
            weighted = value * vec[3, :, lanes]
            add(low_key, half, t, weighted * value)
            add(low_key + 1, half, t, weighted * image)
        return body

    def last(half, t, y, r, lanes, value, total):
        image = mass_y[y] * tmp[r, lanes] + vec[2, :, lanes] * total
        add(4, half, t, value * vec[3, :, lanes] * value)
        add(5, half, t, value * image)

    tmp[...] = dot_full(first[...], kxs[...])
    products(first, step(second, 0, None))
    tmp[...] = dot_full(second[...], kxs[...])
    products(second, step(third, 2, None))
    tmp[...] = dot_full(third[...], kbs[...])
    products(third, last)
    prod[...] = jnp.zeros_like(prod)
    for key in range(6):
        for half in range(2):
            prod[key * LOCAL + half * 8 : key * LOCAL + half * 8 + 8, :] = (
                sums[(key, half, 0)] + sums[(key, half, 1)]
            )
    row = lax.dot_general(
        jnp.ones((8, LANES), F32), prod[...], (((1,), (1,)), ((), ())),
        precision=HIGHEST, preferred_element_type=F32,
    )
    mom_ref[:, pl.ds(comp, 1), :] = jnp.broadcast_to(row[0:1][None], (mom_ref.shape[0], 1, LANES))


def krylov_stage(stiff_y, weights, ints, heights, own, left, right, kb, join, wx, peers):
    smem = pl.BlockSpec(memory_space=pltpu.SMEM)

    def whole(array):
        return pl.BlockSpec(array.shape, lambda i: (0,) * array.ndim)

    def chunk(count):
        return pl.BlockSpec((count, 1, 2, LOCAL, LANES), lambda i: (0, i, 0, 0, 0))

    vector = pl.BlockSpec((1, ROWS * LOCAL, 2 * LANES), lambda i: (i, 0, 0))
    shape = jax.ShapeDtypeStruct((3, ROWS * LOCAL, 2 * LANES), F32)

    def body(*refs):
        krylov_body(stiff_y, weights, *refs)

    return pl.pallas_call(
        body,
        grid=(3,),
        in_specs=[smem, smem, chunk(COLUMNS), chunk(GHOST), chunk(GHOST), whole(kb), whole(join), whole(wx)],
        out_specs=[vector, vector, vector, pl.BlockSpec((peers, 8, LANES), lambda i: (0, 0, 0))],
        out_shape=[shape, shape, shape, jax.ShapeDtypeStruct((peers, 8, LANES), F32)],
        scratch_shapes=[
            pltpu.VMEM((ROWS * LOCAL, 2 * LANES), F32),
            pltpu.VMEM((2 * LANES, 2 * LANES), F32),
            pltpu.VMEM((2 * LANES, 2 * LANES), F32),
            pltpu.VMEM((4, 8, 2 * LANES), F32),
            pltpu.VMEM((LANES, LANES), F32),
            pltpu.VMEM((ROWS * LOCAL, 2 * LANES), F32),
        ],
        name="krylov_stage",
    )(ints, heights, own, left, right, kb, join, wx)


def combine_body(mom_ref, v0_ref, v1_ref, v2_ref, out_ref, scr, coef):
    comp = pl.program_id(0)

    @pl.when(comp == 0)
    def _():
        total = jnp.sum(mom_ref[...], axis=0)
        used = (lane_ids((8, LANES)) < LOCAL) & (
            lax.broadcasted_iota(jnp.int32, (8, LANES), 0) < 3
        )
        m = [jnp.where(used, turn(total, -LOCAL * k), 1.0) for k in range(6)]
        inv = 1.0 / m[0]
        m = [value * inv for value in m]
        d0, d1, d2 = (1.0 / jnp.sqrt(m[k]) for k in (1, 3, 5))
        g0, g1, g2 = d0, m[1] * d1, m[2] * d2
        l10 = m[2] * d0 * d1
        l20 = m[3] * d0 * d2
        k21 = m[4] * d1 * d2
        p1 = 1.0 - l10 * l10
        e = k21 - l20 * l10
        l21 = e / p1
        p2 = 1.0 - l20 * l20 - l21 * e
        y1 = g1 - l10 * g0
        y2 = g2 - l20 * g0 - l21 * y1
        z2 = y2 / p2
        z1 = y1 / p1 - l21 * z2
        z0 = g0 - l10 * z1 - l20 * z2
        eye = (
            lax.broadcasted_iota(jnp.int32, (LOCAL, LANES), 0) == lane_ids((LOCAL, LANES))
        ).astype(F32)
        for k, value in enumerate((z0 * d0, z1 * d1, z2 * d2)):
            coef[k] = lax.dot_general(
                eye, jnp.where(used, value, 0.0), (((1,), (1,)), ((), ())),
                precision=HIGHEST, preferred_element_type=F32,
            )

    pick = lane_ids((LOCAL, 8)) == comp
    c0, c1, c2 = (
        jnp.broadcast_to(
            jnp.sum(jnp.where(pick, coef[k], 0.0), axis=1, keepdims=True), (LOCAL, LANES)
        )
        for k in range(3)
    )
    for y in range(ROWS):
        rows = slice(y * LOCAL, (y + 1) * LOCAL)
        for t in range(2):
            lanes = slice(t * LANES, (t + 1) * LANES)
            value = (
                c0 * v0_ref[0, rows, lanes] + c1 * v1_ref[0, rows, lanes] + c2 * v2_ref[0, rows, lanes]
            )
            if y <= Q - 1:
                scr[0, t, pl.ds(y, LOCAL, stride=16), :] = value
            if y >= Q - 1:
                scr[1, t, pl.ds(y - Q + 1, LOCAL, stride=16), :] = value
    lane = lane_ids((16, LANES))
    run = COLUMNS * Q // 2
    for ey in range(2):
        turned = []
        for r in range(2 * LOCAL):
            start = GHOST * Q if r % 2 == 0 else 0
            value = scr[ey, r % 2, (r // 2) * 16 : (r // 2) * 16 + 16, :]
            turned.append(turn(value, run * r - start))
        for tile in range(COLUMNS * Q * LOCAL // LANES):
            low, high = tile * LANES // run, (tile * LANES + LANES - 1) // run
            value = turned[low]
            for r in range(low + 1, high + 1):
                value = jnp.where(lane >= run * r - LANES * tile, turned[r], value)
            out_ref[0, ey, :, tile * LANES : (tile + 1) * LANES] = value[:Q]


def combine(moments, v0, v1, v2):
    vector = pl.BlockSpec((1, ROWS * LOCAL, 2 * LANES), lambda i: (i, 0, 0))
    return pl.pallas_call(
        combine_body,
        grid=(3,),
        in_specs=[pl.BlockSpec(moments.shape, lambda i: (0, 0, 0)), vector, vector, vector],
        out_specs=pl.BlockSpec((1, 2, Q, COLUMNS * Q * LOCAL), lambda i: (i, 0, 0, 0)),
        out_shape=jax.ShapeDtypeStruct((3, 2, Q, COLUMNS * Q * LOCAL), F32),
        scratch_shapes=[pltpu.VMEM((2, 2, 256, LANES), F32), pltpu.VMEM((3, LOCAL, 8), F32)],
        name="combine",
    )(moments, v0, v1, v2)


def make_tables():
    derivative, weights = gll_tables(Q)
    basis, basis_slope, span_slope = fourier_table(PLANES)
    table = np.concatenate([basis.T, basis_slope.T], axis=1)
    table = table.astype(np.float32)
    eye = np.eye(Q)
    nodes = np.zeros((2, LANES, LANES))
    nodes[0, :NODES, :NODES] = np.kron(eye, derivative.T)
    nodes[1, :NODES, :NODES] = np.kron(derivative.T, eye)
    order = np.zeros((176, LANES))
    for qx in range(Q):
        for qy in range(Q):
            order[qx * 16 + qy, qy * Q + qx] = 1.0
    stack = np.concatenate([order, order @ nodes[0], order @ nodes[1]], axis=1)
    stack = np.concatenate(halves(stack), axis=0)
    plane = np.concatenate([nodes[0], nodes[1]], axis=1)
    mass = np.zeros((1, LANES), np.float32)
    mass[0, :NODES] = np.kron(weights, weights)
    stiff = (derivative.T * weights) @ derivative
    kb = np.zeros((2 * LANES, 2 * LANES))
    join = np.eye(2 * LANES)
    wx = np.zeros((1, 2 * LANES), np.float32)
    ends = []
    for t in range(2):
        for place in range(Q):
            low = t * LANES + place * Q
            kb[low : low + Q, low : low + Q] = stiff
            wx[0, low : low + Q] = weights
            ends.append(low)
    for left, right in zip(ends[:-1], ends[1:]):
        join[left + Q - 1, right] = 1.0
        join[right, left + Q - 1] = 1.0
    for t in range(2):
        join[t * LANES + NODES : (t + 1) * LANES] = 0.0
    return dict(
        table=table, stack=stack, dz=halves(span_slope), plane=halves(plane), mass=mass,
        kb=kb.astype(np.float32), join=join.astype(np.float32), wx=wx,
        stiff=stiff.tolist(), weights=weights.tolist(),
    )


def local(adjoint_velocity, base_flow, column_widths, row_heights, base_phase):
    tables = make_tables()
    elem_count = lax.axis_size("elem")
    ints = jnp.stack([lax.axis_index("four").astype(jnp.int32), base_phase[0]])
    send = pack(adjoint_velocity)
    arrived = lax.all_to_all(send, "four", split_axis=0, concat_axis=0, tiled=True)
    fields, *turned = base_stage(
        ints, column_widths, row_heights, base_flow, jnp.asarray(tables["table"]),
        jnp.asarray(tables["stack"]), *(jnp.asarray(a) for a in tables["dz"]),
    )
    source = lines_stage(
        ints, column_widths, row_heights, arrived, fields, turned,
        *(jnp.asarray(a) for a in tables["plane"]), jnp.asarray(tables["mass"]),
    )
    own = lax.all_to_all(source, "four", split_axis=0, concat_axis=0, tiled=True)
    up = [(i, i + 1) for i in range(elem_count - 1)]
    left = lax.ppermute(own[COLUMNS - GHOST :], "elem", up)
    right = lax.ppermute(own[:GHOST], "elem", [(j, i) for i, j in up])
    v0, v1, v2, moments = krylov_stage(
        tables["stiff"], tables["weights"], ints, row_heights, own, left, right,
        jnp.asarray(tables["kb"]), jnp.asarray(tables["join"]), jnp.asarray(tables["wx"]), elem_count,
    )
    moments = lax.all_to_all(moments, "elem", split_axis=0, concat_axis=0, tiled=True)
    return combine(moments, v0, v1, v2)


def solution(mesh):
    split_spec = P(None, None, None, ("elem", "four"))
    return jax.shard_map(
        local,
        mesh=mesh,
        in_specs=(split_spec, split_spec, P("elem"), P(), P()),
        out_specs=split_spec,
        check_vma=False,
    )
```

```python
import jax
import jax.numpy as jnp
import numpy as np
from jax import lax
from jax.experimental import pallas as pl
from jax.experimental.pallas import tpu as pltpu
from jax.sharding import PartitionSpec as P

Q = 11
PLANES = 256
PEERS = 16
LOCAL = 16
COLUMNS = 16
GHOST = 3
ROWS = 21
NODES = Q * Q
LANES = 128
NU = 0.005
DT = 0.01
SIGMA = 1.0 / (NU * DT)
HIGHEST = lax.Precision.HIGHEST
F32 = jnp.float32
BF16 = jnp.bfloat16


def legendre_values(points, node_count):
    table_rows = np.zeros((points.shape[0], node_count))
    table_rows[:, 0] = 1.0
    table_rows[:, 1] = points
    for degree_now in range(2, node_count):
        table_rows[:, degree_now] = (
            (2 * degree_now - 1) * points * table_rows[:, degree_now - 1]
            - (degree_now - 1) * table_rows[:, degree_now - 2]
        ) / degree_now
    return table_rows


def gll_tables(node_count):
    degree = node_count - 1
    points = np.cos(np.pi * np.arange(node_count) / degree)
    for newton_step in range(60):
        legendre = legendre_values(points, node_count)
        points = points - (points * legendre[:, degree] - legendre[:, degree - 1]) / (
            node_count * legendre[:, degree]
        )
    legendre = legendre_values(points, node_count)
    weights = 2.0 / (degree * node_count * legendre[:, degree] ** 2)
    points = points[::-1]
    weights = weights[::-1]
    end_values = legendre[::-1, degree]
    derivative = np.zeros((node_count, node_count))
    for row_index in range(node_count):
        for column in range(node_count):
            if row_index != column:
                derivative[row_index, column] = end_values[row_index] / (
                    end_values[column] * (points[row_index] - points[column])
                )
    derivative[0, 0] = -degree * node_count / 4.0
    derivative[degree, degree] = degree * node_count / 4.0
    return derivative, weights


def fourier_table(plane_count):
    positions = np.arange(plane_count)
    basis_rows = np.zeros((plane_count, plane_count))
    basis_rows[0] = 1.0 / np.sqrt(plane_count)
    basis_rows[1] = np.cos(np.pi * positions) / np.sqrt(plane_count)
    for wave_index in range(1, plane_count // 2):
        angle = 2.0 * np.pi * wave_index * positions / plane_count
        basis_rows[2 * wave_index] = np.sqrt(2.0 / plane_count) * np.cos(angle)
        basis_rows[2 * wave_index + 1] = np.sqrt(2.0 / plane_count) * np.sin(angle)
    wave_counts = np.arange(plane_count) // 2
    wave_counts[1] = plane_count // 2
    wave_counts[0] = 0
    wavenumbers = 2.0 * np.pi * wave_counts / (plane_count / 64.0)
    rotate = np.zeros((plane_count, plane_count))
    for wave_index in range(1, plane_count // 2):
        rotate[2 * wave_index, 2 * wave_index + 1] = wavenumbers[2 * wave_index]
        rotate[2 * wave_index + 1, 2 * wave_index] = -wavenumbers[2 * wave_index]
    return basis_rows, rotate.T @ basis_rows, basis_rows.T @ rotate @ basis_rows


def halves(array):
    high = np.asarray(array, np.float32).astype(jnp.bfloat16)
    low = (np.asarray(array, np.float64) - high.astype(np.float64)).astype(jnp.bfloat16)
    return high, low


def split(value):
    high = value.astype(BF16)
    return high, (value - high.astype(F32)).astype(BF16)


def dot(left, right):
    return jnp.dot(left, right, preferred_element_type=F32)


def dot_full(left, right):
    return jnp.dot(left, right, precision=HIGHEST, preferred_element_type=F32)


def lane_ids(shape):
    return lax.broadcasted_iota(jnp.int32, shape, len(shape) - 1)


def turn(value, shift):
    shift = shift % LANES
    return value if shift == 0 else pltpu.roll(value, shift, value.ndim - 1)


def block_transpose(arrays, count):
    lane = lane_ids(arrays[0].shape)
    turned = [turn(array, Q * k) for k, array in enumerate(arrays)]
    results = []
    for place in range(count):
        distance = (lane - Q * place) & (LANES - 1)
        chosen = turned[0]
        for k in range(1, len(turned)):
            chosen = jnp.where(distance >= Q * k, turned[k], chosen)
        chosen = jnp.where(distance < NODES, chosen, 0.0)
        results.append(turn(chosen, -Q * place))
    return results


def pack_body(in_ref, out_ref, flat, scr0, scr1):
    lane = lane_ids((16, LANES))
    scratches = (scr0, scr1)
    tiles = COLUMNS * Q * LOCAL // LANES
    for qy in range(Q):
        for tile in range(tiles):
            flat[tile, pl.ds(qy, 2, stride=16), :] = in_ref[0, qy, :, tile * LANES : (tile + 1) * LANES]
    for ey in range(2):
        rows = slice(ey * 16, ey * 16 + 16)
        for j in range(LOCAL):
            for t in range(2):
                offset = j * COLUMNS * Q + NODES * t
                tile, shift = offset // LANES, offset % LANES
                first = flat[tile, rows, :]
                if shift and tile + 1 < tiles:
                    first = jnp.where(lane >= shift, first, flat[tile + 1, rows, :])
                scratches[t][ey, j * 16 : j * 16 + 16, :] = turn(first, -shift)
    for ey in range(2):
        for t in range(2):
            rows = [scratches[t][ey, pl.ds(qy, LOCAL, stride=16), :] for qy in range(Q)]
            for place, value in enumerate(block_transpose(rows, Q if t == 0 else COLUMNS - Q)):
                out_ref[Q * t + place, 0, ey] = value


def pack(adjoint):
    return pl.pallas_call(
        pack_body,
        grid=(3,),
        in_specs=[pl.BlockSpec((1, Q, 2, COLUMNS * Q * LOCAL), lambda i: (i, 0, 0, 0))],
        out_specs=pl.BlockSpec((PEERS, 1, 2, LOCAL, LANES), lambda i: (0, i, 0, 0, 0)),
        out_shape=jax.ShapeDtypeStruct((PEERS, 3, 2, LOCAL, LANES), F32),
        scratch_shapes=[
            pltpu.VMEM((COLUMNS * Q * LOCAL // LANES, 32, LANES), F32),
            pltpu.VMEM((2, 256, LANES), F32),
            pltpu.VMEM((2, 256, LANES), F32),
        ],
        name="pack",
    )(jnp.transpose(adjoint, (0, 2, 1, 3)))


def base_body(ints, widths, heights, base_ref, table_ref, stack_ref, dzh_ref, dzl_ref,
              field_ref, fgh_ref, fgl_ref, fh_ref, fl_ref, scr):
    step = pl.program_id(0)

    @pl.when(step == 0)
    def _():
        scr[...] = jnp.zeros_like(scr)
        rows = pltpu.roll(table_ref[...], (PLANES - ints[1]) % PLANES, 0)
        for k in range(2):
            high, low = split(rows[:, k * PLANES : (k + 1) * PLANES])
            fgh_ref[k * PLANES : (k + 1) * PLANES, :] = high
            fgl_ref[k * PLANES : (k + 1) * PLANES, :] = low
        high, low = split(jnp.transpose(rows[:, :PLANES]))
        fh_ref[...] = high
        fl_ref[...] = low

    for qx in range(Q):
        part = base_ref[0, 0, :, qx * PLANES : (qx + 1) * PLANES]
        scr[qx * 16 : qx * 16 + Q, :] = part
        scr[176 + qx * 16 : 176 + qx * 16 + Q, :] = part
    mixed = lax.dot_general(
        scr[...], stack_ref[...], (((0,), (0,)), ((), ())), preferred_element_type=F32
    )
    plain = mixed[:, :LANES]
    field_ref[0, 0, 0] = plain
    field_ref[1, 0, 0] = mixed[:, LANES : 2 * LANES] * (2.0 / widths[ints[0]])
    field_ref[2, 0, 0] = mixed[:, 2 * LANES :] * (2.0 / heights[step % 2])
    exact = plain.astype(BF16)
    field_ref[3, 0, 0] = dot(dzh_ref[...], exact) + dot(dzl_ref[...], exact)


def base_stage(ints, widths, heights, base, table, stack, dz_high, dz_low):
    smem = pl.BlockSpec(memory_space=pltpu.SMEM)

    def whole(shape):
        return pl.BlockSpec(shape, lambda i: (0,) * len(shape))

    return pl.pallas_call(
        base_body,
        grid=(6,),
        in_specs=[
            smem, smem, smem,
            pl.BlockSpec((1, 1, Q, Q * PLANES), lambda i: (i // 2, i % 2, 0, 0)),
            whole(table.shape), whole(stack.shape), whole(dz_high.shape), whole(dz_low.shape),
        ],
        out_specs=[
            pl.BlockSpec((4, 1, 1, PLANES, LANES), lambda i: (0, i // 2, i % 2, 0, 0)),
            whole((2 * PLANES, PLANES)), whole((2 * PLANES, PLANES)),
            whole((PLANES, PLANES)), whole((PLANES, PLANES)),
        ],
        out_shape=[
            jax.ShapeDtypeStruct((4, 3, 2, PLANES, LANES), F32),
            jax.ShapeDtypeStruct((2 * PLANES, PLANES), BF16),
            jax.ShapeDtypeStruct((2 * PLANES, PLANES), BF16),
            jax.ShapeDtypeStruct((PLANES, PLANES), BF16),
            jax.ShapeDtypeStruct((PLANES, PLANES), BF16),
        ],
        scratch_shapes=[pltpu.VMEM((352, PLANES), BF16)],
        name="base_stage",
    )(ints, widths, heights, base, table, stack, dz_high, dz_low)


def lines_body(ints, widths, heights, in_ref, field_ref, fgh_ref, fgl_ref, fh_ref, fl_ref,
               dh_ref, dl_ref, mass_ref, out_ref):
    ey = pl.program_id(0)
    width, height = widths[ints[0]], heights[ey]
    coeffs = [in_ref[:, c, 0].reshape(PLANES, LANES) for c in range(3)]
    high, low = split(jnp.concatenate(coeffs, axis=1))
    both = dot(fgh_ref[...], high) + dot(fgh_ref[...], low) + dot(fgl_ref[...], high)
    lines = [both[:PLANES, c * LANES : (c + 1) * LANES] for c in range(3)]
    slopes = [None, None, [both[PLANES:, c * LANES : (c + 1) * LANES] for c in range(3)]]
    high, low = split(jnp.concatenate(lines, axis=0))
    plane = dot(high, dh_ref[...]) + dot(low, dh_ref[...]) + dot(high, dl_ref[...])
    per_c = [plane[c * PLANES : (c + 1) * PLANES] for c in range(3)]
    slopes[0] = [part[:, :LANES] * (2.0 / width) for part in per_c]
    slopes[1] = [part[:, LANES:] * (2.0 / height) for part in per_c]
    pieces = []
    for c in range(3):
        total = field_ref[0, 0, 0] * slopes[0][c]
        for d in range(1, 3):
            total = total + field_ref[0, d, 0] * slopes[d][c]
        for d in range(3):
            total = total - lines[d] * field_ref[1 + c, d, 0]
        pieces.append(total)
    high, low = split(jnp.concatenate(pieces, axis=1))
    hat = dot(fh_ref[...], high) + dot(fh_ref[...], low) + dot(fl_ref[...], high)
    mass = mass_ref[...] * (width * height * 0.25)
    lane = lane_ids((PLANES, LANES))
    for c in range(3):
        source = SIGMA * coeffs[c] + hat[:, c * LANES : (c + 1) * LANES] * (1.0 / NU)
        value = jnp.where(lane < NODES, mass * source, width)
        out_ref[:, c, 0] = value.reshape(PEERS, LOCAL, LANES)


def lines_stage(ints, widths, heights, arrived, fields, tables, d_high, d_low, mass):
    smem = pl.BlockSpec(memory_space=pltpu.SMEM)

    def whole(array):
        return pl.BlockSpec(array.shape, lambda i: (0,) * array.ndim)

    block = pl.BlockSpec((PEERS, 3, 1, LOCAL, LANES), lambda i: (0, 0, i, 0, 0))
    return pl.pallas_call(
        lines_body,
        grid=(2,),
        in_specs=[
            smem, smem, smem, block,
            pl.BlockSpec((4, 3, 1, PLANES, LANES), lambda i: (0, 0, i, 0, 0)),
        ] + [whole(a) for a in tables] + [whole(d_high), whole(d_low), whole(mass)],
        out_specs=block,
        out_shape=jax.ShapeDtypeStruct((PEERS, 3, 2, LOCAL, LANES), F32),
        name="lines_stage",
    )(ints, widths, heights, arrived, fields, *tables, d_high, d_low, mass)


def krylov_body(stiff_y, weights, ints, heights, own_ref, left_ref, right_ref, kb_ref, join_ref, wx_ref,
                v0_ref, v1_ref, v2_ref, mom_ref, loc, kxs, kbs, vec, prod, tmp):
    comp = pl.program_id(0)
    column_refs = (
        [left_ref.at[k] for k in range(GHOST)]
        + [own_ref.at[k] for k in range(COLUMNS)]
        + [right_ref.at[k] for k in range(GHOST)]
    )

    @pl.when(comp == 0)
    def _():
        lane = lane_ids((8, LANES))
        for t in range(2):
            here = jnp.zeros((8, LANES), F32)
            for place in range(Q):
                width = column_refs[Q * t + place][0, 0, 0:8, NODES : NODES + 1]
                inside = (lane >= Q * place) & (lane < Q * place + Q)
                here = jnp.where(inside, width, here)
            vec[0, :, t * LANES : (t + 1) * LANES] = here
        here = vec[0]
        inverse = jnp.where(here > 0.0, 1.0 / jnp.where(here > 0.0, here, 1.0), 0.0)
        line = lane_ids((8, 2 * LANES))
        own = ((line >= GHOST * Q) & (line < NODES)) | (
            (line >= LANES) & (line < LANES + (Q - GHOST) * Q)
        )
        own = own.astype(F32)
        mass_x = here * wx_ref[...]
        vec[1] = dot_full(mass_x, join_ref[...])
        vec[2] = mass_x * own
        place = jnp.where(line >= LANES, line - LANES, line)
        place = place - Q * ((place * 5958) >> 16)
        edge = (place == 0) | (place == Q - 1)
        left_end = (line == GHOST * Q) & (pltpu.roll(here, 1, 1) == 0.0)
        right_end = (line == LANES + (Q - GHOST) * Q - 1) & (
            pltpu.roll(here, 2 * LANES - 1, 1) == 0.0
        )
        shared = edge & jnp.logical_not(left_end | right_end)
        vec[3] = own * jnp.where(shared, 0.5, 1.0)
        scaled = kb_ref[...] * inverse[0:1]
        kxs[...] = dot_full(scaled, join_ref[...])
        kbs[...] = scaled * own[0:1]

    for t in range(2):
        before = None
        for ey in range(2):
            chunks = [column_refs[Q * t + place][0, ey] for place in range(Q)]
            placed = block_transpose(chunks, Q)
            for qy in range(Q):
                value = placed[qy]
                y = qy + (Q - 1) * ey
                if ey == 0 and qy == Q - 1:
                    before = value
                    continue
                if ey == 1 and qy == 0:
                    value = value + before
                loc[y * LOCAL : (y + 1) * LOCAL, t * LANES : (t + 1) * LANES] = value

    h0, h1 = heights[0], heights[1]
    inv0, inv1 = 1.0 / h0, 1.0 / h1
    mass_y = []
    for y in range(ROWS):
        if y < Q - 1:
            mass_y.append(h0 * weights[y])
        elif y == Q - 1:
            mass_y.append(h0 * weights[y] + h1 * weights[0])
        else:
            mass_y.append(h1 * weights[y - Q + 1])

    def products(source_ref, body):
        for half in range(2):
            plane = ints[0] * LOCAL + half * 8 + lax.broadcasted_iota(jnp.int32, (8, LANES), 0)
            kappa = jnp.where(plane == 1, PLANES // 2, plane >> 1).astype(F32)
            beta = kappa * (2.0 * np.pi / (PLANES / 64.0))
            lam = (beta * beta + SIGMA) * 0.25
            for t in range(2):
                rows = [pl.ds(y * LOCAL + half * 8, 8) for y in range(ROWS)]
                lanes = pl.ds(t * LANES, LANES)
                values = [source_ref[r, lanes] for r in rows]
                for y in range(ROWS):
                    total = (lam * mass_y[y]) * values[y]
                    if y <= Q - 1:
                        inner = stiff_y[y][0] * values[0]
                        for m in range(1, Q):
                            inner = inner + stiff_y[y][m] * values[m]
                        total = total + inv0 * inner
                    if y >= Q - 1:
                        inner = stiff_y[y - Q + 1][0] * values[Q - 1]
                        for m in range(1, Q):
                            inner = inner + stiff_y[y - Q + 1][m] * values[Q - 1 + m]
                        total = total + inv1 * inner
                    body(half, t, y, rows[y], lanes, values[y], total)

    first, second, third = v0_ref.at[0], v1_ref.at[0], v2_ref.at[0]
    first[...] = dot_full(loc[...], join_ref[...])
    sums = {}

    def add(key, half, t, value):
        key = (key, half, t)
        sums[key] = value if key not in sums else sums[key] + value

    def step(target, low_key, previous):
        def body(half, t, y, r, lanes, value, total):
            image = mass_y[y] * tmp[r, lanes] + vec[1, :, lanes] * total
            target[r, lanes] = image
            weighted = value * vec[3, :, lanes]
            add(low_key, half, t, weighted * value)
            add(low_key + 1, half, t, weighted * image)
        return body

    def last(half, t, y, r, lanes, value, total):
        image = mass_y[y] * tmp[r, lanes] + vec[2, :, lanes] * total
        add(4, half, t, value * vec[3, :, lanes] * value)
        add(5, half, t, value * image)

    tmp[...] = dot_full(first[...], kxs[...])
    products(first, step(second, 0, None))
    tmp[...] = dot_full(second[...], kxs[...])
    products(second, step(third, 2, None))
    tmp[...] = dot_full(third[...], kbs[...])
    products(third, last)
    prod[...] = jnp.zeros_like(prod)
    for key in range(6):
        for half in range(2):
            prod[key * LOCAL + half * 8 : key * LOCAL + half * 8 + 8, :] = (
                sums[(key, half, 0)] + sums[(key, half, 1)]
            )
    row = lax.dot_general(
        jnp.ones((8, LANES), F32), prod[...], (((1,), (1,)), ((), ())),
        precision=HIGHEST, preferred_element_type=F32,
    )
    mom_ref[:, pl.ds(comp, 1), :] = jnp.broadcast_to(row[0:1][None], (mom_ref.shape[0], 1, LANES))


def krylov_stage(stiff_y, weights, ints, heights, own, left, right, kb, join, wx, peers):
    smem = pl.BlockSpec(memory_space=pltpu.SMEM)

    def whole(array):
        return pl.BlockSpec(array.shape, lambda i: (0,) * array.ndim)

    def chunk(count):
        return pl.BlockSpec((count, 1, 2, LOCAL, LANES), lambda i: (0, i, 0, 0, 0))

    vector = pl.BlockSpec((1, ROWS * LOCAL, 2 * LANES), lambda i: (i, 0, 0))
    shape = jax.ShapeDtypeStruct((3, ROWS * LOCAL, 2 * LANES), F32)

    def body(*refs):
        krylov_body(stiff_y, weights, *refs)

    return pl.pallas_call(
        body,
        grid=(3,),
        in_specs=[smem, smem, chunk(COLUMNS), chunk(GHOST), chunk(GHOST), whole(kb), whole(join), whole(wx)],
        out_specs=[vector, vector, vector, pl.BlockSpec((peers, 8, LANES), lambda i: (0, 0, 0))],
        out_shape=[shape, shape, shape, jax.ShapeDtypeStruct((peers, 8, LANES), F32)],
        scratch_shapes=[
            pltpu.VMEM((ROWS * LOCAL, 2 * LANES), F32),
            pltpu.VMEM((2 * LANES, 2 * LANES), F32),
            pltpu.VMEM((2 * LANES, 2 * LANES), F32),
            pltpu.VMEM((4, 8, 2 * LANES), F32),
            pltpu.VMEM((LANES, LANES), F32),
            pltpu.VMEM((ROWS * LOCAL, 2 * LANES), F32),
        ],
        name="krylov_stage",
    )(ints, heights, own, left, right, kb, join, wx)


def unpack_body(v0_ref, v1_ref, v2_ref, u0_ref, u1_ref, u2_ref, scr, flat):
    lane = lane_ids((16, LANES))
    run = COLUMNS * Q // 2
    for vector, target in ((v0_ref, u0_ref), (v1_ref, u1_ref), (v2_ref, u2_ref)):
        for y in range(ROWS):
            rows = slice(y * LOCAL, (y + 1) * LOCAL)
            for t in range(2):
                value = vector[0, rows, t * LANES : (t + 1) * LANES]
                if y <= Q - 1:
                    scr[0, t, pl.ds(y, LOCAL, stride=16), :] = value
                if y >= Q - 1:
                    scr[1, t, pl.ds(y - Q + 1, LOCAL, stride=16), :] = value
        for ey in range(2):
            turned = []
            for r in range(2 * LOCAL):
                start = GHOST * Q if r % 2 == 0 else 0
                value = scr[ey, r % 2, (r // 2) * 16 : (r // 2) * 16 + 16, :]
                turned.append(turn(value, run * r - start))
            for tile in range(COLUMNS * Q * LOCAL // LANES):
                low, high = tile * LANES // run, (tile * LANES + LANES - 1) // run
                value = turned[low]
                for r in range(low + 1, high + 1):
                    value = jnp.where(lane >= run * r - LANES * tile, turned[r], value)
                flat[tile, ey * 16 : ey * 16 + 16, :] = value
        for qy in range(Q):
            for tile in range(COLUMNS * Q * LOCAL // LANES):
                target[0, qy, :, tile * LANES : (tile + 1) * LANES] = flat[
                    tile, pl.ds(qy, 2, stride=16), :
                ]


def unpack(v0, v1, v2):
    vector = pl.BlockSpec((1, ROWS * LOCAL, 2 * LANES), lambda i: (i, 0, 0))
    target = pl.BlockSpec((1, Q, 2, COLUMNS * Q * LOCAL), lambda i: (i, 0, 0, 0))
    shape = jax.ShapeDtypeStruct((3, Q, 2, COLUMNS * Q * LOCAL), F32)
    return pl.pallas_call(
        unpack_body,
        grid=(3,),
        in_specs=[vector] * 3,
        out_specs=[target] * 3,
        out_shape=[shape] * 3,
        scratch_shapes=[
            pltpu.VMEM((2, 2, 256, LANES), F32),
            pltpu.VMEM((COLUMNS * Q * LOCAL // LANES, 32, LANES), F32),
        ],
        name="unpack",
    )(v0, v1, v2)


def finish_body(mom_ref, u0_ref, u1_ref, u2_ref, out_ref, coef):
    comp = pl.program_id(0)
    tiles = COLUMNS * Q * LOCAL // LANES

    @pl.when(comp == 0)
    def _():
        total = jnp.sum(mom_ref[...], axis=0)
        used = (lane_ids((8, LANES)) < LOCAL) & (
            lax.broadcasted_iota(jnp.int32, (8, LANES), 0) < 3
        )
        m = [jnp.where(used, turn(total, -LOCAL * k), 1.0) for k in range(6)]
        inv = 1.0 / m[0]
        m = [value * inv for value in m]
        d0, d1, d2 = (1.0 / jnp.sqrt(m[k]) for k in (1, 3, 5))
        g0, g1, g2 = d0, m[1] * d1, m[2] * d2
        l10 = m[2] * d0 * d1
        l20 = m[3] * d0 * d2
        k21 = m[4] * d1 * d2
        p1 = 1.0 - l10 * l10
        e = k21 - l20 * l10
        l21 = e / p1
        p2 = 1.0 - l20 * l20 - l21 * e
        y1 = g1 - l10 * g0
        y2 = g2 - l20 * g0 - l21 * y1
        z2 = y2 / p2
        z1 = y1 / p1 - l21 * z2
        z0 = g0 - l10 * z1 - l20 * z2
        lane = lane_ids((8, LANES))
        for k, value in enumerate((z0 * d0, z1 * d1, z2 * d2)):
            wide = [jnp.broadcast_to(value[:, j : j + 1], (8, LANES)) for j in range(LOCAL)]
            for tile in range(tiles):
                low = tile * LANES // (COLUMNS * Q)
                high = (tile * LANES + LANES - 1) // (COLUMNS * Q)
                chosen = wide[low]
                if high > low:
                    chosen = jnp.where(lane >= COLUMNS * Q * high - LANES * tile, wide[high], chosen)
                coef[k, tile] = chosen

    for tile in range(tiles):
        lanes = slice(tile * LANES, (tile + 1) * LANES)
        c0, c1, c2 = (
            jnp.broadcast_to(coef[k, tile, pl.ds(comp, 1), :], (2, LANES)) for k in range(3)
        )
        for qy in range(Q):
            out_ref[0, qy, :, lanes] = (
                c0 * u0_ref[0, qy, :, lanes]
                + c1 * u1_ref[0, qy, :, lanes]
                + c2 * u2_ref[0, qy, :, lanes]
            )


def finish(moments, u0, u1, u2):
    target = pl.BlockSpec((1, Q, 2, COLUMNS * Q * LOCAL), lambda i: (i, 0, 0, 0))
    out = pl.pallas_call(
        finish_body,
        grid=(3,),
        in_specs=[pl.BlockSpec(moments.shape, lambda i: (0, 0, 0)), target, target, target],
        out_specs=target,
        out_shape=jax.ShapeDtypeStruct((3, Q, 2, COLUMNS * Q * LOCAL), F32),
        scratch_shapes=[pltpu.VMEM((3, COLUMNS * Q * LOCAL // LANES, 8, LANES), F32)],
        name="finish",
    )(moments, u0, u1, u2)
    return jnp.transpose(out, (0, 2, 1, 3))


def make_tables():
    derivative, weights = gll_tables(Q)
    basis, basis_slope, span_slope = fourier_table(PLANES)
    table = np.concatenate([basis.T, basis_slope.T], axis=1)
    table = table.astype(np.float32)
    eye = np.eye(Q)
    nodes = np.zeros((2, LANES, LANES))
    nodes[0, :NODES, :NODES] = np.kron(eye, derivative.T)
    nodes[1, :NODES, :NODES] = np.kron(derivative.T, eye)
    order = np.zeros((176, LANES))
    for qx in range(Q):
        for qy in range(Q):
            order[qx * 16 + qy, qy * Q + qx] = 1.0
    stack = np.concatenate([order, order @ nodes[0], order @ nodes[1]], axis=1)
    stack = np.concatenate(halves(stack), axis=0)
    plane = np.concatenate([nodes[0], nodes[1]], axis=1)
    mass = np.zeros((1, LANES), np.float32)
    mass[0, :NODES] = np.kron(weights, weights)
    stiff = (derivative.T * weights) @ derivative
    kb = np.zeros((2 * LANES, 2 * LANES))
    join = np.eye(2 * LANES)
    wx = np.zeros((1, 2 * LANES), np.float32)
    ends = []
    for t in range(2):
        for place in range(Q):
            low = t * LANES + place * Q
            kb[low : low + Q, low : low + Q] = stiff
            wx[0, low : low + Q] = weights
            ends.append(low)
    for left, right in zip(ends[:-1], ends[1:]):
        join[left + Q - 1, right] = 1.0
        join[right, left + Q - 1] = 1.0
    for t in range(2):
        join[t * LANES + NODES : (t + 1) * LANES] = 0.0
    return dict(
        table=table, stack=stack, dz=halves(span_slope), plane=halves(plane), mass=mass,
        kb=kb.astype(np.float32), join=join.astype(np.float32), wx=wx,
        stiff=stiff.tolist(), weights=weights.tolist(),
    )


def local(adjoint_velocity, base_flow, column_widths, row_heights, base_phase):
    tables = make_tables()
    elem_count = lax.axis_size("elem")
    ints = jnp.stack([lax.axis_index("four").astype(jnp.int32), base_phase[0]])
    send = pack(adjoint_velocity)
    arrived = lax.all_to_all(send, "four", split_axis=0, concat_axis=0, tiled=True)
    fields, *turned = base_stage(
        ints, column_widths, row_heights, base_flow, jnp.asarray(tables["table"]),
        jnp.asarray(tables["stack"]), *(jnp.asarray(a) for a in tables["dz"]),
    )
    source = lines_stage(
        ints, column_widths, row_heights, arrived, fields, turned,
        *(jnp.asarray(a) for a in tables["plane"]), jnp.asarray(tables["mass"]),
    )
    own = lax.all_to_all(source, "four", split_axis=0, concat_axis=0, tiled=True)
    up = [(i, i + 1) for i in range(elem_count - 1)]
    left = lax.ppermute(own[COLUMNS - GHOST :], "elem", up)
    right = lax.ppermute(own[:GHOST], "elem", [(j, i) for i, j in up])
    v0, v1, v2, moments = krylov_stage(
        tables["stiff"], tables["weights"], ints, row_heights, own, left, right,
        jnp.asarray(tables["kb"]), jnp.asarray(tables["join"]), jnp.asarray(tables["wx"]), elem_count,
    )
    moments = lax.all_to_all(moments, "elem", split_axis=0, concat_axis=0, tiled=True)
    return finish(moments, *unpack(v0, v1, v2))


def solution(mesh):
    split_spec = P(None, None, None, ("elem", "four"))
    return jax.shard_map(
        local,
        mesh=mesh,
        in_specs=(split_spec, split_spec, P("elem"), P(), P()),
        out_specs=split_spec,
        check_vma=False,
    )
```

```python
import jax
import jax.numpy as jnp
import numpy as np
from jax import lax
from jax.experimental import pallas as pl
from jax.experimental.pallas import tpu as pltpu
from jax.sharding import PartitionSpec as P

Q = 11
PLANES = 256
PEERS = 16
LOCAL = 16
COLUMNS = 16
GHOST = 3
ROWS = 21
NODES = Q * Q
LANES = 128
NU = 0.005
DT = 0.01
SIGMA = 1.0 / (NU * DT)
HIGHEST = lax.Precision.HIGHEST
F32 = jnp.float32
BF16 = jnp.bfloat16


def legendre_values(points, node_count):
    table_rows = np.zeros((points.shape[0], node_count))
    table_rows[:, 0] = 1.0
    table_rows[:, 1] = points
    for degree_now in range(2, node_count):
        table_rows[:, degree_now] = (
            (2 * degree_now - 1) * points * table_rows[:, degree_now - 1]
            - (degree_now - 1) * table_rows[:, degree_now - 2]
        ) / degree_now
    return table_rows


def gll_tables(node_count):
    degree = node_count - 1
    points = np.cos(np.pi * np.arange(node_count) / degree)
    for newton_step in range(60):
        legendre = legendre_values(points, node_count)
        points = points - (points * legendre[:, degree] - legendre[:, degree - 1]) / (
            node_count * legendre[:, degree]
        )
    legendre = legendre_values(points, node_count)
    weights = 2.0 / (degree * node_count * legendre[:, degree] ** 2)
    points = points[::-1]
    weights = weights[::-1]
    end_values = legendre[::-1, degree]
    derivative = np.zeros((node_count, node_count))
    for row_index in range(node_count):
        for column in range(node_count):
            if row_index != column:
                derivative[row_index, column] = end_values[row_index] / (
                    end_values[column] * (points[row_index] - points[column])
                )
    derivative[0, 0] = -degree * node_count / 4.0
    derivative[degree, degree] = degree * node_count / 4.0
    return derivative, weights


def fourier_table(plane_count):
    positions = np.arange(plane_count)
    basis_rows = np.zeros((plane_count, plane_count))
    basis_rows[0] = 1.0 / np.sqrt(plane_count)
    basis_rows[1] = np.cos(np.pi * positions) / np.sqrt(plane_count)
    for wave_index in range(1, plane_count // 2):
        angle = 2.0 * np.pi * wave_index * positions / plane_count
        basis_rows[2 * wave_index] = np.sqrt(2.0 / plane_count) * np.cos(angle)
        basis_rows[2 * wave_index + 1] = np.sqrt(2.0 / plane_count) * np.sin(angle)
    wave_counts = np.arange(plane_count) // 2
    wave_counts[1] = plane_count // 2
    wave_counts[0] = 0
    wavenumbers = 2.0 * np.pi * wave_counts / (plane_count / 64.0)
    rotate = np.zeros((plane_count, plane_count))
    for wave_index in range(1, plane_count // 2):
        rotate[2 * wave_index, 2 * wave_index + 1] = wavenumbers[2 * wave_index]
        rotate[2 * wave_index + 1, 2 * wave_index] = -wavenumbers[2 * wave_index]
    return basis_rows, rotate.T @ basis_rows, basis_rows.T @ rotate @ basis_rows


def halves(array):
    high = np.asarray(array, np.float32).astype(jnp.bfloat16)
    low = (np.asarray(array, np.float64) - high.astype(np.float64)).astype(jnp.bfloat16)
    return high, low


def split(value):
    high = value.astype(BF16)
    return high, (value - high.astype(F32)).astype(BF16)


def dot(left, right):
    return jnp.dot(left, right, preferred_element_type=F32)


def dot_full(left, right):
    return jnp.dot(left, right, precision=HIGHEST, preferred_element_type=F32)


def lane_ids(shape):
    return lax.broadcasted_iota(jnp.int32, shape, len(shape) - 1)


def turn(value, shift):
    shift = shift % LANES
    return value if shift == 0 else pltpu.roll(value, shift, value.ndim - 1)


def block_transpose(arrays, count):
    lane = lane_ids(arrays[0].shape)
    turned = [turn(array, Q * k) for k, array in enumerate(arrays)]
    results = []
    for place in range(count):
        distance = (lane - Q * place) & (LANES - 1)
        chosen = turned[0]
        for k in range(1, len(turned)):
            chosen = jnp.where(distance >= Q * k, turned[k], chosen)
        chosen = jnp.where(distance < NODES, chosen, 0.0)
        results.append(turn(chosen, -Q * place))
    return results


def pack_body(in_ref, out_ref, flat, scr0, scr1):
    lane = lane_ids((16, LANES))
    scratches = (scr0, scr1)
    tiles = COLUMNS * Q * LOCAL // LANES
    for qy in range(Q):
        for tile in range(tiles):
            flat[tile, pl.ds(qy, 2, stride=16), :] = in_ref[0, qy, :, tile * LANES : (tile + 1) * LANES]
    for ey in range(2):
        rows = slice(ey * 16, ey * 16 + 16)
        for j in range(LOCAL):
            for t in range(2):
                offset = j * COLUMNS * Q + NODES * t
                tile, shift = offset // LANES, offset % LANES
                first = flat[tile, rows, :]
                if shift and tile + 1 < tiles:
                    first = jnp.where(lane >= shift, first, flat[tile + 1, rows, :])
                scratches[t][ey, j * 16 : j * 16 + 16, :] = turn(first, -shift)
    for ey in range(2):
        for t in range(2):
            rows = [scratches[t][ey, pl.ds(qy, LOCAL, stride=16), :] for qy in range(Q)]
            for place, value in enumerate(block_transpose(rows, Q if t == 0 else COLUMNS - Q)):
                out_ref[Q * t + place, 0, ey] = value


def pack(adjoint):
    return pl.pallas_call(
        pack_body,
        grid=(3,),
        in_specs=[pl.BlockSpec((1, Q, 2, COLUMNS * Q * LOCAL), lambda i: (i, 0, 0, 0))],
        out_specs=pl.BlockSpec((PEERS, 1, 2, LOCAL, LANES), lambda i: (0, i, 0, 0, 0)),
        out_shape=jax.ShapeDtypeStruct((PEERS, 3, 2, LOCAL, LANES), F32),
        scratch_shapes=[
            pltpu.VMEM((COLUMNS * Q * LOCAL // LANES, 32, LANES), F32),
            pltpu.VMEM((2, 256, LANES), F32),
            pltpu.VMEM((2, 256, LANES), F32),
        ],
        name="pack",
    )(jnp.transpose(adjoint, (0, 2, 1, 3)))


def base_body(ints, widths, heights, base_ref, table_ref, stack_ref, dzh_ref, dzl_ref,
              field_ref, fgh_ref, fgl_ref, fh_ref, fl_ref, scr):
    step = pl.program_id(0)

    @pl.when(step == 0)
    def _():
        scr[...] = jnp.zeros_like(scr)
        rows = pltpu.roll(table_ref[...], (PLANES - ints[1]) % PLANES, 0)
        for k in range(2):
            high, low = split(rows[:, k * PLANES : (k + 1) * PLANES])
            fgh_ref[k * PLANES : (k + 1) * PLANES, :] = high
            fgl_ref[k * PLANES : (k + 1) * PLANES, :] = low
        high, low = split(jnp.transpose(rows[:, :PLANES]))
        fh_ref[...] = high
        fl_ref[...] = low

    for qx in range(Q):
        part = base_ref[0, 0, :, qx * PLANES : (qx + 1) * PLANES]
        scr[qx * 16 : qx * 16 + Q, :] = part
        scr[176 + qx * 16 : 176 + qx * 16 + Q, :] = part
    mixed = lax.dot_general(
        scr[...], stack_ref[...], (((0,), (0,)), ((), ())), preferred_element_type=F32
    )
    plain = mixed[:, :LANES]
    field_ref[0, 0, 0] = plain
    field_ref[1, 0, 0] = mixed[:, LANES : 2 * LANES] * (2.0 / widths[ints[0]])
    field_ref[2, 0, 0] = mixed[:, 2 * LANES :] * (2.0 / heights[step % 2])
    exact = plain.astype(BF16)
    field_ref[3, 0, 0] = dot(dzh_ref[...], exact) + dot(dzl_ref[...], exact)


def base_stage(ints, widths, heights, base, table, stack, dz_high, dz_low):
    smem = pl.BlockSpec(memory_space=pltpu.SMEM)

    def whole(shape):
        return pl.BlockSpec(shape, lambda i: (0,) * len(shape))

    return pl.pallas_call(
        base_body,
        grid=(6,),
        in_specs=[
            smem, smem, smem,
            pl.BlockSpec((1, 1, Q, Q * PLANES), lambda i: (i // 2, i % 2, 0, 0)),
            whole(table.shape), whole(stack.shape), whole(dz_high.shape), whole(dz_low.shape),
        ],
        out_specs=[
            pl.BlockSpec((4, 1, 1, PLANES, LANES), lambda i: (0, i // 2, i % 2, 0, 0)),
            whole((2 * PLANES, PLANES)), whole((2 * PLANES, PLANES)),
            whole((PLANES, PLANES)), whole((PLANES, PLANES)),
        ],
        out_shape=[
            jax.ShapeDtypeStruct((4, 3, 2, PLANES, LANES), F32),
            jax.ShapeDtypeStruct((2 * PLANES, PLANES), BF16),
            jax.ShapeDtypeStruct((2 * PLANES, PLANES), BF16),
            jax.ShapeDtypeStruct((PLANES, PLANES), BF16),
            jax.ShapeDtypeStruct((PLANES, PLANES), BF16),
        ],
        scratch_shapes=[pltpu.VMEM((352, PLANES), BF16)],
        name="base_stage",
    )(ints, widths, heights, base, table, stack, dz_high, dz_low)


def lines_body(ints, widths, heights, in_ref, field_ref, fgh_ref, fgl_ref, fh_ref, fl_ref,
               dh_ref, dl_ref, mass_ref, out_ref):
    ey = pl.program_id(0)
    width, height = widths[ints[0]], heights[ey]
    coeffs = [in_ref[:, c, 0].reshape(PLANES, LANES) for c in range(3)]
    high, low = split(jnp.concatenate(coeffs, axis=1))
    both = dot(fgh_ref[...], high) + dot(fgh_ref[...], low) + dot(fgl_ref[...], high)
    lines = [both[:PLANES, c * LANES : (c + 1) * LANES] for c in range(3)]
    slopes = [None, None, [both[PLANES:, c * LANES : (c + 1) * LANES] for c in range(3)]]
    high, low = split(jnp.concatenate(lines, axis=0))
    plane = dot(high, dh_ref[...]) + dot(low, dh_ref[...]) + dot(high, dl_ref[...])
    per_c = [plane[c * PLANES : (c + 1) * PLANES] for c in range(3)]
    slopes[0] = [part[:, :LANES] * (2.0 / width) for part in per_c]
    slopes[1] = [part[:, LANES:] * (2.0 / height) for part in per_c]
    pieces = []
    for c in range(3):
        total = field_ref[0, 0, 0] * slopes[0][c]
        for d in range(1, 3):
            total = total + field_ref[0, d, 0] * slopes[d][c]
        for d in range(3):
            total = total - lines[d] * field_ref[1 + c, d, 0]
        pieces.append(total)
    high, low = split(jnp.concatenate(pieces, axis=1))
    hat = dot(fh_ref[...], high) + dot(fh_ref[...], low) + dot(fl_ref[...], high)
    mass = mass_ref[...] * (width * height * 0.25)
    lane = lane_ids((PLANES, LANES))
    for c in range(3):
        source = SIGMA * coeffs[c] + hat[:, c * LANES : (c + 1) * LANES] * (1.0 / NU)
        value = jnp.where(lane < NODES, mass * source, width)
        out_ref[:, c, 0] = value.reshape(PEERS, LOCAL, LANES)


def lines_stage(ints, widths, heights, arrived, fields, tables, d_high, d_low, mass):
    smem = pl.BlockSpec(memory_space=pltpu.SMEM)

    def whole(array):
        return pl.BlockSpec(array.shape, lambda i: (0,) * array.ndim)

    block = pl.BlockSpec((PEERS, 3, 1, LOCAL, LANES), lambda i: (0, 0, i, 0, 0))
    return pl.pallas_call(
        lines_body,
        grid=(2,),
        in_specs=[
            smem, smem, smem, block,
            pl.BlockSpec((4, 3, 1, PLANES, LANES), lambda i: (0, 0, i, 0, 0)),
        ] + [whole(a) for a in tables] + [whole(d_high), whole(d_low), whole(mass)],
        out_specs=block,
        out_shape=jax.ShapeDtypeStruct((PEERS, 3, 2, LOCAL, LANES), F32),
        name="lines_stage",
    )(ints, widths, heights, arrived, fields, *tables, d_high, d_low, mass)


def join_columns(chunks):
    lane = lane_ids(chunks[0].shape)
    place = lane - Q * ((lane * 5958) >> 16)
    at_first = (place == 0) & (lane < NODES)
    at_last = (place == Q - 1) & (lane < NODES)
    results = []
    for k, chunk in enumerate(chunks):
        if chunk is None:
            results.append(None)
            continue
        extra = 0.0
        if k > 0 and chunks[k - 1] is not None:
            extra = jnp.where(at_first, turn(chunks[k - 1], -(Q - 1)), extra)
        if k + 1 < len(chunks) and chunks[k + 1] is not None:
            extra = jnp.where(at_last, turn(chunks[k + 1], Q - 1), extra)
        results.append(chunk + extra)
    return results


def split3(value):
    high = value.astype(BF16)
    rest = value - high.astype(F32)
    mid = rest.astype(BF16)
    return high, mid, (rest - mid.astype(F32)).astype(BF16)


def dot_split(value, parts):
    high, mid, low = split3(value)
    total = dot(low, parts[0]) + dot(high, parts[2])
    total = total + dot(mid, parts[1])
    total = total + dot(mid, parts[0]) + dot(high, parts[1])
    return total + dot(high, parts[0])


def stiff_rows(stiff, values):
    middle = Q // 2
    even = [values[m] + values[Q - 1 - m] for m in range(middle)] + [values[middle]]
    odd = [values[m] - values[Q - 1 - m] for m in range(middle)]
    results = [None] * Q
    for row in range(middle + 1):
        total = None
        for m in range(middle + 1):
            factor = stiff[row][m] if m == middle or row == middle else (
                0.5 * (stiff[row][m] + stiff[row][Q - 1 - m])
            )
            term = factor * even[m]
            total = term if total is None else total + term
        if row == middle:
            results[row] = total
            continue
        other = None
        for m in range(middle):
            term = (0.5 * (stiff[row][m] - stiff[row][Q - 1 - m])) * odd[m]
            other = term if other is None else other + term
        results[row] = total + other
        results[Q - 1 - row] = total - other
    return results


def krylov_body(stiff_y, weights, ints, heights, own_ref, left_ref, right_ref, kb_ref, kn_ref, wx_ref,
                v0_ref, v1_ref, v2_ref, mom_ref, kxs, kbs, vec, prod, tmp):
    comp = pl.program_id(0)
    column_refs = (
        [left_ref.at[k] for k in range(GHOST)]
        + [own_ref.at[k] for k in range(COLUMNS)]
        + [right_ref.at[k] for k in range(GHOST)]
    )

    @pl.when(comp == 0)
    def _():
        lane = lane_ids((8, LANES))
        widths = [ref[0, 0, 0:8, NODES : NODES + 1] for ref in column_refs]
        zero = jnp.zeros((8, 1), F32)
        widths = [zero] + widths + [zero]
        for t in range(2):
            here = jnp.zeros((8, LANES), F32)
            near = here
            for place in range(Q):
                k = Q * t + place + 1
                low, high = Q * place, Q * place + Q - 1
                here = jnp.where((lane >= low) & (lane <= high), widths[k], here)
                near = jnp.where(lane == low, widths[k - 1], near)
                near = jnp.where(lane == high, widths[k + 1], near)
            vec[0, :, t * LANES : (t + 1) * LANES] = here
            vec[1, :, t * LANES : (t + 1) * LANES] = near
        here, near = vec[0], vec[1]
        line = lane_ids((8, 2 * LANES))
        own = ((line >= GHOST * Q) & (line < NODES)) | (
            (line >= LANES) & (line < LANES + (Q - GHOST) * Q)
        )
        own = own.astype(F32)
        mass_x = here * wx_ref[...]
        vec[2] = mass_x * own
        vec[1] = mass_x + near * wx_ref[...]
        vec[3] = own * jnp.where(near > 0.0, 0.5, 1.0)
        inverse, inverse_near = (
            jnp.where(value > 0.0, 1.0 / jnp.where(value > 0.0, value, 1.0), 0.0)[0:1]
            for value in (here, near)
        )
        scaled = kb_ref[...] * inverse
        for k, part in enumerate(split3(scaled + kn_ref[...] * inverse_near)):
            kxs[k] = part
        for k, part in enumerate(split3(scaled * own[0:1])):
            kbs[k] = part

    first, second, third = v0_ref.at[0], v1_ref.at[0], v2_ref.at[0]
    before = [None, None]
    for ey in range(2):
        chunks = join_columns([ref[0, ey] for ref in column_refs])
        for t in range(2):
            placed = block_transpose(chunks[Q * t : Q * t + Q], Q)
            for qy in range(Q):
                value = placed[qy]
                y = qy + (Q - 1) * ey
                if ey == 0 and qy == Q - 1:
                    before[t] = value
                    continue
                if ey == 1 and qy == 0:
                    value = value + before[t]
                first[y * LOCAL : (y + 1) * LOCAL, t * LANES : (t + 1) * LANES] = value

    h0, h1 = heights[0], heights[1]
    inverse_y = (1.0 / h0, 1.0 / h1)
    mass_y = []
    for y in range(ROWS):
        if y < Q - 1:
            mass_y.append(h0 * weights[y])
        elif y == Q - 1:
            mass_y.append((h0 + h1) * weights[0])
        else:
            mass_y.append(h1 * weights[y - Q + 1])

    def apply(source, target, operator, mass_row, low_key):
        tmp[...] = dot_split(source[...], [operator[k] for k in range(3)])
        sums = [[], []]
        for half in range(2):
            plane = ints[0] * LOCAL + half * 8 + lax.broadcasted_iota(jnp.int32, (8, LANES), 0)
            kappa = jnp.where(plane == 1, PLANES // 2, plane >> 1).astype(F32)
            beta = kappa * (2.0 * np.pi / (PLANES / 64.0))
            lam = (beta * beta + SIGMA) * 0.25
            square = cross = None
            for t in range(2):
                lanes = slice(t * LANES, (t + 1) * LANES)
                mass_x = vec[mass_row, :, lanes]
                shift = lam * mass_x
                weight = vec[3, :, lanes]
                here_square = here_cross = None
                shared = None
                for ey in range(2):
                    rows = [
                        slice(y * LOCAL + half * 8, y * LOCAL + half * 8 + 8)
                        for y in range((Q - 1) * ey, (Q - 1) * ey + Q)
                    ]
                    values = [source[r, lanes] for r in rows]
                    scale = mass_x * inverse_y[ey]
                    stiff = [scale * value for value in stiff_rows(stiff_y, values)]
                    if ey == 0:
                        shared = stiff.pop()
                    else:
                        stiff[0] = stiff[0] + shared
                    for k, part in enumerate(stiff):
                        y, value = (Q - 1) * ey + k, values[k]
                        image = mass_y[y] * (tmp[rows[k], lanes] + shift * value) + part
                        if target is not None:
                            target[rows[k], lanes] = image
                        one, two = value * value, value * image
                        here_square = one if here_square is None else here_square + one
                        here_cross = two if here_cross is None else here_cross + two
                here_square = here_square * weight
                if target is not None:
                    here_cross = here_cross * weight
                square = here_square if square is None else square + here_square
                cross = here_cross if cross is None else cross + here_cross
            prod[low_key * LOCAL + half * 8 : low_key * LOCAL + half * 8 + 8, :] = square
            prod[(low_key + 1) * LOCAL + half * 8 : (low_key + 1) * LOCAL + half * 8 + 8, :] = cross

    prod[6 * LOCAL :, :] = jnp.zeros((LANES - 6 * LOCAL, LANES), F32)
    apply(first, second, kxs, 1, 0)
    apply(second, third, kxs, 1, 2)
    apply(third, None, kbs, 2, 4)
    row = lax.dot_general(
        jnp.ones((8, LANES), F32), prod[...], (((1,), (1,)), ((), ())),
        precision=HIGHEST, preferred_element_type=F32,
    )
    mom_ref[:, pl.ds(comp, 1), :] = jnp.broadcast_to(row[0:1][None], (mom_ref.shape[0], 1, LANES))


def krylov_stage(stiff_y, weights, ints, heights, own, left, right, kb, near, wx, peers):
    smem = pl.BlockSpec(memory_space=pltpu.SMEM)

    def whole(array):
        return pl.BlockSpec(array.shape, lambda i: (0,) * array.ndim)

    def chunk(count):
        return pl.BlockSpec((count, 1, 2, LOCAL, LANES), lambda i: (0, i, 0, 0, 0))

    vector = pl.BlockSpec((1, ROWS * LOCAL, 2 * LANES), lambda i: (i, 0, 0))
    shape = jax.ShapeDtypeStruct((3, ROWS * LOCAL, 2 * LANES), F32)

    def body(*refs):
        krylov_body(stiff_y, weights, *refs)

    return pl.pallas_call(
        body,
        grid=(3,),
        in_specs=[smem, smem, chunk(COLUMNS), chunk(GHOST), chunk(GHOST), whole(kb), whole(near), whole(wx)],
        out_specs=[vector, vector, vector, pl.BlockSpec((peers, 8, LANES), lambda i: (0, 0, 0))],
        out_shape=[shape, shape, shape, jax.ShapeDtypeStruct((peers, 8, LANES), F32)],
        scratch_shapes=[
            pltpu.VMEM((3, 2 * LANES, 2 * LANES), BF16),
            pltpu.VMEM((3, 2 * LANES, 2 * LANES), BF16),
            pltpu.VMEM((4, 8, 2 * LANES), F32),
            pltpu.VMEM((LANES, LANES), F32),
            pltpu.VMEM((ROWS * LOCAL, 2 * LANES), F32),
        ],
        name="krylov_stage",
    )(ints, heights, own, left, right, kb, near, wx)


def unpack_body(v0_ref, v1_ref, v2_ref, u0_ref, u1_ref, u2_ref, scr, flat):
    lane = lane_ids((16, LANES))
    run = COLUMNS * Q // 2
    for vector, target in ((v0_ref, u0_ref), (v1_ref, u1_ref), (v2_ref, u2_ref)):
        for y in range(ROWS):
            rows = slice(y * LOCAL, (y + 1) * LOCAL)
            for t in range(2):
                value = vector[0, rows, t * LANES : (t + 1) * LANES]
                if y <= Q - 1:
                    scr[0, t, pl.ds(y, LOCAL, stride=16), :] = value
                if y >= Q - 1:
                    scr[1, t, pl.ds(y - Q + 1, LOCAL, stride=16), :] = value
        for ey in range(2):
            turned = []
            for r in range(2 * LOCAL):
                start = GHOST * Q if r % 2 == 0 else 0
                value = scr[ey, r % 2, (r // 2) * 16 : (r // 2) * 16 + 16, :]
                turned.append(turn(value, run * r - start))
            for tile in range(COLUMNS * Q * LOCAL // LANES):
                low, high = tile * LANES // run, (tile * LANES + LANES - 1) // run
                value = turned[low]
                for r in range(low + 1, high + 1):
                    value = jnp.where(lane >= run * r - LANES * tile, turned[r], value)
                flat[tile, ey * 16 : ey * 16 + 16, :] = value
        for qy in range(Q):
            for tile in range(COLUMNS * Q * LOCAL // LANES):
                target[0, qy, :, tile * LANES : (tile + 1) * LANES] = flat[
                    tile, pl.ds(qy, 2, stride=16), :
                ]


def unpack(v0, v1, v2):
    vector = pl.BlockSpec((1, ROWS * LOCAL, 2 * LANES), lambda i: (i, 0, 0))
    target = pl.BlockSpec((1, Q, 2, COLUMNS * Q * LOCAL), lambda i: (i, 0, 0, 0))
    shape = jax.ShapeDtypeStruct((3, Q, 2, COLUMNS * Q * LOCAL), F32)
    return pl.pallas_call(
        unpack_body,
        grid=(3,),
        in_specs=[vector] * 3,
        out_specs=[target] * 3,
        out_shape=[shape] * 3,
        scratch_shapes=[
            pltpu.VMEM((2, 2, 256, LANES), F32),
            pltpu.VMEM((COLUMNS * Q * LOCAL // LANES, 32, LANES), F32),
        ],
        name="unpack",
    )(v0, v1, v2)


def finish_body(mom_ref, u0_ref, u1_ref, u2_ref, out_ref, coef):
    comp = pl.program_id(0)
    tiles = COLUMNS * Q * LOCAL // LANES

    @pl.when(comp == 0)
    def _():
        total = jnp.sum(mom_ref[...], axis=0)
        used = (lane_ids((8, LANES)) < LOCAL) & (
            lax.broadcasted_iota(jnp.int32, (8, LANES), 0) < 3
        )
        m = [jnp.where(used, turn(total, -LOCAL * k), 1.0) for k in range(6)]
        inv = 1.0 / m[0]
        m = [value * inv for value in m]
        d0, d1, d2 = (1.0 / jnp.sqrt(m[k]) for k in (1, 3, 5))
        g0, g1, g2 = d0, m[1] * d1, m[2] * d2
        l10 = m[2] * d0 * d1
        l20 = m[3] * d0 * d2
        k21 = m[4] * d1 * d2
        p1 = 1.0 - l10 * l10
        e = k21 - l20 * l10
        l21 = e / p1
        p2 = 1.0 - l20 * l20 - l21 * e
        y1 = g1 - l10 * g0
        y2 = g2 - l20 * g0 - l21 * y1
        z2 = y2 / p2
        z1 = y1 / p1 - l21 * z2
        z0 = g0 - l10 * z1 - l20 * z2
        lane = lane_ids((8, LANES))
        for k, value in enumerate((z0 * d0, z1 * d1, z2 * d2)):
            wide = [jnp.broadcast_to(value[:, j : j + 1], (8, LANES)) for j in range(LOCAL)]
            for tile in range(tiles):
                low = tile * LANES // (COLUMNS * Q)
                high = (tile * LANES + LANES - 1) // (COLUMNS * Q)
                chosen = wide[low]
                if high > low:
                    chosen = jnp.where(lane >= COLUMNS * Q * high - LANES * tile, wide[high], chosen)
                coef[k, tile] = chosen

    for tile in range(tiles):
        lanes = slice(tile * LANES, (tile + 1) * LANES)
        c0, c1, c2 = (
            jnp.broadcast_to(coef[k, tile, pl.ds(comp, 1), :], (2, LANES)) for k in range(3)
        )
        for qy in range(Q):
            out_ref[0, qy, :, lanes] = (
                c0 * u0_ref[0, qy, :, lanes]
                + c1 * u1_ref[0, qy, :, lanes]
                + c2 * u2_ref[0, qy, :, lanes]
            )


def finish(moments, u0, u1, u2):
    target = pl.BlockSpec((1, Q, 2, COLUMNS * Q * LOCAL), lambda i: (i, 0, 0, 0))
    out = pl.pallas_call(
        finish_body,
        grid=(3,),
        in_specs=[pl.BlockSpec(moments.shape, lambda i: (0, 0, 0)), target, target, target],
        out_specs=target,
        out_shape=jax.ShapeDtypeStruct((3, Q, 2, COLUMNS * Q * LOCAL), F32),
        scratch_shapes=[pltpu.VMEM((3, COLUMNS * Q * LOCAL // LANES, 8, LANES), F32)],
        name="finish",
    )(moments, u0, u1, u2)
    return jnp.transpose(out, (0, 2, 1, 3))


def make_tables():
    derivative, weights = gll_tables(Q)
    basis, basis_slope, span_slope = fourier_table(PLANES)
    table = np.concatenate([basis.T, basis_slope.T], axis=1)
    table = table.astype(np.float32)
    eye = np.eye(Q)
    nodes = np.zeros((2, LANES, LANES))
    nodes[0, :NODES, :NODES] = np.kron(eye, derivative.T)
    nodes[1, :NODES, :NODES] = np.kron(derivative.T, eye)
    order = np.zeros((176, LANES))
    for qx in range(Q):
        for qy in range(Q):
            order[qx * 16 + qy, qy * Q + qx] = 1.0
    stack = np.concatenate([order, order @ nodes[0], order @ nodes[1]], axis=1)
    stack = np.concatenate(halves(stack), axis=0)
    plane = np.concatenate([nodes[0], nodes[1]], axis=1)
    mass = np.zeros((1, LANES), np.float32)
    mass[0, :NODES] = np.kron(weights, weights)
    stiff = (derivative.T * weights) @ derivative
    kb = np.zeros((2 * LANES, 2 * LANES))
    join = np.eye(2 * LANES)
    wx = np.zeros((1, 2 * LANES), np.float32)
    ends = []
    for t in range(2):
        for place in range(Q):
            low = t * LANES + place * Q
            kb[low : low + Q, low : low + Q] = stiff
            wx[0, low : low + Q] = weights
            ends.append(low)
    for left, right in zip(ends[:-1], ends[1:]):
        join[left + Q - 1, right] = 1.0
        join[right, left + Q - 1] = 1.0
    return dict(
        table=table, stack=stack, dz=halves(span_slope), plane=halves(plane), mass=mass,
        kb=kb.astype(np.float32), near=(kb @ join - kb).astype(np.float32), wx=wx,
        stiff=stiff.tolist(), weights=weights.tolist(),
    )


def local(adjoint_velocity, base_flow, column_widths, row_heights, base_phase):
    tables = make_tables()
    elem_count = lax.axis_size("elem")
    ints = jnp.stack([lax.axis_index("four").astype(jnp.int32), base_phase[0]])
    send = pack(adjoint_velocity)
    arrived = lax.all_to_all(send, "four", split_axis=0, concat_axis=0, tiled=True)
    fields, *turned = base_stage(
        ints, column_widths, row_heights, base_flow, jnp.asarray(tables["table"]),
        jnp.asarray(tables["stack"]), *(jnp.asarray(a) for a in tables["dz"]),
    )
    source = lines_stage(
        ints, column_widths, row_heights, arrived, fields, turned,
        *(jnp.asarray(a) for a in tables["plane"]), jnp.asarray(tables["mass"]),
    )
    own = lax.all_to_all(source, "four", split_axis=0, concat_axis=0, tiled=True)
    up = [(i, i + 1) for i in range(elem_count - 1)]
    left = lax.ppermute(own[COLUMNS - GHOST :], "elem", up)
    right = lax.ppermute(own[:GHOST], "elem", [(j, i) for i, j in up])
    v0, v1, v2, moments = krylov_stage(
        tables["stiff"], tables["weights"], ints, row_heights, own, left, right,
        jnp.asarray(tables["kb"]), jnp.asarray(tables["near"]), jnp.asarray(tables["wx"]), elem_count,
    )
    moments = lax.all_to_all(moments, "elem", split_axis=0, concat_axis=0, tiled=True)
    return finish(moments, *unpack(v0, v1, v2))


def solution(mesh):
    split_spec = P(None, None, None, ("elem", "four"))
    return jax.shard_map(
        local,
        mesh=mesh,
        in_specs=(split_spec, split_spec, P("elem"), P(), P()),
        out_specs=split_spec,
        check_vma=False,
    )
```

```python
import jax
import jax.numpy as jnp
import numpy as np
from jax import lax
from jax.experimental import pallas as pl
from jax.experimental.pallas import tpu as pltpu
from jax.sharding import PartitionSpec as P

Q = 11
PLANES = 256
PEERS = 16
LOCAL = 16
COLUMNS = 16
GHOST = 3
ROWS = 21
NODES = Q * Q
LANES = 128
NU = 0.005
DT = 0.01
SIGMA = 1.0 / (NU * DT)
HIGHEST = lax.Precision.HIGHEST
F32 = jnp.float32
BF16 = jnp.bfloat16


def legendre_values(points, node_count):
    table_rows = np.zeros((points.shape[0], node_count))
    table_rows[:, 0] = 1.0
    table_rows[:, 1] = points
    for degree_now in range(2, node_count):
        table_rows[:, degree_now] = (
            (2 * degree_now - 1) * points * table_rows[:, degree_now - 1]
            - (degree_now - 1) * table_rows[:, degree_now - 2]
        ) / degree_now
    return table_rows


def gll_tables(node_count):
    degree = node_count - 1
    points = np.cos(np.pi * np.arange(node_count) / degree)
    for newton_step in range(60):
        legendre = legendre_values(points, node_count)
        points = points - (points * legendre[:, degree] - legendre[:, degree - 1]) / (
            node_count * legendre[:, degree]
        )
    legendre = legendre_values(points, node_count)
    weights = 2.0 / (degree * node_count * legendre[:, degree] ** 2)
    points = points[::-1]
    weights = weights[::-1]
    end_values = legendre[::-1, degree]
    derivative = np.zeros((node_count, node_count))
    for row_index in range(node_count):
        for column in range(node_count):
            if row_index != column:
                derivative[row_index, column] = end_values[row_index] / (
                    end_values[column] * (points[row_index] - points[column])
                )
    derivative[0, 0] = -degree * node_count / 4.0
    derivative[degree, degree] = degree * node_count / 4.0
    return derivative, weights


def fourier_table(plane_count):
    positions = np.arange(plane_count)
    basis_rows = np.zeros((plane_count, plane_count))
    basis_rows[0] = 1.0 / np.sqrt(plane_count)
    basis_rows[1] = np.cos(np.pi * positions) / np.sqrt(plane_count)
    for wave_index in range(1, plane_count // 2):
        angle = 2.0 * np.pi * wave_index * positions / plane_count
        basis_rows[2 * wave_index] = np.sqrt(2.0 / plane_count) * np.cos(angle)
        basis_rows[2 * wave_index + 1] = np.sqrt(2.0 / plane_count) * np.sin(angle)
    wave_counts = np.arange(plane_count) // 2
    wave_counts[1] = plane_count // 2
    wave_counts[0] = 0
    wavenumbers = 2.0 * np.pi * wave_counts / (plane_count / 64.0)
    rotate = np.zeros((plane_count, plane_count))
    for wave_index in range(1, plane_count // 2):
        rotate[2 * wave_index, 2 * wave_index + 1] = wavenumbers[2 * wave_index]
        rotate[2 * wave_index + 1, 2 * wave_index] = -wavenumbers[2 * wave_index]
    return basis_rows, rotate.T @ basis_rows, basis_rows.T @ rotate @ basis_rows


def halves(array):
    high = np.asarray(array, np.float32).astype(jnp.bfloat16)
    low = (np.asarray(array, np.float64) - high.astype(np.float64)).astype(jnp.bfloat16)
    return high, low


def split(value):
    high = value.astype(BF16)
    return high, (value - high.astype(F32)).astype(BF16)


def dot(left, right):
    return jnp.dot(left, right, preferred_element_type=F32)


def dot3(left_high, left_low, high, low):
    half = left_high.shape[0] // 2
    parts = [slice(0, half), slice(half, None)]
    totals = [dot(left_high[p], low) for p in parts]
    totals = [t + dot(left_low[p], high) for t, p in zip(totals, parts)]
    return [t + dot(left_high[p], high) for t, p in zip(totals, parts)]


def dot_full(left, right):
    return jnp.dot(left, right, precision=HIGHEST, preferred_element_type=F32)


def in_hbm(array):
    return pltpu.with_memory_space_constraint(array, pltpu.HBM)


def lane_ids(shape):
    return lax.broadcasted_iota(jnp.int32, shape, len(shape) - 1)


def turn(value, shift):
    shift = shift % LANES
    return value if shift == 0 else pltpu.roll(value, shift, value.ndim - 1)


def block_transpose(arrays, count):
    lane = lane_ids(arrays[0].shape)
    turned = [turn(array, Q * k) for k, array in enumerate(arrays)]
    results = []
    for place in range(count):
        distance = (lane - Q * place) & (LANES - 1)
        chosen = turned[0]
        for k in range(1, len(turned)):
            chosen = jnp.where(distance >= Q * k, turned[k], chosen)
        chosen = jnp.where(distance < NODES, chosen, 0.0)
        results.append(turn(chosen, -Q * place))
    return results


def pack_body(in_ref, out_ref, flat, scr0, scr1):
    lane = lane_ids((16, LANES))
    scratches = (scr0, scr1)
    tiles = COLUMNS * Q * LOCAL // LANES
    for qy in range(Q):
        for tile in range(tiles):
            flat[tile, pl.ds(qy, 2, stride=16), :] = in_ref[0, qy, :, tile * LANES : (tile + 1) * LANES]
    for ey in range(2):
        rows = slice(ey * 16, ey * 16 + 16)
        for j in range(LOCAL):
            for t in range(2):
                offset = j * COLUMNS * Q + NODES * t
                tile, shift = offset // LANES, offset % LANES
                first = flat[tile, rows, :]
                if shift and tile + 1 < tiles:
                    first = jnp.where(lane >= shift, first, flat[tile + 1, rows, :])
                scratches[t][ey, j * 16 : j * 16 + 16, :] = turn(first, -shift)
    for ey in range(2):
        for t in range(2):
            rows = [scratches[t][ey, pl.ds(qy, LOCAL, stride=16), :] for qy in range(Q)]
            for place, value in enumerate(block_transpose(rows, Q if t == 0 else COLUMNS - Q)):
                out_ref[Q * t + place, 0, ey] = value


def pack(adjoint):
    return pl.pallas_call(
        pack_body,
        grid=(3,),
        in_specs=[pl.BlockSpec((1, Q, 2, COLUMNS * Q * LOCAL), lambda i: (i, 0, 0, 0))],
        out_specs=pl.BlockSpec((PEERS, 1, 2, LOCAL, LANES), lambda i: (0, i, 0, 0, 0)),
        out_shape=jax.ShapeDtypeStruct((PEERS, 3, 2, LOCAL, LANES), F32),
        scratch_shapes=[
            pltpu.VMEM((COLUMNS * Q * LOCAL // LANES, 32, LANES), F32),
            pltpu.VMEM((2, 256, LANES), F32),
            pltpu.VMEM((2, 256, LANES), F32),
        ],
        name="pack",
    )(jnp.transpose(adjoint, (0, 2, 1, 3)))


def base_body(ints, widths, heights, base_ref, table_ref, stack_ref, dzh_ref, dzl_ref,
              field_ref, fgh_ref, fgl_ref, fh_ref, fl_ref, scr):
    step = pl.program_id(0)

    @pl.when(step == 0)
    def _():
        scr[...] = jnp.zeros_like(scr)
        rows = pltpu.roll(table_ref[...], (PLANES - ints[1]) % PLANES, 0)
        for k in range(2):
            high, low = split(rows[:, k * PLANES : (k + 1) * PLANES])
            fgh_ref[k * PLANES : (k + 1) * PLANES, :] = high
            fgl_ref[k * PLANES : (k + 1) * PLANES, :] = low
        high, low = split(jnp.transpose(rows[:, :PLANES]))
        fh_ref[...] = high
        fl_ref[...] = low

    for qx in range(Q):
        part = base_ref[0, 0, :, qx * PLANES : (qx + 1) * PLANES]
        scr[qx * 16 : qx * 16 + Q, :] = part
        scr[176 + qx * 16 : 176 + qx * 16 + Q, :] = part
    mixed = lax.dot_general(
        scr[...], stack_ref[...], (((0,), (0,)), ((), ())), preferred_element_type=F32
    )
    plain = mixed[:, :LANES]
    field_ref[0, 0, 0] = plain
    field_ref[1, 0, 0] = mixed[:, LANES : 2 * LANES] * (2.0 / widths[ints[0]])
    field_ref[2, 0, 0] = mixed[:, 2 * LANES :] * (2.0 / heights[step % 2])
    exact = plain.astype(BF16)
    field_ref[3, 0, 0] = dot(dzh_ref[...], exact) + dot(dzl_ref[...], exact)


def base_stage(ints, widths, heights, base, table, stack, dz_high, dz_low):
    smem = pl.BlockSpec(memory_space=pltpu.SMEM)

    def whole(shape):
        return pl.BlockSpec(shape, lambda i: (0,) * len(shape))

    return pl.pallas_call(
        base_body,
        grid=(6,),
        in_specs=[
            smem, smem, smem,
            pl.BlockSpec((1, 1, Q, Q * PLANES), lambda i: (i // 2, i % 2, 0, 0)),
            whole(table.shape), whole(stack.shape), whole(dz_high.shape), whole(dz_low.shape),
        ],
        out_specs=[
            pl.BlockSpec((4, 1, 1, PLANES, LANES), lambda i: (0, i // 2, i % 2, 0, 0)),
            whole((2 * PLANES, PLANES)), whole((2 * PLANES, PLANES)),
            whole((PLANES, PLANES)), whole((PLANES, PLANES)),
        ],
        out_shape=[
            jax.ShapeDtypeStruct((4, 3, 2, PLANES, LANES), F32),
            jax.ShapeDtypeStruct((2 * PLANES, PLANES), BF16),
            jax.ShapeDtypeStruct((2 * PLANES, PLANES), BF16),
            jax.ShapeDtypeStruct((PLANES, PLANES), BF16),
            jax.ShapeDtypeStruct((PLANES, PLANES), BF16),
        ],
        scratch_shapes=[pltpu.VMEM((352, PLANES), BF16)],
        name="base_stage",
    )(ints, widths, heights, base, table, stack, dz_high, dz_low)


def lines_body(ints, widths, heights, in_ref, field_hbm, fgh_ref, fgl_ref, fh_ref, fl_ref,
               dh_ref, dl_ref, mass_ref, out_ref, fields, lines, slopes, sems):
    copies = [
        pltpu.make_async_copy(field_hbm.at[k], fields.at[k], sems.at[k]) for k in range(4)
    ]
    for copy in copies:
        copy.start()
    width = widths[ints[0]]
    pairs = [((2 * p) // 2, (2 * p) % 2, (2 * p + 1) % 2) for p in range(3)]
    double_dh = jnp.concatenate([dh_ref[...], dh_ref[...]], axis=0)

    def coeffs(c, ey):
        return in_ref[:, c, ey].reshape(PLANES, LANES)

    for c, _, _ in pairs:
        high, low = split(jnp.concatenate([coeffs(c, 0), coeffs(c, 1)], axis=1))
        both = dot3(fgh_ref[...], fgl_ref[...], high, low)
        for ey in range(2):
            line = both[0][:, ey * LANES : (ey + 1) * LANES]
            lines[c, ey] = line
            slopes[2, c, ey] = both[1][:, ey * LANES : (ey + 1) * LANES]
            high_line, low_line = split(line)
            wide = jnp.concatenate([high_line, low_line], axis=1)
            parts = [slice(0, LANES), slice(LANES, PLANES)]
            planes = [dot(wide[p], double_dh) for p in parts]
            planes = [v + dot(high_line[p], dl_ref[...]) for v, p in zip(planes, parts)]
            for plane, p in zip(planes, parts):
                slopes[0, c, ey, p] = plane[:, :LANES] * (2.0 / width)
                slopes[1, c, ey, p] = plane[:, LANES:] * (2.0 / heights[ey])
    for copy in copies:
        copy.wait()
    lane = lane_ids((PLANES, LANES))
    for c in range(3):
        pieces = []
        for ey in range(2):
            total = fields[0, 0, ey] * slopes[0, c, ey]
            for d in range(1, 3):
                total = total + fields[0, d, ey] * slopes[d, c, ey]
            for d in range(3):
                total = total - lines[d, ey] * fields[1 + c, d, ey]
            pieces.append(total)
        high, low = split(jnp.concatenate(pieces, axis=1))
        hat = jnp.concatenate(dot3(fh_ref[...], fl_ref[...], high, low), axis=0)
        for ey in range(2):
            mass = mass_ref[...] * (width * heights[ey] * 0.25)
            source = SIGMA * coeffs(c, ey) + hat[:, ey * LANES : (ey + 1) * LANES] * (1.0 / NU)
            value = jnp.where(lane < NODES, mass * source, width)
            out_ref[:, c, ey] = value.reshape(PEERS, LOCAL, LANES)


def lines_stage(ints, widths, heights, arrived, fields, tables, d_high, d_low, mass):
    smem = pl.BlockSpec(memory_space=pltpu.SMEM)

    def whole(array):
        return pl.BlockSpec(array.shape, lambda i: (0,) * array.ndim)

    return pl.pallas_call(
        lines_body,
        grid=(1,),
        in_specs=[smem, smem, smem, whole(arrived), pl.BlockSpec(memory_space=pl.ANY)]
        + [whole(a) for a in tables] + [whole(d_high), whole(d_low), whole(mass)],
        out_specs=whole(arrived),
        out_shape=jax.ShapeDtypeStruct((PEERS, 3, 2, LOCAL, LANES), F32),
        scratch_shapes=[
            pltpu.VMEM((4, 3, 2, PLANES, LANES), F32),
            pltpu.VMEM((3, 2, PLANES, LANES), F32),
            pltpu.VMEM((3, 3, 2, PLANES, LANES), F32),
            pltpu.SemaphoreType.DMA((4,)),
        ],
        compiler_params=pltpu.CompilerParams(vmem_limit_bytes=24 * 2**20),
        name="lines_stage",
    )(*map(in_hbm, (ints, widths, heights)), arrived, in_hbm(fields), *map(in_hbm, tables), d_high, d_low, mass)


def join_columns(chunks):
    lane = lane_ids(chunks[0].shape)
    place = lane - Q * ((lane * 5958) >> 16)
    at_first = (place == 0) & (lane < NODES)
    at_last = (place == Q - 1) & (lane < NODES)
    results = []
    for k, chunk in enumerate(chunks):
        if chunk is None:
            results.append(None)
            continue
        extra = 0.0
        if k > 0 and chunks[k - 1] is not None:
            extra = jnp.where(at_first, turn(chunks[k - 1], -(Q - 1)), extra)
        if k + 1 < len(chunks) and chunks[k + 1] is not None:
            extra = jnp.where(at_last, turn(chunks[k + 1], Q - 1), extra)
        results.append(chunk + extra)
    return results


def split3(value):
    high = value.astype(BF16)
    rest = value - high.astype(F32)
    mid = rest.astype(BF16)
    return high, mid, (rest - mid.astype(F32)).astype(BF16)


def dot_split(source, target, operator):
    cut = 176
    parts = [slice(0, cut), slice(cut, ROWS * LOCAL)]
    pieces = [split3(source[p, :]) for p in parts]
    totals = [None, None]
    for left, right in ((2, 0), (0, 2), (1, 1), (1, 0), (0, 1), (0, 0)):
        for k in range(2):
            value = dot(pieces[k][left], operator[right])
            totals[k] = value if totals[k] is None else totals[k] + value
    for k in range(2):
        target[parts[k], :] = totals[k]


def stiff_rows(stiff, values):
    middle = Q // 2
    even = [values[m] + values[Q - 1 - m] for m in range(middle)] + [values[middle]]
    odd = [values[m] - values[Q - 1 - m] for m in range(middle)]
    results = [None] * Q
    for row in range(middle + 1):
        total = None
        for m in range(middle + 1):
            factor = stiff[row][m] if m == middle or row == middle else (
                0.5 * (stiff[row][m] + stiff[row][Q - 1 - m])
            )
            term = factor * even[m]
            total = term if total is None else total + term
        if row == middle:
            results[row] = total
            continue
        other = None
        for m in range(middle):
            term = (0.5 * (stiff[row][m] - stiff[row][Q - 1 - m])) * odd[m]
            other = term if other is None else other + term
        results[row] = total + other
        results[Q - 1 - row] = total - other
    return results


def krylov_body(stiff_y, weights, ints, heights, own_ref, left_ref, right_ref, kb_ref, kn_ref, wx_ref,
                v0_ref, v1_ref, v2_ref, mom_ref, kxs, kbs, vec, prod, tmp):
    comp = pl.program_id(0)
    column_refs = (
        [left_ref.at[k] for k in range(GHOST)]
        + [own_ref.at[k] for k in range(COLUMNS)]
        + [right_ref.at[k] for k in range(GHOST)]
    )

    @pl.when(comp == 0)
    def _():
        lane = lane_ids((8, LANES))
        widths = [ref[0, 0, 0:8, NODES : NODES + 1] for ref in column_refs]
        zero = jnp.zeros((8, 1), F32)
        widths = [zero] + widths + [zero]
        for t in range(2):
            here = jnp.zeros((8, LANES), F32)
            near = here
            for place in range(Q):
                k = Q * t + place + 1
                low, high = Q * place, Q * place + Q - 1
                here = jnp.where((lane >= low) & (lane <= high), widths[k], here)
                near = jnp.where(lane == low, widths[k - 1], near)
                near = jnp.where(lane == high, widths[k + 1], near)
            vec[0, :, t * LANES : (t + 1) * LANES] = here
            vec[1, :, t * LANES : (t + 1) * LANES] = near
        here, near = vec[0], vec[1]
        line = lane_ids((8, 2 * LANES))
        own = ((line >= GHOST * Q) & (line < NODES)) | (
            (line >= LANES) & (line < LANES + (Q - GHOST) * Q)
        )
        own = own.astype(F32)
        mass_x = here * wx_ref[...]
        vec[2] = mass_x * own
        vec[1] = mass_x + near * wx_ref[...]
        vec[3] = own * jnp.where(near > 0.0, 0.5, 1.0)
        inverse, inverse_near = (
            jnp.where(value > 0.0, 1.0 / jnp.where(value > 0.0, value, 1.0), 0.0)[0:1]
            for value in (here, near)
        )
        scaled = kb_ref[...] * inverse
        for k, part in enumerate(split3(scaled + kn_ref[...] * inverse_near)):
            kxs[k] = part
        for k, part in enumerate(split3(scaled * own[0:1])):
            kbs[k] = part

    first, second, third = v0_ref.at[0], v1_ref.at[0], v2_ref.at[0]
    before = [None, None]
    for ey in range(2):
        chunks = join_columns([ref[0, ey] for ref in column_refs])
        for t in range(2):
            placed = block_transpose(chunks[Q * t : Q * t + Q], Q)
            for qy in range(Q):
                value = placed[qy]
                y = qy + (Q - 1) * ey
                if ey == 0 and qy == Q - 1:
                    before[t] = value
                    continue
                if ey == 1 and qy == 0:
                    value = value + before[t]
                first[y * LOCAL : (y + 1) * LOCAL, t * LANES : (t + 1) * LANES] = value

    h0, h1 = heights[0], heights[1]
    inverse_y = (1.0 / h0, 1.0 / h1)
    mass_y = []
    for y in range(ROWS):
        if y < Q - 1:
            mass_y.append(h0 * weights[y])
        elif y == Q - 1:
            mass_y.append((h0 + h1) * weights[0])
        else:
            mass_y.append(h1 * weights[y - Q + 1])

    def apply(source, target, operator, mass_row, low_key):
        dot_split(source, tmp, operator)
        sums = [[], []]
        for half in range(2):
            plane = ints[0] * LOCAL + half * 8 + lax.broadcasted_iota(jnp.int32, (8, LANES), 0)
            kappa = jnp.where(plane == 1, PLANES // 2, plane >> 1).astype(F32)
            beta = kappa * (2.0 * np.pi / (PLANES / 64.0))
            lam = (beta * beta + SIGMA) * 0.25
            square = cross = None
            for t in range(2):
                lanes = slice(t * LANES, (t + 1) * LANES)
                mass_x = vec[mass_row, :, lanes]
                shift = lam * mass_x
                weight = vec[3, :, lanes]
                here_square = here_cross = None
                shared = None
                for ey in range(2):
                    rows = [
                        slice(y * LOCAL + half * 8, y * LOCAL + half * 8 + 8)
                        for y in range((Q - 1) * ey, (Q - 1) * ey + Q)
                    ]
                    values = [source[r, lanes] for r in rows]
                    scale = mass_x * inverse_y[ey]
                    stiff = [scale * value for value in stiff_rows(stiff_y, values)]
                    if ey == 0:
                        shared = stiff.pop()
                    else:
                        stiff[0] = stiff[0] + shared
                    for k, part in enumerate(stiff):
                        y, value = (Q - 1) * ey + k, values[k]
                        image = mass_y[y] * (tmp[rows[k], lanes] + shift * value) + part
                        if target is not None:
                            target[rows[k], lanes] = image
                        one, two = value * value, value * image
                        here_square = one if here_square is None else here_square + one
                        here_cross = two if here_cross is None else here_cross + two
                here_square = here_square * weight
                if target is not None:
                    here_cross = here_cross * weight
                square = here_square if square is None else square + here_square
                cross = here_cross if cross is None else cross + here_cross
            prod[low_key * LOCAL + half * 8 : low_key * LOCAL + half * 8 + 8, :] = square
            prod[(low_key + 1) * LOCAL + half * 8 : (low_key + 1) * LOCAL + half * 8 + 8, :] = cross

    prod[6 * LOCAL :, :] = jnp.zeros((LANES - 6 * LOCAL, LANES), F32)
    apply(first, second, kxs, 1, 0)
    apply(second, third, kxs, 1, 2)
    apply(third, None, kbs, 2, 4)
    row = lax.dot_general(
        jnp.ones((8, LANES), F32), prod[...], (((1,), (1,)), ((), ())),
        precision=HIGHEST, preferred_element_type=F32,
    )
    mom_ref[:, pl.ds(comp, 1), :] = jnp.broadcast_to(row[0:1][None], (mom_ref.shape[0], 1, LANES))


def krylov_stage(stiff_y, weights, ints, heights, own, left, right, kb, near, wx, peers):
    smem = pl.BlockSpec(memory_space=pltpu.SMEM)

    def whole(array):
        return pl.BlockSpec(array.shape, lambda i: (0,) * array.ndim)

    def chunk(count):
        return pl.BlockSpec((count, 1, 2, LOCAL, LANES), lambda i: (0, i, 0, 0, 0))

    vector = pl.BlockSpec((1, ROWS * LOCAL, 2 * LANES), lambda i: (i, 0, 0))
    shape = jax.ShapeDtypeStruct((3, ROWS * LOCAL, 2 * LANES), F32)

    def body(*refs):
        krylov_body(stiff_y, weights, *refs)

    return pl.pallas_call(
        body,
        grid=(3,),
        in_specs=[smem, smem, chunk(COLUMNS), chunk(GHOST), chunk(GHOST), whole(kb), whole(near), whole(wx)],
        out_specs=[vector, vector, vector, pl.BlockSpec((peers, 8, LANES), lambda i: (0, 0, 0))],
        out_shape=[shape, shape, shape, jax.ShapeDtypeStruct((peers, 8, LANES), F32)],
        scratch_shapes=[
            pltpu.VMEM((3, 2 * LANES, 2 * LANES), BF16),
            pltpu.VMEM((3, 2 * LANES, 2 * LANES), BF16),
            pltpu.VMEM((4, 8, 2 * LANES), F32),
            pltpu.VMEM((LANES, LANES), F32),
            pltpu.VMEM((ROWS * LOCAL, 2 * LANES), F32),
        ],
        compiler_params=pltpu.CompilerParams(vmem_limit_bytes=24 * 2**20),
        name="krylov_stage",
    )(in_hbm(ints), in_hbm(heights), own, left, right, kb, near, wx)


def unpack_body(v0_ref, v1_ref, v2_ref, u0_ref, u1_ref, u2_ref, scr, flat):
    lane = lane_ids((16, LANES))
    run = COLUMNS * Q // 2
    for vector, target in ((v0_ref, u0_ref), (v1_ref, u1_ref), (v2_ref, u2_ref)):
        for y in range(ROWS):
            rows = slice(y * LOCAL, (y + 1) * LOCAL)
            for t in range(2):
                value = vector[0, rows, t * LANES : (t + 1) * LANES]
                if y <= Q - 1:
                    scr[0, t, pl.ds(y, LOCAL, stride=16), :] = value
                if y >= Q - 1:
                    scr[1, t, pl.ds(y - Q + 1, LOCAL, stride=16), :] = value
        for ey in range(2):
            turned = []
            for r in range(2 * LOCAL):
                start = GHOST * Q if r % 2 == 0 else 0
                value = scr[ey, r % 2, (r // 2) * 16 : (r // 2) * 16 + 16, :]
                turned.append(turn(value, run * r - start))
            for tile in range(COLUMNS * Q * LOCAL // LANES):
                low, high = tile * LANES // run, (tile * LANES + LANES - 1) // run
                value = turned[low]
                for r in range(low + 1, high + 1):
                    value = jnp.where(lane >= run * r - LANES * tile, turned[r], value)
                flat[tile, ey * 16 : ey * 16 + 16, :] = value
        for qy in range(Q):
            for tile in range(COLUMNS * Q * LOCAL // LANES):
                target[0, qy, :, tile * LANES : (tile + 1) * LANES] = flat[
                    tile, pl.ds(qy, 2, stride=16), :
                ]


def unpack(v0, v1, v2):
    vector = pl.BlockSpec((1, ROWS * LOCAL, 2 * LANES), lambda i: (i, 0, 0))
    target = pl.BlockSpec((1, Q, 2, COLUMNS * Q * LOCAL), lambda i: (i, 0, 0, 0))
    shape = pltpu.HBM((3, Q, 2, COLUMNS * Q * LOCAL), F32)
    return pl.pallas_call(
        unpack_body,
        grid=(3,),
        in_specs=[vector] * 3,
        out_specs=[target] * 3,
        out_shape=[shape] * 3,
        scratch_shapes=[
            pltpu.VMEM((2, 2, 256, LANES), F32),
            pltpu.VMEM((COLUMNS * Q * LOCAL // LANES, 32, LANES), F32),
        ],
        compiler_params=pltpu.CompilerParams(vmem_limit_bytes=24 * 2**20),
        name="unpack",
    )(v0, v1, v2)


def finish_body(mom_ref, u0_ref, u1_ref, u2_ref, out_ref, coef):
    comp = pl.program_id(0)
    tiles = COLUMNS * Q * LOCAL // LANES

    @pl.when(comp == 0)
    def _():
        total = jnp.sum(mom_ref[...], axis=0)
        used = (lane_ids((8, LANES)) < LOCAL) & (
            lax.broadcasted_iota(jnp.int32, (8, LANES), 0) < 3
        )
        m = [jnp.where(used, turn(total, -LOCAL * k), 1.0) for k in range(6)]
        inv = 1.0 / m[0]
        m = [value * inv for value in m]
        d0, d1, d2 = (1.0 / jnp.sqrt(m[k]) for k in (1, 3, 5))
        g0, g1, g2 = d0, m[1] * d1, m[2] * d2
        l10 = m[2] * d0 * d1
        l20 = m[3] * d0 * d2
        k21 = m[4] * d1 * d2
        p1 = 1.0 - l10 * l10
        e = k21 - l20 * l10
        l21 = e / p1
        p2 = 1.0 - l20 * l20 - l21 * e
        y1 = g1 - l10 * g0
        y2 = g2 - l20 * g0 - l21 * y1
        z2 = y2 / p2
        z1 = y1 / p1 - l21 * z2
        z0 = g0 - l10 * z1 - l20 * z2
        lane = lane_ids((8, LANES))
        for k, value in enumerate((z0 * d0, z1 * d1, z2 * d2)):
            wide = [jnp.broadcast_to(value[:, j : j + 1], (8, LANES)) for j in range(LOCAL)]
            for tile in range(tiles):
                low = tile * LANES // (COLUMNS * Q)
                high = (tile * LANES + LANES - 1) // (COLUMNS * Q)
                chosen = wide[low]
                if high > low:
                    chosen = jnp.where(lane >= COLUMNS * Q * high - LANES * tile, wide[high], chosen)
                coef[k, tile] = chosen

    for tile in range(tiles):
        lanes = slice(tile * LANES, (tile + 1) * LANES)
        c0, c1, c2 = (
            jnp.broadcast_to(coef[k, tile, pl.ds(comp, 1), :], (2, LANES)) for k in range(3)
        )
        for qy in range(Q):
            out_ref[0, qy, :, lanes] = (
                c0 * u0_ref[0, qy, :, lanes]
                + c1 * u1_ref[0, qy, :, lanes]
                + c2 * u2_ref[0, qy, :, lanes]
            )


def finish(moments, u0, u1, u2):
    target = pl.BlockSpec((1, Q, 2, COLUMNS * Q * LOCAL), lambda i: (i, 0, 0, 0))
    out = pl.pallas_call(
        finish_body,
        grid=(3,),
        in_specs=[pl.BlockSpec(moments.shape, lambda i: (0, 0, 0)), target, target, target],
        out_specs=target,
        out_shape=jax.ShapeDtypeStruct((3, Q, 2, COLUMNS * Q * LOCAL), F32),
        scratch_shapes=[pltpu.VMEM((3, COLUMNS * Q * LOCAL // LANES, 8, LANES), F32)],
        compiler_params=pltpu.CompilerParams(vmem_limit_bytes=24 * 2**20),
        name="finish",
    )(moments, in_hbm(u0), in_hbm(u1), in_hbm(u2))
    return jnp.transpose(out, (0, 2, 1, 3))


def make_tables():
    derivative, weights = gll_tables(Q)
    basis, basis_slope, span_slope = fourier_table(PLANES)
    table = np.concatenate([basis.T, basis_slope.T], axis=1)
    table = table.astype(np.float32)
    eye = np.eye(Q)
    nodes = np.zeros((2, LANES, LANES))
    nodes[0, :NODES, :NODES] = np.kron(eye, derivative.T)
    nodes[1, :NODES, :NODES] = np.kron(derivative.T, eye)
    order = np.zeros((176, LANES))
    for qx in range(Q):
        for qy in range(Q):
            order[qx * 16 + qy, qy * Q + qx] = 1.0
    stack = np.concatenate([order, order @ nodes[0], order @ nodes[1]], axis=1)
    stack = np.concatenate(halves(stack), axis=0)
    plane = np.concatenate([nodes[0], nodes[1]], axis=1)
    mass = np.zeros((1, LANES), np.float32)
    mass[0, :NODES] = np.kron(weights, weights)
    stiff = (derivative.T * weights) @ derivative
    kb = np.zeros((2 * LANES, 2 * LANES))
    join = np.eye(2 * LANES)
    wx = np.zeros((1, 2 * LANES), np.float32)
    ends = []
    for t in range(2):
        for place in range(Q):
            low = t * LANES + place * Q
            kb[low : low + Q, low : low + Q] = stiff
            wx[0, low : low + Q] = weights
            ends.append(low)
    for left, right in zip(ends[:-1], ends[1:]):
        join[left + Q - 1, right] = 1.0
        join[right, left + Q - 1] = 1.0
    return dict(
        table=table, stack=stack, dz=halves(span_slope), plane=halves(plane), mass=mass,
        kb=kb.astype(np.float32), near=(kb @ join - kb).astype(np.float32), wx=wx,
        stiff=stiff.tolist(), weights=weights.tolist(),
    )


def local(adjoint_velocity, base_flow, column_widths, row_heights, base_phase):
    tables = make_tables()
    elem_count = lax.axis_size("elem")
    ints = jnp.stack([lax.axis_index("four").astype(jnp.int32), base_phase[0]])
    send = pack(adjoint_velocity)
    arrived = lax.all_to_all(send, "four", split_axis=0, concat_axis=0, tiled=True)
    fields, *turned = base_stage(
        ints, column_widths, row_heights, base_flow, jnp.asarray(tables["table"]),
        jnp.asarray(tables["stack"]), *(jnp.asarray(a) for a in tables["dz"]),
    )
    source = lines_stage(
        ints, column_widths, row_heights, arrived, fields, turned,
        *(jnp.asarray(a) for a in tables["plane"]), jnp.asarray(tables["mass"]),
    )
    own = lax.all_to_all(source, "four", split_axis=0, concat_axis=0, tiled=True)
    up = [(i, i + 1) for i in range(elem_count - 1)]
    left = lax.ppermute(own[COLUMNS - GHOST :], "elem", up)
    right = lax.ppermute(own[:GHOST], "elem", [(j, i) for i, j in up])
    v0, v1, v2, moments = krylov_stage(
        tables["stiff"], tables["weights"], ints, row_heights, own, left, right,
        jnp.asarray(tables["kb"]), jnp.asarray(tables["near"]), jnp.asarray(tables["wx"]), elem_count,
    )
    moments = lax.all_to_all(moments, "elem", split_axis=0, concat_axis=0, tiled=True)
    return finish(moments, *unpack(v0, v1, v2))


def solution(mesh):
    split_spec = P(None, None, None, ("elem", "four"))
    return jax.shard_map(
        local,
        mesh=mesh,
        in_specs=(split_spec, split_spec, P("elem"), P(), P()),
        out_specs=split_spec,
        check_vma=False,
    )
```

```python
import jax
import jax.numpy as jnp
import numpy as np
from jax import lax
from jax.experimental import pallas as pl
from jax.experimental.pallas import tpu as pltpu
from jax.sharding import PartitionSpec as P

Q = 11
PLANES = 256
PEERS = 16
LOCAL = 16
COLUMNS = 16
GHOST = 3
ROWS = 21
NODES = Q * Q
LANES = 128
PITCH = 17
FACE = ROWS * Q
TILES = 11
NU = 0.005
DT = 0.01
SIGMA = 1.0 / (NU * DT)
HIGHEST = lax.Precision.HIGHEST
F32 = jnp.float32
BF16 = jnp.bfloat16


def legendre_values(points, node_count):
    table_rows = np.zeros((points.shape[0], node_count))
    table_rows[:, 0] = 1.0
    table_rows[:, 1] = points
    for degree_now in range(2, node_count):
        table_rows[:, degree_now] = (
            (2 * degree_now - 1) * points * table_rows[:, degree_now - 1]
            - (degree_now - 1) * table_rows[:, degree_now - 2]
        ) / degree_now
    return table_rows


def gll_tables(node_count):
    degree = node_count - 1
    points = np.cos(np.pi * np.arange(node_count) / degree)
    for newton_step in range(60):
        legendre = legendre_values(points, node_count)
        points = points - (points * legendre[:, degree] - legendre[:, degree - 1]) / (
            node_count * legendre[:, degree]
        )
    legendre = legendre_values(points, node_count)
    weights = 2.0 / (degree * node_count * legendre[:, degree] ** 2)
    points = points[::-1]
    weights = weights[::-1]
    end_values = legendre[::-1, degree]
    derivative = np.zeros((node_count, node_count))
    for row_index in range(node_count):
        for column in range(node_count):
            if row_index != column:
                derivative[row_index, column] = end_values[row_index] / (
                    end_values[column] * (points[row_index] - points[column])
                )
    derivative[0, 0] = -degree * node_count / 4.0
    derivative[degree, degree] = degree * node_count / 4.0
    return derivative, weights


def fourier_table(plane_count):
    positions = np.arange(plane_count)
    basis_rows = np.zeros((plane_count, plane_count))
    basis_rows[0] = 1.0 / np.sqrt(plane_count)
    basis_rows[1] = np.cos(np.pi * positions) / np.sqrt(plane_count)
    for wave_index in range(1, plane_count // 2):
        angle = 2.0 * np.pi * wave_index * positions / plane_count
        basis_rows[2 * wave_index] = np.sqrt(2.0 / plane_count) * np.cos(angle)
        basis_rows[2 * wave_index + 1] = np.sqrt(2.0 / plane_count) * np.sin(angle)
    wave_counts = np.arange(plane_count) // 2
    wave_counts[1] = plane_count // 2
    wave_counts[0] = 0
    wavenumbers = 2.0 * np.pi * wave_counts / (plane_count / 64.0)
    rotate = np.zeros((plane_count, plane_count))
    for wave_index in range(1, plane_count // 2):
        rotate[2 * wave_index, 2 * wave_index + 1] = wavenumbers[2 * wave_index]
        rotate[2 * wave_index + 1, 2 * wave_index] = -wavenumbers[2 * wave_index]
    return basis_rows, rotate.T @ basis_rows, basis_rows.T @ rotate @ basis_rows


def halves(array):
    high = np.asarray(array, np.float32).astype(jnp.bfloat16)
    low = (np.asarray(array, np.float64) - high.astype(np.float64)).astype(jnp.bfloat16)
    return high, low


def split(value):
    high = value.astype(BF16)
    return high, (value - high.astype(F32)).astype(BF16)


def dot(left, right):
    return jnp.dot(left, right, preferred_element_type=F32)


def dot3(left_high, left_low, high, low):
    half = left_high.shape[0] // 2
    parts = [slice(0, half), slice(half, None)]
    totals = [dot(left_high[p], low) for p in parts]
    totals = [t + dot(left_low[p], high) for t, p in zip(totals, parts)]
    return [t + dot(left_high[p], high) for t, p in zip(totals, parts)]


def dot_full(left, right):
    return jnp.dot(left, right, precision=HIGHEST, preferred_element_type=F32)


def in_hbm(array):
    return pltpu.with_memory_space_constraint(array, pltpu.HBM)


def lane_ids(shape):
    return lax.broadcasted_iota(jnp.int32, shape, len(shape) - 1)


def turn(value, shift):
    shift = shift % LANES
    return value if shift == 0 else pltpu.roll(value, shift, value.ndim - 1)


def block_transpose(arrays, places, offset=0):
    lane = lane_ids(arrays[0].shape)
    turned = [turn(array, Q * k - offset) for k, array in enumerate(arrays)]
    results = []
    for place in places:
        distance = (lane - Q * place) & (LANES - 1)
        chosen = turned[0]
        for k in range(1, len(turned)):
            chosen = jnp.where(distance >= Q * k, turned[k], chosen)
        chosen = jnp.where(distance < NODES, chosen, 0.0)
        results.append(turn(chosen, -Q * place))
    return results


def pack_body(in_ref, out_ref, flat, scr0, scr1):
    lane = lane_ids((16, LANES))
    scratches = (scr0, scr1)
    tiles = COLUMNS * Q * LOCAL // LANES
    for qy in range(Q):
        for tile in range(tiles):
            flat[tile, pl.ds(qy, 2, stride=16), :] = in_ref[0, qy, :, tile * LANES : (tile + 1) * LANES]
    for ey in range(2):
        rows = slice(ey * 16, ey * 16 + 16)
        for j in range(LOCAL):
            for t in range(2):
                offset = j * COLUMNS * Q + NODES * t
                tile, shift = offset // LANES, offset % LANES
                first = flat[tile, rows, :]
                if shift and tile + 1 < tiles:
                    first = jnp.where(lane >= shift, first, flat[tile + 1, rows, :])
                scratches[t][ey, j * PITCH : j * PITCH + 16, :] = turn(first, -shift)
    for ey in range(2):
        for t in range(2):
            rows = [scratches[t][ey, pl.ds(qy, LOCAL, stride=PITCH), :] for qy in range(Q)]
            for place, value in enumerate(block_transpose(rows, range(Q if t == 0 else COLUMNS - Q))):
                out_ref[Q * t + place, 0, ey] = value


def pack(adjoint):
    return pl.pallas_call(
        pack_body,
        grid=(3,),
        in_specs=[pl.BlockSpec((1, Q, 2, COLUMNS * Q * LOCAL), lambda i: (i, 0, 0, 0))],
        out_specs=pl.BlockSpec((PEERS, 1, 2, LOCAL, LANES), lambda i: (0, i, 0, 0, 0)),
        out_shape=jax.ShapeDtypeStruct((PEERS, 3, 2, LOCAL, LANES), F32),
        scratch_shapes=[
            pltpu.VMEM((COLUMNS * Q * LOCAL // LANES, 32, LANES), F32),
            pltpu.VMEM((2, LOCAL * PITCH, LANES), F32),
            pltpu.VMEM((2, LOCAL * PITCH, LANES), F32),
        ],
        compiler_params=pltpu.CompilerParams(vmem_limit_bytes=24 * 2**20),
        name="pack",
    )(in_hbm(jnp.transpose(adjoint, (0, 2, 1, 3))))


def base_body(ints, widths, heights, base_ref, table_ref, stack_ref, dzh_ref, dzl_ref,
              field_ref, fgh_ref, fgl_ref, fh_ref, fl_ref, scr):
    step = pl.program_id(0)

    @pl.when(step == 0)
    def _():
        scr[...] = jnp.zeros_like(scr)
        rows = pltpu.roll(table_ref[...], (PLANES - ints[1]) % PLANES, 0)
        for k in range(2):
            high, low = split(rows[:, k * PLANES : (k + 1) * PLANES])
            fgh_ref[k * PLANES : (k + 1) * PLANES, :] = high
            fgl_ref[k * PLANES : (k + 1) * PLANES, :] = low
        high, low = split(jnp.transpose(rows[:, :PLANES]))
        fh_ref[...] = high
        fl_ref[...] = low

    for qx in range(Q):
        part = base_ref[0, 0, :, qx * PLANES : (qx + 1) * PLANES]
        scr[qx * 16 : qx * 16 + Q, :] = part
        scr[176 + qx * 16 : 176 + qx * 16 + Q, :] = part
    mixed = lax.dot_general(
        scr[...], stack_ref[...], (((0,), (0,)), ((), ())), preferred_element_type=F32
    )
    plain = mixed[:, :LANES]
    field_ref[0, 0, 0] = plain
    field_ref[1, 0, 0] = mixed[:, LANES : 2 * LANES] * (2.0 / widths[ints[0]])
    field_ref[2, 0, 0] = mixed[:, 2 * LANES :] * (2.0 / heights[step % 2])
    exact = plain.astype(BF16)
    field_ref[3, 0, 0] = dot(dzh_ref[...], exact) + dot(dzl_ref[...], exact)


def base_stage(ints, widths, heights, base, table, stack, dz_high, dz_low):
    smem = pl.BlockSpec(memory_space=pltpu.SMEM)

    def whole(shape):
        return pl.BlockSpec(shape, lambda i: (0,) * len(shape))

    return pl.pallas_call(
        base_body,
        grid=(6,),
        in_specs=[
            smem, smem, smem,
            pl.BlockSpec((1, 1, Q, Q * PLANES), lambda i: (i // 2, i % 2, 0, 0)),
            whole(table.shape), whole(stack.shape), whole(dz_high.shape), whole(dz_low.shape),
        ],
        out_specs=[
            pl.BlockSpec((4, 1, 1, PLANES, LANES), lambda i: (0, i // 2, i % 2, 0, 0)),
            whole((2 * PLANES, PLANES)), whole((2 * PLANES, PLANES)),
            whole((PLANES, PLANES)), whole((PLANES, PLANES)),
        ],
        out_shape=[
            jax.ShapeDtypeStruct((4, 3, 2, PLANES, LANES), F32),
            jax.ShapeDtypeStruct((2 * PLANES, PLANES), BF16),
            jax.ShapeDtypeStruct((2 * PLANES, PLANES), BF16),
            jax.ShapeDtypeStruct((PLANES, PLANES), BF16),
            jax.ShapeDtypeStruct((PLANES, PLANES), BF16),
        ],
        scratch_shapes=[pltpu.VMEM((352, PLANES), BF16)],
        name="base_stage",
    )(ints, widths, heights, base, table, stack, dz_high, dz_low)


def lines_body(ints, widths, heights, in_ref, field_hbm, fgh_ref, fgl_ref, fh_ref, fl_ref,
               dh_ref, dl_ref, mass_ref, out_ref, fields, lines, slopes, packed, sems):
    copies = [
        pltpu.make_async_copy(field_hbm.at[k], fields.at[k], sems.at[k]) for k in range(4)
    ]
    for copy in copies:
        copy.start()
    width = widths[ints[0]]
    pairs = [((2 * p) // 2, (2 * p) % 2, (2 * p + 1) % 2) for p in range(3)]
    double_dh = jnp.concatenate([dh_ref[...], dh_ref[...]], axis=0)

    def coeffs(c, ey):
        return in_ref[:, c, ey].reshape(PLANES, LANES)

    for c, _, _ in pairs:
        high, low = split(jnp.concatenate([coeffs(c, 0), coeffs(c, 1)], axis=1))
        both = dot3(fgh_ref[...], fgl_ref[...], high, low)
        for ey in range(2):
            line = both[0][:, ey * LANES : (ey + 1) * LANES]
            lines[c, ey] = line
            slopes[2, c, ey] = both[1][:, ey * LANES : (ey + 1) * LANES]
            high_line, low_line = split(line)
            wide = jnp.concatenate([high_line, low_line], axis=1)
            parts = [slice(0, LANES), slice(LANES, PLANES)]
            planes = [dot(wide[p], double_dh) for p in parts]
            planes = [v + dot(high_line[p], dl_ref[...]) for v, p in zip(planes, parts)]
            for plane, p in zip(planes, parts):
                slopes[0, c, ey, p] = plane[:, :LANES] * (2.0 / width)
                slopes[1, c, ey, p] = plane[:, LANES:] * (2.0 / heights[ey])
    for copy in copies:
        copy.wait()
    lane = lane_ids((PLANES, LANES))
    for c in range(3):
        pieces = []
        for ey in range(2):
            total = fields[0, 0, ey] * slopes[0, c, ey]
            for d in range(1, 3):
                total = total + fields[0, d, ey] * slopes[d, c, ey]
            for d in range(3):
                total = total - lines[d, ey] * fields[1 + c, d, ey]
            pieces.append(total)
        high, low = split(jnp.concatenate(pieces, axis=1))
        hat = jnp.concatenate(dot3(fh_ref[...], fl_ref[...], high, low), axis=0)
        values = []
        for ey in range(2):
            mass = mass_ref[...] * (width * heights[ey] * 0.25)
            source = SIGMA * coeffs(c, ey) + hat[:, ey * LANES : (ey + 1) * LANES] * (1.0 / NU)
            values.append(mass * source)
        values[0] = values[0] + jnp.where(lane >= NODES - Q, turn(values[1], NODES - Q), 0.0)
        for ey in range(2):
            packed[c, ey] = values[ey]
    lane = lane_ids((PEERS, 8, LANES))
    pieces = []
    for half in range(2):
        for c in range(3):
            base = (half * 3 + c) * FACE
            for ey in range(2):
                value = packed[c, ey].reshape(PEERS, 2, 8, LANES)[:, half]
                pieces.append((base + NODES * ey, turn(value, base + (NODES - Q) * ey)))
    pieces.append((6 * FACE, jnp.full((PEERS, 8, LANES), width, F32)))
    starts = [start for start, _ in pieces] + [TILES * LANES]
    for tile in range(TILES):
        low, high = tile * LANES, (tile + 1) * LANES
        chosen = None
        for k, (start, value) in enumerate(pieces):
            if start < high and starts[k + 1] > low:
                chosen = value if chosen is None else jnp.where(lane >= start - low, value, chosen)
        out_ref[:, tile] = chosen


def lines_stage(ints, widths, heights, arrived, fields, tables, d_high, d_low, mass):
    smem = pl.BlockSpec(memory_space=pltpu.SMEM)

    def whole(array):
        return pl.BlockSpec(array.shape, lambda i: (0,) * array.ndim)

    return pl.pallas_call(
        lines_body,
        grid=(1,),
        in_specs=[smem, smem, smem, whole(arrived), pl.BlockSpec(memory_space=pl.ANY)]
        + [whole(a) for a in tables] + [whole(d_high), whole(d_low), whole(mass)],
        out_specs=pl.BlockSpec((PEERS, TILES, 8, LANES), lambda i: (0, 0, 0, 0)),
        out_shape=jax.ShapeDtypeStruct((PEERS, TILES, 8, LANES), F32),
        scratch_shapes=[
            pltpu.VMEM((4, 3, 2, PLANES, LANES), F32),
            pltpu.VMEM((3, 2, PLANES, LANES), F32),
            pltpu.VMEM((3, 3, 2, PLANES, LANES), F32),
            pltpu.VMEM((3, 2, PLANES, LANES), F32),
            pltpu.SemaphoreType.DMA((4,)),
        ],
        compiler_params=pltpu.CompilerParams(vmem_limit_bytes=24 * 2**20),
        name="lines_stage",
    )(*map(in_hbm, (ints, widths, heights)), arrived, in_hbm(fields), *map(in_hbm, tables), d_high, d_low, mass)


def join_columns(chunks, offset):
    lane = (lane_ids(chunks[0].shape) - offset) & (LANES - 1)
    place = lane - Q * ((lane * 5958) >> 16)
    at_first = (place == 0) & (lane < NODES)
    at_last = (place == Q - 1) & (lane < NODES)
    results = []
    for k, chunk in enumerate(chunks):
        extra = 0.0
        if k > 0:
            extra = jnp.where(at_first, turn(chunks[k - 1], -(Q - 1)), extra)
        if k + 1 < len(chunks):
            extra = jnp.where(at_last, turn(chunks[k + 1], Q - 1), extra)
        results.append(chunk + extra)
    return results


def split3(value):
    high = value.astype(BF16)
    rest = value - high.astype(F32)
    mid = rest.astype(BF16)
    return high, mid, (rest - mid.astype(F32)).astype(BF16)


def dot_split(source, target, operator):
    cut = 176
    parts = [slice(0, cut), slice(cut, ROWS * LOCAL)]
    pieces = [split3(source[p, :]) for p in parts]
    totals = [None, None]
    for left, right in ((2, 0), (0, 2), (1, 1), (1, 0), (0, 1), (0, 0)):
        for k in range(2):
            value = dot(pieces[k][left], operator[right])
            totals[k] = value if totals[k] is None else totals[k] + value
    for k in range(2):
        target[parts[k], :] = totals[k]


def stiff_rows(stiff, values):
    middle = Q // 2
    even = [values[m] + values[Q - 1 - m] for m in range(middle)] + [values[middle]]
    odd = [values[m] - values[Q - 1 - m] for m in range(middle)]
    results = [None] * Q
    for row in range(middle + 1):
        total = None
        for m in range(middle + 1):
            factor = stiff[row][m] if m == middle or row == middle else (
                0.5 * (stiff[row][m] + stiff[row][Q - 1 - m])
            )
            term = factor * even[m]
            total = term if total is None else total + term
        if row == middle:
            results[row] = total
            continue
        other = None
        for m in range(middle):
            term = (0.5 * (stiff[row][m] - stiff[row][Q - 1 - m])) * odd[m]
            other = term if other is None else other + term
        results[row] = total + other
        results[Q - 1 - row] = total - other
    return results


def krylov_body(stiff_y, weights, ints, heights, own_ref, left_ref, right_ref, kb_ref, kn_ref, wx_ref,
                v0_ref, v1_ref, v2_ref, mom_ref, kxs, kbs, vec, prod, tmp):
    column_refs = (
        [left_ref.at[k] for k in range(GHOST)]
        + [own_ref.at[k] for k in range(COLUMNS)]
        + [right_ref.at[k] for k in range(GHOST)]
    )

    lane = lane_ids((8, LANES))
    widths = [ref[TILES - 1, :, LANES - 1 :] for ref in column_refs]
    zero = jnp.zeros((8, 1), F32)
    widths = [zero] + widths + [zero]
    for t in range(2):
        here = jnp.zeros((8, LANES), F32)
        near = here
        for place in range(Q):
            k = Q * t + place + 1
            low, high = Q * place, Q * place + Q - 1
            here = jnp.where((lane >= low) & (lane <= high), widths[k], here)
            near = jnp.where(lane == low, widths[k - 1], near)
            near = jnp.where(lane == high, widths[k + 1], near)
        vec[0, :, t * LANES : (t + 1) * LANES] = here
        vec[1, :, t * LANES : (t + 1) * LANES] = near
    here, near = vec[0], vec[1]
    line = lane_ids((8, 2 * LANES))
    own = ((line >= GHOST * Q) & (line < NODES)) | (
        (line >= LANES) & (line < LANES + (Q - GHOST) * Q)
    )
    own = own.astype(F32)
    mass_x = here * wx_ref[...]
    vec[2] = mass_x * own
    vec[1] = mass_x + near * wx_ref[...]
    vec[3] = own * jnp.where(near > 0.0, 0.5, 1.0)
    inverse, inverse_near = (
        jnp.where(value > 0.0, 1.0 / jnp.where(value > 0.0, value, 1.0), 0.0)[0:1]
        for value in (here, near)
    )
    scaled = kb_ref[...] * inverse
    for k, part in enumerate(split3(scaled + kn_ref[...] * inverse_near)):
        kxs[k] = part
    for k, part in enumerate(split3(scaled * own[0:1])):
        kbs[k] = part

    h0, h1 = heights[0], heights[1]
    inverse_y = (1.0 / h0, 1.0 / h1)
    mass_y = []
    for y in range(ROWS):
        if y < Q - 1:
            mass_y.append(h0 * weights[y])
        elif y == Q - 1:
            mass_y.append((h0 + h1) * weights[0])
        else:
            mass_y.append(h1 * weights[y - Q + 1])

    def apply(source, target, operator, mass_row, low_key):
        dot_split(source, tmp, operator)
        sums = [[], []]
        for half in range(2):
            plane = ints[0] * LOCAL + half * 8 + lax.broadcasted_iota(jnp.int32, (8, LANES), 0)
            kappa = jnp.where(plane == 1, PLANES // 2, plane >> 1).astype(F32)
            beta = kappa * (2.0 * np.pi / (PLANES / 64.0))
            lam = (beta * beta + SIGMA) * 0.25
            square = cross = None
            for t in range(2):
                lanes = slice(t * LANES, (t + 1) * LANES)
                mass_x = vec[mass_row, :, lanes]
                shift = lam * mass_x
                weight = vec[3, :, lanes]
                here_square = here_cross = None
                shared = None
                for ey in range(2):
                    rows = [
                        slice(y * LOCAL + half * 8, y * LOCAL + half * 8 + 8)
                        for y in range((Q - 1) * ey, (Q - 1) * ey + Q)
                    ]
                    values = [source[r, lanes] for r in rows]
                    scale = mass_x * inverse_y[ey]
                    stiff = [scale * value for value in stiff_rows(stiff_y, values)]
                    if ey == 0:
                        shared = stiff.pop()
                    else:
                        stiff[0] = stiff[0] + shared
                    for k, part in enumerate(stiff):
                        y, value = (Q - 1) * ey + k, values[k]
                        image = mass_y[y] * (tmp[rows[k], lanes] + shift * value) + part
                        if target is not None:
                            target[rows[k], lanes] = image
                        one, two = value * value, value * image
                        here_square = one if here_square is None else here_square + one
                        here_cross = two if here_cross is None else here_cross + two
                here_square = here_square * weight
                if target is not None:
                    here_cross = here_cross * weight
                square = here_square if square is None else square + here_square
                cross = here_cross if cross is None else cross + here_cross
            prod[low_key * LOCAL + half * 8 : low_key * LOCAL + half * 8 + 8, :] = square
            prod[(low_key + 1) * LOCAL + half * 8 : (low_key + 1) * LOCAL + half * 8 + 8, :] = cross

    lane = lane_ids((8, LANES))
    for comp in range(3):
        first, second, third = v0_ref.at[comp], v1_ref.at[comp], v2_ref.at[comp]
        for half in range(2):
            for ey in range(2):
                start = (half * 3 + comp) * FACE + (NODES - Q) * ey
                tile, offset = start // LANES, start % LANES
                chunks = [ref[tile] for ref in column_refs]
                if offset:
                    chunks = [
                        jnp.where(lane >= offset, chunk, ref[tile + 1])
                        for chunk, ref in zip(chunks, column_refs)
                    ]
                chunks = join_columns(chunks, offset)
                places = range(ey, Q)
                for t in range(2):
                    for qy, value in zip(
                        places, block_transpose(chunks[Q * t : Q * t + Q], places, offset)
                    ):
                        row = (qy + (Q - 1) * ey) * LOCAL + half * 8
                        first[row : row + 8, t * LANES : (t + 1) * LANES] = value
        prod[6 * LOCAL :, :] = jnp.zeros((LANES - 6 * LOCAL, LANES), F32)
        apply(first, second, kxs, 1, 0)
        apply(second, third, kxs, 1, 2)
        apply(third, None, kbs, 2, 4)
        row = lax.dot_general(
            jnp.ones((8, LANES), F32), prod[...], (((1,), (1,)), ((), ())),
            precision=HIGHEST, preferred_element_type=F32,
        )
        mom_ref[:, comp : comp + 1, :] = jnp.broadcast_to(
            row[0:1][None], (mom_ref.shape[0], 1, LANES)
        )


def krylov_stage(stiff_y, weights, ints, heights, own, left, right, kb, near, wx, peers):
    smem = pl.BlockSpec(memory_space=pltpu.SMEM)

    def whole(array):
        return pl.BlockSpec(array.shape, lambda i: (0,) * array.ndim)

    def chunk(count):
        return pl.BlockSpec((count, TILES, 8, LANES), lambda i: (0, 0, 0, 0))

    vector = pl.BlockSpec((3, ROWS * LOCAL, 2 * LANES), lambda i: (0, 0, 0))
    shape = jax.ShapeDtypeStruct((3, ROWS * LOCAL, 2 * LANES), F32)

    def body(*refs):
        krylov_body(stiff_y, weights, *refs)

    return pl.pallas_call(
        body,
        grid=(1,),
        in_specs=[smem, smem, chunk(COLUMNS), chunk(GHOST), chunk(GHOST), whole(kb), whole(near), whole(wx)],
        out_specs=[vector, vector, vector, pl.BlockSpec((peers, 8, LANES), lambda i: (0, 0, 0))],
        out_shape=[shape, shape, shape, jax.ShapeDtypeStruct((peers, 8, LANES), F32)],
        scratch_shapes=[
            pltpu.VMEM((3, 2 * LANES, 2 * LANES), BF16),
            pltpu.VMEM((3, 2 * LANES, 2 * LANES), BF16),
            pltpu.VMEM((4, 8, 2 * LANES), F32),
            pltpu.VMEM((LANES, LANES), F32),
            pltpu.VMEM((ROWS * LOCAL, 2 * LANES), F32),
        ],
        compiler_params=pltpu.CompilerParams(vmem_limit_bytes=24 * 2**20),
        name="krylov_stage",
    )(in_hbm(ints), in_hbm(heights), own, left, right, kb, near, wx)


def unpack_body(v0_ref, v1_ref, v2_ref, out_ref, scr, flat):
    lane = lane_ids((16, LANES))
    run = COLUMNS * Q // 2
    for k, vector in enumerate((v0_ref, v1_ref, v2_ref)):
        for y in range(ROWS):
            rows = slice(y * LOCAL, (y + 1) * LOCAL)
            for t in range(2):
                value = vector[0, rows, t * LANES : (t + 1) * LANES]
                if y <= Q - 1:
                    scr[0, t, pl.ds(y, LOCAL, stride=PITCH), :] = value
                if y >= Q - 1:
                    scr[1, t, pl.ds(y - Q + 1, LOCAL, stride=PITCH), :] = value
        for ey in range(2):
            turned = []
            for r in range(2 * LOCAL):
                start = GHOST * Q if r % 2 == 0 else 0
                value = scr[ey, r % 2, (r // 2) * PITCH : (r // 2) * PITCH + 16, :]
                turned.append(turn(value, run * r - start))
            for tile in range(COLUMNS * Q * LOCAL // LANES):
                low, high = tile * LANES // run, (tile * LANES + LANES - 1) // run
                value = turned[low]
                for r in range(low + 1, high + 1):
                    value = jnp.where(lane >= run * r - LANES * tile, turned[r], value)
                flat[tile, ey * 16 : ey * 16 + 16, :] = value
        for qy in range(Q):
            for tile in range(COLUMNS * Q * LOCAL // LANES):
                out_ref[0, k, qy, :, tile * LANES : (tile + 1) * LANES] = flat[
                    tile, pl.ds(qy, 2, stride=16), :
                ]


def unpack(v0, v1, v2):
    vector = pl.BlockSpec((1, ROWS * LOCAL, 2 * LANES), lambda i: (i, 0, 0))
    target = pl.BlockSpec((1, 3, Q, 2, COLUMNS * Q * LOCAL), lambda i: (i, 0, 0, 0, 0))
    shape = pltpu.HBM((3, 3, Q, 2, COLUMNS * Q * LOCAL), F32)
    return pl.pallas_call(
        unpack_body,
        grid=(3,),
        in_specs=[vector] * 3,
        out_specs=target,
        out_shape=shape,
        scratch_shapes=[
            pltpu.VMEM((2, 2, LOCAL * PITCH, LANES), F32),
            pltpu.VMEM((COLUMNS * Q * LOCAL // LANES, 32, LANES), F32),
        ],
        compiler_params=pltpu.CompilerParams(vmem_limit_bytes=24 * 2**20),
        name="unpack",
    )(v0, v1, v2)


def finish_body(mom_ref, u_ref, out_ref, coef):
    comp = pl.program_id(0)
    tiles = COLUMNS * Q * LOCAL // LANES

    @pl.when(comp == 0)
    def _():
        total = jnp.sum(mom_ref[...], axis=0)
        used = (lane_ids((8, LANES)) < LOCAL) & (
            lax.broadcasted_iota(jnp.int32, (8, LANES), 0) < 3
        )
        m = [jnp.where(used, turn(total, -LOCAL * k), 1.0) for k in range(6)]
        inv = 1.0 / m[0]
        m = [value * inv for value in m]
        d0, d1, d2 = (1.0 / jnp.sqrt(m[k]) for k in (1, 3, 5))
        g0, g1, g2 = d0, m[1] * d1, m[2] * d2
        l10 = m[2] * d0 * d1
        l20 = m[3] * d0 * d2
        k21 = m[4] * d1 * d2
        p1 = 1.0 - l10 * l10
        e = k21 - l20 * l10
        l21 = e / p1
        p2 = 1.0 - l20 * l20 - l21 * e
        y1 = g1 - l10 * g0
        y2 = g2 - l20 * g0 - l21 * y1
        z2 = y2 / p2
        z1 = y1 / p1 - l21 * z2
        z0 = g0 - l10 * z1 - l20 * z2
        lane = lane_ids((8, LANES))
        for k, value in enumerate((z0 * d0, z1 * d1, z2 * d2)):
            wide = [jnp.broadcast_to(value[:, j : j + 1], (8, LANES)) for j in range(LOCAL)]
            for tile in range(tiles):
                low = tile * LANES // (COLUMNS * Q)
                high = (tile * LANES + LANES - 1) // (COLUMNS * Q)
                chosen = wide[low]
                if high > low:
                    chosen = jnp.where(lane >= COLUMNS * Q * high - LANES * tile, wide[high], chosen)
                coef[k, tile] = chosen

    for tile in range(tiles):
        lanes = slice(tile * LANES, (tile + 1) * LANES)
        c0, c1, c2 = (
            jnp.broadcast_to(coef[k, tile, pl.ds(comp, 1), :], (2, LANES)) for k in range(3)
        )
        for qy in range(Q):
            out_ref[0, qy, :, lanes] = (
                c0 * u_ref[0, 0, qy, :, lanes]
                + c1 * u_ref[0, 1, qy, :, lanes]
                + c2 * u_ref[0, 2, qy, :, lanes]
            )


def finish(moments, vectors):
    target = pl.BlockSpec((1, Q, 2, COLUMNS * Q * LOCAL), lambda i: (i, 0, 0, 0))
    out = pl.pallas_call(
        finish_body,
        grid=(3,),
        in_specs=[
            pl.BlockSpec(moments.shape, lambda i: (0, 0, 0)),
            pl.BlockSpec((1, 3, Q, 2, COLUMNS * Q * LOCAL), lambda i: (i, 0, 0, 0, 0)),
        ],
        out_specs=target,
        out_shape=jax.ShapeDtypeStruct((3, Q, 2, COLUMNS * Q * LOCAL), F32),
        scratch_shapes=[pltpu.VMEM((3, COLUMNS * Q * LOCAL // LANES, 8, LANES), F32)],
        compiler_params=pltpu.CompilerParams(vmem_limit_bytes=24 * 2**20),
        name="finish",
    )(moments, in_hbm(vectors))
    return jnp.transpose(out, (0, 2, 1, 3))


def make_tables():
    derivative, weights = gll_tables(Q)
    basis, basis_slope, span_slope = fourier_table(PLANES)
    table = np.concatenate([basis.T, basis_slope.T], axis=1)
    table = table.astype(np.float32)
    eye = np.eye(Q)
    nodes = np.zeros((2, LANES, LANES))
    nodes[0, :NODES, :NODES] = np.kron(eye, derivative.T)
    nodes[1, :NODES, :NODES] = np.kron(derivative.T, eye)
    order = np.zeros((176, LANES))
    for qx in range(Q):
        for qy in range(Q):
            order[qx * 16 + qy, qy * Q + qx] = 1.0
    stack = np.concatenate([order, order @ nodes[0], order @ nodes[1]], axis=1)
    stack = np.concatenate(halves(stack), axis=0)
    plane = np.concatenate([nodes[0], nodes[1]], axis=1)
    mass = np.zeros((1, LANES), np.float32)
    mass[0, :NODES] = np.kron(weights, weights)
    stiff = (derivative.T * weights) @ derivative
    kb = np.zeros((2 * LANES, 2 * LANES))
    join = np.eye(2 * LANES)
    wx = np.zeros((1, 2 * LANES), np.float32)
    ends = []
    for t in range(2):
        for place in range(Q):
            low = t * LANES + place * Q
            kb[low : low + Q, low : low + Q] = stiff
            wx[0, low : low + Q] = weights
            ends.append(low)
    for left, right in zip(ends[:-1], ends[1:]):
        join[left + Q - 1, right] = 1.0
        join[right, left + Q - 1] = 1.0
    return dict(
        table=table, stack=stack, dz=halves(span_slope), plane=halves(plane), mass=mass,
        kb=kb.astype(np.float32), near=(kb @ join - kb).astype(np.float32), wx=wx,
        stiff=stiff.tolist(), weights=weights.tolist(),
    )


def local(adjoint_velocity, base_flow, column_widths, row_heights, base_phase):
    tables = make_tables()
    elem_count = lax.axis_size("elem")
    ints = jnp.stack([lax.axis_index("four").astype(jnp.int32), base_phase[0]])
    send = pack(adjoint_velocity)
    arrived = lax.all_to_all(send, "four", split_axis=0, concat_axis=0, tiled=True)
    fields, *turned = base_stage(
        ints, column_widths, row_heights, base_flow, jnp.asarray(tables["table"]),
        jnp.asarray(tables["stack"]), *(jnp.asarray(a) for a in tables["dz"]),
    )
    source = lines_stage(
        ints, column_widths, row_heights, arrived, fields, turned,
        *(jnp.asarray(a) for a in tables["plane"]), jnp.asarray(tables["mass"]),
    )
    own = lax.all_to_all(source, "four", split_axis=0, concat_axis=0, tiled=True)
    up = [(i, i + 1) for i in range(elem_count - 1)]
    left = lax.ppermute(own[COLUMNS - GHOST :], "elem", up)
    right = lax.ppermute(own[:GHOST], "elem", [(j, i) for i, j in up])
    v0, v1, v2, moments = krylov_stage(
        tables["stiff"], tables["weights"], ints, row_heights, own, left, right,
        jnp.asarray(tables["kb"]), jnp.asarray(tables["near"]), jnp.asarray(tables["wx"]), elem_count,
    )
    moments = lax.all_to_all(moments, "elem", split_axis=0, concat_axis=0, tiled=True)
    return finish(moments, unpack(v0, v1, v2))


def solution(mesh):
    split_spec = P(None, None, None, ("elem", "four"))
    return jax.shard_map(
        local,
        mesh=mesh,
        in_specs=(split_spec, split_spec, P("elem"), P(), P()),
        out_specs=split_spec,
        check_vma=False,
    )
```

```python
import jax
import jax.numpy as jnp
import numpy as np
from jax import lax
from jax.experimental import pallas as pl
from jax.experimental.pallas import tpu as pltpu
from jax.sharding import PartitionSpec as P

Q = 11
PLANES = 256
PEERS = 16
LOCAL = 16
COLUMNS = 16
GHOST = 3
ROWS = 21
NODES = Q * Q
LANES = 128
PITCH = 17
FACE = ROWS * Q
TILES = 11
NU = 0.005
DT = 0.01
SIGMA = 1.0 / (NU * DT)
HIGHEST = lax.Precision.HIGHEST
F32 = jnp.float32
BF16 = jnp.bfloat16


def legendre_values(points, node_count):
    table_rows = np.zeros((points.shape[0], node_count))
    table_rows[:, 0] = 1.0
    table_rows[:, 1] = points
    for degree_now in range(2, node_count):
        table_rows[:, degree_now] = (
            (2 * degree_now - 1) * points * table_rows[:, degree_now - 1]
            - (degree_now - 1) * table_rows[:, degree_now - 2]
        ) / degree_now
    return table_rows


def gll_tables(node_count):
    degree = node_count - 1
    points = np.cos(np.pi * np.arange(node_count) / degree)
    for newton_step in range(60):
        legendre = legendre_values(points, node_count)
        points = points - (points * legendre[:, degree] - legendre[:, degree - 1]) / (
            node_count * legendre[:, degree]
        )
    legendre = legendre_values(points, node_count)
    weights = 2.0 / (degree * node_count * legendre[:, degree] ** 2)
    points = points[::-1]
    weights = weights[::-1]
    end_values = legendre[::-1, degree]
    derivative = np.zeros((node_count, node_count))
    for row_index in range(node_count):
        for column in range(node_count):
            if row_index != column:
                derivative[row_index, column] = end_values[row_index] / (
                    end_values[column] * (points[row_index] - points[column])
                )
    derivative[0, 0] = -degree * node_count / 4.0
    derivative[degree, degree] = degree * node_count / 4.0
    return derivative, weights


def fourier_table(plane_count):
    positions = np.arange(plane_count)
    basis_rows = np.zeros((plane_count, plane_count))
    basis_rows[0] = 1.0 / np.sqrt(plane_count)
    basis_rows[1] = np.cos(np.pi * positions) / np.sqrt(plane_count)
    for wave_index in range(1, plane_count // 2):
        angle = 2.0 * np.pi * wave_index * positions / plane_count
        basis_rows[2 * wave_index] = np.sqrt(2.0 / plane_count) * np.cos(angle)
        basis_rows[2 * wave_index + 1] = np.sqrt(2.0 / plane_count) * np.sin(angle)
    wave_counts = np.arange(plane_count) // 2
    wave_counts[1] = plane_count // 2
    wave_counts[0] = 0
    wavenumbers = 2.0 * np.pi * wave_counts / (plane_count / 64.0)
    rotate = np.zeros((plane_count, plane_count))
    for wave_index in range(1, plane_count // 2):
        rotate[2 * wave_index, 2 * wave_index + 1] = wavenumbers[2 * wave_index]
        rotate[2 * wave_index + 1, 2 * wave_index] = -wavenumbers[2 * wave_index]
    return basis_rows, rotate.T @ basis_rows, basis_rows.T @ rotate @ basis_rows


def halves(array):
    high = np.asarray(array, np.float32).astype(jnp.bfloat16)
    low = (np.asarray(array, np.float64) - high.astype(np.float64)).astype(jnp.bfloat16)
    return high, low


def split(value):
    high = value.astype(BF16)
    return high, (value - high.astype(F32)).astype(BF16)


def dot(left, right):
    return jnp.dot(left, right, preferred_element_type=F32)


def dot3(left_high, left_low, high, low):
    half = left_high.shape[0] // 2
    parts = [slice(0, half), slice(half, None)]
    totals = [dot(left_high[p], low) for p in parts]
    totals = [t + dot(left_low[p], high) for t, p in zip(totals, parts)]
    return [t + dot(left_high[p], high) for t, p in zip(totals, parts)]


def dot_full(left, right):
    return jnp.dot(left, right, precision=HIGHEST, preferred_element_type=F32)


def in_hbm(array):
    return pltpu.with_memory_space_constraint(array, pltpu.HBM)


def to_groups(array):
    array = jnp.transpose(array, (0, 2, 1, 3)).reshape(3, Q, 2, Q, 2, LANES)
    return jnp.transpose(array, (0, 1, 3, 4, 2, 5)).reshape(3, NODES, 4, LANES)


def from_groups(array):
    array = jnp.transpose(array.reshape(3, Q, Q, 2, 2, LANES), (0, 1, 4, 2, 3, 5))
    return jnp.transpose(array.reshape(3, Q, 2, COLUMNS * Q * LOCAL), (0, 2, 1, 3))


def lane_ids(shape):
    return lax.broadcasted_iota(jnp.int32, shape, len(shape) - 1)


def turn(value, shift):
    shift = shift % LANES
    return value if shift == 0 else pltpu.roll(value, shift, value.ndim - 1)


def block_transpose(arrays, places, offset=0, first=0):
    lane = lane_ids(arrays[0].shape)
    turned = [turn(array, Q * (first + k) - offset) for k, array in enumerate(arrays)]
    results = []
    for place in places:
        distance = (lane - Q * place) & (LANES - 1)
        chosen = turned[0]
        for k in range(1, len(turned)):
            chosen = jnp.where(distance >= Q * (first + k), turned[k], chosen)
        inside = distance < Q * (first + len(turned))
        if first:
            inside = inside & (distance >= Q * first)
        chosen = jnp.where(inside, chosen, 0.0)
        results.append(turn(chosen, -Q * place))
    return results


def pack_body(in_ref, out_ref, flat, scr0, scr1):
    lane = lane_ids((16, LANES))
    scratches = (scr0, scr1)
    tiles = COLUMNS * Q * LOCAL // LANES
    for qy in range(Q):
        for pair in range(Q):
            flat[pair, pl.ds(qy, 4, stride=16), :] = in_ref[0, qy * Q + pair]
    for ey in range(2):
        def read(tile):
            low = (tile % 2) * 32 + ey * 16
            return flat[tile // 2, low : low + 16, :]

        for j in range(LOCAL):
            for t in range(2):
                offset = j * COLUMNS * Q + NODES * t
                tile, shift = offset // LANES, offset % LANES
                first = read(tile)
                if shift and tile + 1 < tiles:
                    first = jnp.where(lane >= shift, first, read(tile + 1))
                scratches[t][ey, j * PITCH : j * PITCH + 16, :] = turn(first, -shift)
    for ey in range(2):
        for t in range(2):
            rows = [scratches[t][ey, pl.ds(qy, LOCAL, stride=PITCH), :] for qy in range(Q)]
            for place, value in enumerate(block_transpose(rows, range(Q if t == 0 else COLUMNS - Q))):
                out_ref[Q * t + place, 0, ey] = value


def pack(adjoint):
    return pl.pallas_call(
        pack_body,
        grid=(3,),
        in_specs=[pl.BlockSpec((1, NODES, 4, LANES), lambda i: (i, 0, 0, 0))],
        out_specs=pl.BlockSpec((PEERS, 1, 2, LOCAL, LANES), lambda i: (0, i, 0, 0, 0)),
        out_shape=jax.ShapeDtypeStruct((PEERS, 3, 2, LOCAL, LANES), F32),
        scratch_shapes=[
            pltpu.VMEM((Q, 64, LANES), F32),
            pltpu.VMEM((2, LOCAL * PITCH, LANES), F32),
            pltpu.VMEM((2, LOCAL * PITCH, LANES), F32),
        ],
        compiler_params=pltpu.CompilerParams(vmem_limit_bytes=24 * 2**20),
        name="pack",
    )(in_hbm(to_groups(adjoint)))


def base_body(ints, widths, heights, base_ref, table_ref, stack_ref, dzh_ref, dzl_ref,
              field_ref, fgh_ref, fgl_ref, fh_ref, fl_ref, scr):
    step = pl.program_id(0)

    @pl.when(step == 0)
    def _():
        scr[...] = jnp.zeros_like(scr)
        rows = pltpu.roll(table_ref[...], (PLANES - ints[1]) % PLANES, 0)
        for k in range(2):
            high, low = split(rows[:, k * PLANES : (k + 1) * PLANES])
            fgh_ref[k * PLANES : (k + 1) * PLANES, :] = high
            fgl_ref[k * PLANES : (k + 1) * PLANES, :] = low
        high, low = split(jnp.transpose(rows[:, :PLANES]))
        fh_ref[...] = high
        fl_ref[...] = low

    for qx in range(Q):
        part = base_ref[0, 0, :, qx * PLANES : (qx + 1) * PLANES]
        scr[qx * 16 : qx * 16 + Q, :] = part
        scr[176 + qx * 16 : 176 + qx * 16 + Q, :] = part
    mixed = lax.dot_general(
        scr[...], stack_ref[...], (((0,), (0,)), ((), ())), preferred_element_type=F32
    )
    plain = mixed[:, :LANES]
    field_ref[0, 0, 0] = plain
    field_ref[1, 0, 0] = mixed[:, LANES : 2 * LANES] * (2.0 / widths[ints[0]])
    field_ref[2, 0, 0] = mixed[:, 2 * LANES :] * (2.0 / heights[step % 2])
    exact = plain.astype(BF16)
    field_ref[3, 0, 0] = dot(dzh_ref[...], exact) + dot(dzl_ref[...], exact)


def base_stage(ints, widths, heights, base, table, stack, dz_high, dz_low):
    smem = pl.BlockSpec(memory_space=pltpu.SMEM)

    def whole(shape):
        return pl.BlockSpec(shape, lambda i: (0,) * len(shape))

    return pl.pallas_call(
        base_body,
        grid=(6,),
        in_specs=[
            smem, smem, smem,
            pl.BlockSpec((1, 1, Q, Q * PLANES), lambda i: (i // 2, i % 2, 0, 0)),
            whole(table.shape), whole(stack.shape), whole(dz_high.shape), whole(dz_low.shape),
        ],
        out_specs=[
            pl.BlockSpec((4, 1, 1, PLANES, LANES), lambda i: (0, i // 2, i % 2, 0, 0)),
            whole((2 * PLANES, PLANES)), whole((2 * PLANES, PLANES)),
            whole((PLANES, PLANES)), whole((PLANES, PLANES)),
        ],
        out_shape=[
            jax.ShapeDtypeStruct((4, 3, 2, PLANES, LANES), F32),
            jax.ShapeDtypeStruct((2 * PLANES, PLANES), BF16),
            jax.ShapeDtypeStruct((2 * PLANES, PLANES), BF16),
            jax.ShapeDtypeStruct((PLANES, PLANES), BF16),
            jax.ShapeDtypeStruct((PLANES, PLANES), BF16),
        ],
        scratch_shapes=[pltpu.VMEM((352, PLANES), BF16)],
        name="base_stage",
    )(ints, widths, heights, base, table, stack, dz_high, dz_low)


def lines_body(ints, widths, heights, in_ref, field_hbm, fgh_ref, fgl_ref, fh_ref, fl_ref,
               dh_ref, dl_ref, mass_ref, out_ref, fields, lines, slopes, packed, sems):
    copies = [
        pltpu.make_async_copy(field_hbm.at[k], fields.at[k], sems.at[k]) for k in range(4)
    ]
    for copy in copies:
        copy.start()
    width = widths[ints[0]]
    pairs = [((2 * p) // 2, (2 * p) % 2, (2 * p + 1) % 2) for p in range(3)]
    double_dh = jnp.concatenate([dh_ref[...], dh_ref[...]], axis=0)

    def coeffs(c, ey):
        return in_ref[:, c, ey].reshape(PLANES, LANES)

    for c, _, _ in pairs:
        high, low = split(jnp.concatenate([coeffs(c, 0), coeffs(c, 1)], axis=1))
        both = dot3(fgh_ref[...], fgl_ref[...], high, low)
        for ey in range(2):
            line = both[0][:, ey * LANES : (ey + 1) * LANES]
            lines[c, ey] = line
            slopes[2, c, ey] = both[1][:, ey * LANES : (ey + 1) * LANES]
            high_line, low_line = split(line)
            wide = jnp.concatenate([high_line, low_line], axis=1)
            parts = [slice(0, LANES), slice(LANES, PLANES)]
            planes = [dot(wide[p], double_dh) for p in parts]
            planes = [v + dot(high_line[p], dl_ref[...]) for v, p in zip(planes, parts)]
            for plane, p in zip(planes, parts):
                slopes[0, c, ey, p] = plane[:, :LANES] * (2.0 / width)
                slopes[1, c, ey, p] = plane[:, LANES:] * (2.0 / heights[ey])
    for copy in copies:
        copy.wait()
    lane = lane_ids((PLANES, LANES))
    for c in range(3):
        pieces = []
        for ey in range(2):
            total = fields[0, 0, ey] * slopes[0, c, ey]
            for d in range(1, 3):
                total = total + fields[0, d, ey] * slopes[d, c, ey]
            for d in range(3):
                total = total - lines[d, ey] * fields[1 + c, d, ey]
            pieces.append(total)
        high, low = split(jnp.concatenate(pieces, axis=1))
        hat = jnp.concatenate(dot3(fh_ref[...], fl_ref[...], high, low), axis=0)
        values = []
        for ey in range(2):
            mass = mass_ref[...] * (width * heights[ey] * 0.25)
            source = SIGMA * coeffs(c, ey) + hat[:, ey * LANES : (ey + 1) * LANES] * (1.0 / NU)
            values.append(mass * source)
        values[0] = values[0] + jnp.where(lane >= NODES - Q, turn(values[1], NODES - Q), 0.0)
        for ey in range(2):
            packed[c, ey] = values[ey]
    lane = lane_ids((PEERS, 8, LANES))
    pieces = []
    for half in range(2):
        for c in range(3):
            base = (half * 3 + c) * FACE
            for ey in range(2):
                value = packed[c, ey].reshape(PEERS, 2, 8, LANES)[:, half]
                pieces.append((base + NODES * ey, turn(value, base + (NODES - Q) * ey)))
    pieces.append((6 * FACE, jnp.full((PEERS, 8, LANES), width, F32)))
    starts = [start for start, _ in pieces] + [TILES * LANES]
    for tile in range(TILES):
        low, high = tile * LANES, (tile + 1) * LANES
        chosen = None
        for k, (start, value) in enumerate(pieces):
            if start < high and starts[k + 1] > low:
                chosen = value if chosen is None else jnp.where(lane >= start - low, value, chosen)
        out_ref[:, tile] = chosen


def lines_stage(ints, widths, heights, arrived, fields, tables, d_high, d_low, mass):
    smem = pl.BlockSpec(memory_space=pltpu.SMEM)

    def whole(array):
        return pl.BlockSpec(array.shape, lambda i: (0,) * array.ndim)

    return pl.pallas_call(
        lines_body,
        grid=(1,),
        in_specs=[smem, smem, smem, whole(arrived), pl.BlockSpec(memory_space=pl.ANY)]
        + [whole(a) for a in tables] + [whole(d_high), whole(d_low), whole(mass)],
        out_specs=pl.BlockSpec((PEERS, TILES, 8, LANES), lambda i: (0, 0, 0, 0)),
        out_shape=jax.ShapeDtypeStruct((PEERS, TILES, 8, LANES), F32),
        scratch_shapes=[
            pltpu.VMEM((4, 3, 2, PLANES, LANES), F32),
            pltpu.VMEM((3, 2, PLANES, LANES), F32),
            pltpu.VMEM((3, 3, 2, PLANES, LANES), F32),
            pltpu.VMEM((3, 2, PLANES, LANES), F32),
            pltpu.SemaphoreType.DMA((4,)),
        ],
        compiler_params=pltpu.CompilerParams(vmem_limit_bytes=24 * 2**20),
        name="lines_stage",
    )(*map(in_hbm, (ints, widths, heights)), arrived, in_hbm(fields), *map(in_hbm, tables), d_high, d_low, mass)


def join_columns(chunks, offset, partial=()):
    lane = (lane_ids(chunks[0].shape) - offset) & (LANES - 1)
    place = lane - Q * ((lane * 5958) >> 16)
    at_first = (place == 0) & (lane < NODES)
    at_last = (place == Q - 1) & (lane < NODES)
    results = []
    for k, chunk in enumerate(chunks):
        extra = 0.0
        if k > 0:
            extra = jnp.where(at_first, turn(chunks[k - 1], -(Q - 1)), extra)
        if k + 1 < len(chunks):
            extra = jnp.where(at_last, turn(chunks[k + 1], Q - 1), extra)
        results.append(extra if k in partial else chunk + extra)
    return results


def windows(refs, start):
    tile, offset = start // LANES, start % LANES
    chunks = [ref[tile] for ref in refs]
    if offset:
        lane = lane_ids((8, LANES))
        chunks = [
            jnp.where(lane >= offset, chunk, ref[tile + 1]) for chunk, ref in zip(chunks, refs)
        ]
    return chunks, offset


def face_parts():
    for comp in range(3):
        for half in range(2):
            for ey in range(2):
                start = (half * 3 + comp) * FACE + (NODES - Q) * ey
                yield comp, start, range(ey, Q), (Q - 1) * ey * LOCAL + half * 8


def place_body(own_ref, out_ref):
    refs = [own_ref.at[k] for k in range(COLUMNS)]
    cut = Q - GHOST
    for comp, start, places, base in face_parts():
        chunks, offset = windows(refs, start)
        chunks = join_columns(chunks, offset)
        sides = [
            block_transpose(chunks[:cut], places, offset, GHOST),
            block_transpose(chunks[cut:], places, offset),
        ]
        for t, values in enumerate(sides):
            for qy, value in zip(places, values):
                row = base + qy * LOCAL
                out_ref[comp, row : row + 8, t * LANES : (t + 1) * LANES] = value


def place_stage(own):
    return pl.pallas_call(
        place_body,
        grid=(1,),
        in_specs=[pl.BlockSpec(own.shape, lambda i: (0, 0, 0, 0))],
        out_specs=pl.BlockSpec((3, ROWS * LOCAL, 2 * LANES), lambda i: (0, 0, 0)),
        out_shape=jax.ShapeDtypeStruct((3, ROWS * LOCAL, 2 * LANES), F32),
        compiler_params=pltpu.CompilerParams(vmem_limit_bytes=24 * 2**20),
        name="place_stage",
    )(own)


def split3(value):
    high = value.astype(BF16)
    rest = value - high.astype(F32)
    mid = rest.astype(BF16)
    return high, mid, (rest - mid.astype(F32)).astype(BF16)


def dot_split(source, target, operator):
    cut = 176
    parts = [slice(0, cut), slice(cut, ROWS * LOCAL)]
    pieces = [split3(source[p, :]) for p in parts]
    totals = [None, None]
    for left, right in ((2, 0), (0, 2), (1, 1), (1, 0), (0, 1), (0, 0)):
        for k in range(2):
            value = dot(pieces[k][left], operator[right])
            totals[k] = value if totals[k] is None else totals[k] + value
    for k in range(2):
        target[parts[k], :] = totals[k]


def stiff_rows(stiff, values):
    middle = Q // 2
    even = [values[m] + values[Q - 1 - m] for m in range(middle)] + [values[middle]]
    odd = [values[m] - values[Q - 1 - m] for m in range(middle)]
    results = [None] * Q
    for row in range(middle + 1):
        total = None
        for m in range(middle + 1):
            factor = stiff[row][m] if m == middle or row == middle else (
                0.5 * (stiff[row][m] + stiff[row][Q - 1 - m])
            )
            term = factor * even[m]
            total = term if total is None else total + term
        if row == middle:
            results[row] = total
            continue
        other = None
        for m in range(middle):
            term = (0.5 * (stiff[row][m] - stiff[row][Q - 1 - m])) * odd[m]
            other = term if other is None else other + term
        results[row] = total + other
        results[Q - 1 - row] = total - other
    return results


def krylov_body(stiff_y, weights, ints, heights, placed_ref, own_ref, left_ref, right_ref, kb_ref, kn_ref, wx_ref,
                v0_ref, v1_ref, v2_ref, mom_ref, kxs, kbs, vec, prod, tmp):
    column_refs = (
        [left_ref.at[k] for k in range(GHOST)]
        + [own_ref.at[k] for k in range(COLUMNS)]
        + [right_ref.at[k] for k in range(GHOST)]
    )

    lane = lane_ids((8, LANES))
    widths = [ref[TILES - 1, :, LANES - 1 :] for ref in column_refs]
    zero = jnp.zeros((8, 1), F32)
    widths = [zero] + widths + [zero]
    for t in range(2):
        here = jnp.zeros((8, LANES), F32)
        near = here
        for place in range(Q):
            k = Q * t + place + 1
            low, high = Q * place, Q * place + Q - 1
            here = jnp.where((lane >= low) & (lane <= high), widths[k], here)
            near = jnp.where(lane == low, widths[k - 1], near)
            near = jnp.where(lane == high, widths[k + 1], near)
        vec[0, :, t * LANES : (t + 1) * LANES] = here
        vec[1, :, t * LANES : (t + 1) * LANES] = near
    here, near = vec[0], vec[1]
    line = lane_ids((8, 2 * LANES))
    own = ((line >= GHOST * Q) & (line < NODES)) | (
        (line >= LANES) & (line < LANES + (Q - GHOST) * Q)
    )
    own = own.astype(F32)
    mass_x = here * wx_ref[...]
    vec[2] = mass_x * own
    vec[1] = mass_x + near * wx_ref[...]
    vec[3] = own * jnp.where(near > 0.0, 0.5, 1.0)
    inverse, inverse_near = (
        jnp.where(value > 0.0, 1.0 / jnp.where(value > 0.0, value, 1.0), 0.0)[0:1]
        for value in (here, near)
    )
    scaled = kb_ref[...] * inverse
    for k, part in enumerate(split3(scaled + kn_ref[...] * inverse_near)):
        kxs[k] = part
    for k, part in enumerate(split3(scaled * own[0:1])):
        kbs[k] = part

    h0, h1 = heights[0], heights[1]
    inverse_y = (1.0 / h0, 1.0 / h1)
    mass_y = []
    for y in range(ROWS):
        if y < Q - 1:
            mass_y.append(h0 * weights[y])
        elif y == Q - 1:
            mass_y.append((h0 + h1) * weights[0])
        else:
            mass_y.append(h1 * weights[y - Q + 1])

    def apply(source, target, operator, mass_row, low_key):
        dot_split(source, tmp, operator)
        sums = [[], []]
        for half in range(2):
            plane = ints[0] * LOCAL + half * 8 + lax.broadcasted_iota(jnp.int32, (8, LANES), 0)
            kappa = jnp.where(plane == 1, PLANES // 2, plane >> 1).astype(F32)
            beta = kappa * (2.0 * np.pi / (PLANES / 64.0))
            lam = (beta * beta + SIGMA) * 0.25
            square = cross = None
            for t in range(2):
                lanes = slice(t * LANES, (t + 1) * LANES)
                mass_x = vec[mass_row, :, lanes]
                shift = lam * mass_x
                weight = vec[3, :, lanes]
                here_square = here_cross = None
                shared = None
                for ey in range(2):
                    rows = [
                        slice(y * LOCAL + half * 8, y * LOCAL + half * 8 + 8)
                        for y in range((Q - 1) * ey, (Q - 1) * ey + Q)
                    ]
                    values = [source[r, lanes] for r in rows]
                    scale = mass_x * inverse_y[ey]
                    stiff = [scale * value for value in stiff_rows(stiff_y, values)]
                    if ey == 0:
                        shared = stiff.pop()
                    else:
                        stiff[0] = stiff[0] + shared
                    for k, part in enumerate(stiff):
                        y, value = (Q - 1) * ey + k, values[k]
                        image = mass_y[y] * (tmp[rows[k], lanes] + shift * value) + part
                        if target is not None:
                            target[rows[k], lanes] = image
                        one, two = value * value, value * image
                        here_square = one if here_square is None else here_square + one
                        here_cross = two if here_cross is None else here_cross + two
                here_square = here_square * weight
                if target is not None:
                    here_cross = here_cross * weight
                square = here_square if square is None else square + here_square
                cross = here_cross if cross is None else cross + here_cross
            prod[low_key * LOCAL + half * 8 : low_key * LOCAL + half * 8 + 8, :] = square
            prod[(low_key + 1) * LOCAL + half * 8 : (low_key + 1) * LOCAL + half * 8 + 8, :] = cross

    cut = Q - GHOST - 1
    for comp, start, places, base in face_parts():
        left, offset = windows(column_refs[: GHOST + 1], start)
        right, _ = windows(column_refs[-GHOST - 1 :], start)
        sides = [
            block_transpose(join_columns(left, offset, (GHOST,)), places, offset),
            block_transpose(join_columns(right, offset, (0,)), places, offset, cut),
        ]
        for t, values in enumerate(sides):
            lanes = slice(t * LANES, (t + 1) * LANES)
            for qy, value in zip(places, values):
                rows = slice(base + qy * LOCAL, base + qy * LOCAL + 8)
                v0_ref[comp, rows, lanes] = placed_ref[comp, rows, lanes] + value
    for comp in range(3):
        first, second, third = v0_ref.at[comp], v1_ref.at[comp], v2_ref.at[comp]
        prod[6 * LOCAL :, :] = jnp.zeros((LANES - 6 * LOCAL, LANES), F32)
        apply(first, second, kxs, 1, 0)
        apply(second, third, kxs, 1, 2)
        apply(third, None, kbs, 2, 4)
        row = lax.dot_general(
            jnp.ones((8, LANES), F32), prod[...], (((1,), (1,)), ((), ())),
            precision=HIGHEST, preferred_element_type=F32,
        )
        mom_ref[:, comp : comp + 1, :] = jnp.broadcast_to(
            row[0:1][None], (mom_ref.shape[0], 1, LANES)
        )


def krylov_stage(stiff_y, weights, ints, heights, placed, own, left, right, kb, near, wx, peers):
    smem = pl.BlockSpec(memory_space=pltpu.SMEM)

    def whole(array):
        return pl.BlockSpec(array.shape, lambda i: (0,) * array.ndim)

    def chunk(count):
        return pl.BlockSpec((count, TILES, 8, LANES), lambda i: (0, 0, 0, 0))

    vector = pl.BlockSpec((3, ROWS * LOCAL, 2 * LANES), lambda i: (0, 0, 0))
    shape = jax.ShapeDtypeStruct((3, ROWS * LOCAL, 2 * LANES), F32)

    def body(*refs):
        krylov_body(stiff_y, weights, *refs)

    return pl.pallas_call(
        body,
        grid=(1,),
        in_specs=[smem, smem, vector, chunk(COLUMNS), chunk(GHOST), chunk(GHOST), whole(kb), whole(near), whole(wx)],
        out_specs=[vector, vector, vector, pl.BlockSpec((peers, 8, LANES), lambda i: (0, 0, 0))],
        out_shape=[shape, shape, shape, jax.ShapeDtypeStruct((peers, 8, LANES), F32)],
        scratch_shapes=[
            pltpu.VMEM((3, 2 * LANES, 2 * LANES), BF16),
            pltpu.VMEM((3, 2 * LANES, 2 * LANES), BF16),
            pltpu.VMEM((4, 8, 2 * LANES), F32),
            pltpu.VMEM((LANES, LANES), F32),
            pltpu.VMEM((ROWS * LOCAL, 2 * LANES), F32),
        ],
        compiler_params=pltpu.CompilerParams(vmem_limit_bytes=24 * 2**20),
        name="krylov_stage",
    )(in_hbm(ints), in_hbm(heights), placed, own, left, right, kb, near, wx)


def unpack_body(v0_ref, v1_ref, v2_ref, out_ref, scr, flat):
    lane = lane_ids((16, LANES))
    run = COLUMNS * Q // 2
    for k, vector in enumerate((v0_ref, v1_ref, v2_ref)):
        for y in range(ROWS):
            rows = slice(y * LOCAL, (y + 1) * LOCAL)
            for t in range(2):
                value = vector[0, rows, t * LANES : (t + 1) * LANES]
                if y <= Q - 1:
                    scr[0, t, pl.ds(y, LOCAL, stride=PITCH), :] = value
                if y >= Q - 1:
                    scr[1, t, pl.ds(y - Q + 1, LOCAL, stride=PITCH), :] = value
        for ey in range(2):
            turned = []
            for r in range(2 * LOCAL):
                start = GHOST * Q if r % 2 == 0 else 0
                value = scr[ey, r % 2, (r // 2) * PITCH : (r // 2) * PITCH + 16, :]
                turned.append(turn(value, run * r - start))
            for tile in range(COLUMNS * Q * LOCAL // LANES):
                low, high = tile * LANES // run, (tile * LANES + LANES - 1) // run
                value = turned[low]
                for r in range(low + 1, high + 1):
                    value = jnp.where(lane >= run * r - LANES * tile, turned[r], value)
                place = (tile % 2) * 32 + ey * 16
                flat[tile // 2, place : place + 16, :] = value
        for qy in range(Q):
            for pair in range(Q):
                out_ref[0, k, qy * Q + pair] = flat[pair, pl.ds(qy, 4, stride=16), :]


def unpack(v0, v1, v2):
    vector = pl.BlockSpec((1, ROWS * LOCAL, 2 * LANES), lambda i: (i, 0, 0))
    target = pl.BlockSpec((1, 3, NODES, 4, LANES), lambda i: (i, 0, 0, 0, 0))
    shape = pltpu.HBM((3, 3, NODES, 4, LANES), F32)
    return pl.pallas_call(
        unpack_body,
        grid=(3,),
        in_specs=[vector] * 3,
        out_specs=target,
        out_shape=shape,
        scratch_shapes=[
            pltpu.VMEM((2, 2, LOCAL * PITCH, LANES), F32),
            pltpu.VMEM((Q, 64, LANES), F32),
        ],
        compiler_params=pltpu.CompilerParams(vmem_limit_bytes=24 * 2**20),
        name="unpack",
    )(v0, v1, v2)


def finish_body(mom_ref, u_ref, out_ref, coef):
    comp = pl.program_id(0)
    tiles = COLUMNS * Q * LOCAL // LANES

    @pl.when(comp == 0)
    def _():
        total = jnp.sum(mom_ref[...], axis=0)
        used = (lane_ids((8, LANES)) < LOCAL) & (
            lax.broadcasted_iota(jnp.int32, (8, LANES), 0) < 3
        )
        m = [jnp.where(used, turn(total, -LOCAL * k), 1.0) for k in range(6)]
        inv = 1.0 / m[0]
        m = [value * inv for value in m]
        d0, d1, d2 = (1.0 / jnp.sqrt(m[k]) for k in (1, 3, 5))
        g0, g1, g2 = d0, m[1] * d1, m[2] * d2
        l10 = m[2] * d0 * d1
        l20 = m[3] * d0 * d2
        k21 = m[4] * d1 * d2
        p1 = 1.0 - l10 * l10
        e = k21 - l20 * l10
        l21 = e / p1
        p2 = 1.0 - l20 * l20 - l21 * e
        y1 = g1 - l10 * g0
        y2 = g2 - l20 * g0 - l21 * y1
        z2 = y2 / p2
        z1 = y1 / p1 - l21 * z2
        z0 = g0 - l10 * z1 - l20 * z2
        lane = lane_ids((8, LANES))
        for k, value in enumerate((z0 * d0, z1 * d1, z2 * d2)):
            wide = [jnp.broadcast_to(value[:, j : j + 1], (8, LANES)) for j in range(LOCAL)]
            for tile in range(tiles):
                low = tile * LANES // (COLUMNS * Q)
                high = (tile * LANES + LANES - 1) // (COLUMNS * Q)
                chosen = wide[low]
                if high > low:
                    chosen = jnp.where(lane >= COLUMNS * Q * high - LANES * tile, wide[high], chosen)
                coef[k, tile] = chosen

    upper = lax.broadcasted_iota(jnp.int32, (4, LANES), 0) >= 2
    for pair in range(Q):
        factors = []
        for k in range(3):
            one, two = (
                jnp.broadcast_to(coef[k, 2 * pair + side, pl.ds(comp, 1), :], (4, LANES))
                for side in range(2)
            )
            factors.append(jnp.where(upper, two, one))
        for qy in range(Q):
            group = qy * Q + pair
            out_ref[0, group] = (
                factors[0] * u_ref[0, 0, group]
                + factors[1] * u_ref[0, 1, group]
                + factors[2] * u_ref[0, 2, group]
            )


def finish(moments, vectors):
    out = pl.pallas_call(
        finish_body,
        grid=(3,),
        in_specs=[
            pl.BlockSpec(moments.shape, lambda i: (0, 0, 0)),
            pl.BlockSpec((1, 3, NODES, 4, LANES), lambda i: (i, 0, 0, 0, 0)),
        ],
        out_specs=pl.BlockSpec((1, NODES, 4, LANES), lambda i: (i, 0, 0, 0)),
        out_shape=jax.ShapeDtypeStruct((3, NODES, 4, LANES), F32),
        scratch_shapes=[pltpu.VMEM((3, COLUMNS * Q * LOCAL // LANES, 8, LANES), F32)],
        compiler_params=pltpu.CompilerParams(vmem_limit_bytes=24 * 2**20),
        name="finish",
    )(moments, in_hbm(vectors))
    return from_groups(out)


def make_tables():
    derivative, weights = gll_tables(Q)
    basis, basis_slope, span_slope = fourier_table(PLANES)
    table = np.concatenate([basis.T, basis_slope.T], axis=1)
    table = table.astype(np.float32)
    eye = np.eye(Q)
    nodes = np.zeros((2, LANES, LANES))
    nodes[0, :NODES, :NODES] = np.kron(eye, derivative.T)
    nodes[1, :NODES, :NODES] = np.kron(derivative.T, eye)
    order = np.zeros((176, LANES))
    for qx in range(Q):
        for qy in range(Q):
            order[qx * 16 + qy, qy * Q + qx] = 1.0
    stack = np.concatenate([order, order @ nodes[0], order @ nodes[1]], axis=1)
    stack = np.concatenate(halves(stack), axis=0)
    plane = np.concatenate([nodes[0], nodes[1]], axis=1)
    mass = np.zeros((1, LANES), np.float32)
    mass[0, :NODES] = np.kron(weights, weights)
    stiff = (derivative.T * weights) @ derivative
    kb = np.zeros((2 * LANES, 2 * LANES))
    join = np.eye(2 * LANES)
    wx = np.zeros((1, 2 * LANES), np.float32)
    ends = []
    for t in range(2):
        for place in range(Q):
            low = t * LANES + place * Q
            kb[low : low + Q, low : low + Q] = stiff
            wx[0, low : low + Q] = weights
            ends.append(low)
    for left, right in zip(ends[:-1], ends[1:]):
        join[left + Q - 1, right] = 1.0
        join[right, left + Q - 1] = 1.0
    return dict(
        table=table, stack=stack, dz=halves(span_slope), plane=halves(plane), mass=mass,
        kb=kb.astype(np.float32), near=(kb @ join - kb).astype(np.float32), wx=wx,
        stiff=stiff.tolist(), weights=weights.tolist(),
    )


def local(adjoint_velocity, base_flow, column_widths, row_heights, base_phase):
    tables = make_tables()
    elem_count = lax.axis_size("elem")
    ints = jnp.stack([lax.axis_index("four").astype(jnp.int32), base_phase[0]])
    send = pack(adjoint_velocity)
    arrived = lax.all_to_all(send, "four", split_axis=0, concat_axis=0, tiled=True)
    fields, *turned = base_stage(
        ints, column_widths, row_heights, base_flow, jnp.asarray(tables["table"]),
        jnp.asarray(tables["stack"]), *(jnp.asarray(a) for a in tables["dz"]),
    )
    source = lines_stage(
        ints, column_widths, row_heights, arrived, fields, turned,
        *(jnp.asarray(a) for a in tables["plane"]), jnp.asarray(tables["mass"]),
    )
    own = lax.all_to_all(source, "four", split_axis=0, concat_axis=0, tiled=True)
    up = [(i, i + 1) for i in range(elem_count - 1)]
    left = lax.ppermute(own[COLUMNS - GHOST :], "elem", up)
    right = lax.ppermute(own[:GHOST], "elem", [(j, i) for i, j in up])
    v0, v1, v2, moments = krylov_stage(
        tables["stiff"], tables["weights"], ints, row_heights, place_stage(own), own, left, right,
        jnp.asarray(tables["kb"]), jnp.asarray(tables["near"]), jnp.asarray(tables["wx"]), elem_count,
    )
    moments = lax.all_to_all(moments, "elem", split_axis=0, concat_axis=0, tiled=True)
    return finish(moments, unpack(v0, v1, v2))


def solution(mesh):
    split_spec = P(None, None, None, ("elem", "four"))
    return jax.shard_map(
        local,
        mesh=mesh,
        in_specs=(split_spec, split_spec, P("elem"), P(), P()),
        out_specs=split_spec,
        check_vma=False,
    )
```

```python
import jax
import jax.numpy as jnp
import numpy as np
from jax import lax
from jax.experimental import pallas as pl
from jax.experimental.pallas import tpu as pltpu
from jax.sharding import PartitionSpec as P

Q = 11
PLANES = 256
PEERS = 16
LOCAL = 16
COLUMNS = 16
GHOST = 3
ROWS = 21
NODES = Q * Q
LANES = 128
PITCH = 17
FACE = ROWS * Q
TILES = 11
NU = 0.005
DT = 0.01
SIGMA = 1.0 / (NU * DT)
HIGHEST = lax.Precision.HIGHEST
F32 = jnp.float32
BF16 = jnp.bfloat16


def legendre_values(points, node_count):
    table_rows = np.zeros((points.shape[0], node_count))
    table_rows[:, 0] = 1.0
    table_rows[:, 1] = points
    for degree_now in range(2, node_count):
        table_rows[:, degree_now] = (
            (2 * degree_now - 1) * points * table_rows[:, degree_now - 1]
            - (degree_now - 1) * table_rows[:, degree_now - 2]
        ) / degree_now
    return table_rows


def gll_tables(node_count):
    degree = node_count - 1
    points = np.cos(np.pi * np.arange(node_count) / degree)
    for newton_step in range(60):
        legendre = legendre_values(points, node_count)
        points = points - (points * legendre[:, degree] - legendre[:, degree - 1]) / (
            node_count * legendre[:, degree]
        )
    legendre = legendre_values(points, node_count)
    weights = 2.0 / (degree * node_count * legendre[:, degree] ** 2)
    points = points[::-1]
    weights = weights[::-1]
    end_values = legendre[::-1, degree]
    derivative = np.zeros((node_count, node_count))
    for row_index in range(node_count):
        for column in range(node_count):
            if row_index != column:
                derivative[row_index, column] = end_values[row_index] / (
                    end_values[column] * (points[row_index] - points[column])
                )
    derivative[0, 0] = -degree * node_count / 4.0
    derivative[degree, degree] = degree * node_count / 4.0
    return derivative, weights


def fourier_table(plane_count):
    positions = np.arange(plane_count)
    basis_rows = np.zeros((plane_count, plane_count))
    basis_rows[0] = 1.0 / np.sqrt(plane_count)
    basis_rows[1] = np.cos(np.pi * positions) / np.sqrt(plane_count)
    for wave_index in range(1, plane_count // 2):
        angle = 2.0 * np.pi * wave_index * positions / plane_count
        basis_rows[2 * wave_index] = np.sqrt(2.0 / plane_count) * np.cos(angle)
        basis_rows[2 * wave_index + 1] = np.sqrt(2.0 / plane_count) * np.sin(angle)
    wave_counts = np.arange(plane_count) // 2
    wave_counts[1] = plane_count // 2
    wave_counts[0] = 0
    wavenumbers = 2.0 * np.pi * wave_counts / (plane_count / 64.0)
    rotate = np.zeros((plane_count, plane_count))
    for wave_index in range(1, plane_count // 2):
        rotate[2 * wave_index, 2 * wave_index + 1] = wavenumbers[2 * wave_index]
        rotate[2 * wave_index + 1, 2 * wave_index] = -wavenumbers[2 * wave_index]
    return basis_rows, rotate.T @ basis_rows, basis_rows.T @ rotate @ basis_rows


def halves(array):
    high = np.asarray(array, np.float32).astype(jnp.bfloat16)
    low = (np.asarray(array, np.float64) - high.astype(np.float64)).astype(jnp.bfloat16)
    return high, low


def split(value):
    high = value.astype(BF16)
    return high, (value - high.astype(F32)).astype(BF16)


def dot(left, right):
    return jnp.dot(left, right, preferred_element_type=F32)


def dot3(left_high, left_low, high, low):
    half = left_high.shape[0] // 2
    parts = [slice(0, half), slice(half, None)]
    totals = [dot(left_high[p], low) for p in parts]
    totals = [t + dot(left_low[p], high) for t, p in zip(totals, parts)]
    return [t + dot(left_high[p], high) for t, p in zip(totals, parts)]


def dot_full(left, right):
    return jnp.dot(left, right, precision=HIGHEST, preferred_element_type=F32)


def in_hbm(array):
    return pltpu.with_memory_space_constraint(array, pltpu.HBM)


def to_groups(array):
    array = jnp.transpose(array, (0, 2, 1, 3)).reshape(3, Q, 2, Q, 2, LANES)
    return jnp.transpose(array, (0, 1, 3, 4, 2, 5)).reshape(3, NODES, 4, LANES)


def from_groups(array):
    array = jnp.transpose(array.reshape(3, Q, Q, 2, 2, LANES), (0, 1, 4, 2, 3, 5))
    return jnp.transpose(array.reshape(3, Q, 2, COLUMNS * Q * LOCAL), (0, 2, 1, 3))


def lane_ids(shape):
    return lax.broadcasted_iota(jnp.int32, shape, len(shape) - 1)


def turn(value, shift):
    shift = shift % LANES
    return value if shift == 0 else pltpu.roll(value, shift, value.ndim - 1)


def block_transpose(arrays, places, offset=0, first=0):
    lane = lane_ids(arrays[0].shape)
    turned = [turn(array, Q * (first + k) - offset) for k, array in enumerate(arrays)]
    results = []
    for place in places:
        distance = (lane - Q * place) & (LANES - 1)
        chosen = turned[0]
        for k in range(1, len(turned)):
            chosen = jnp.where(distance >= Q * (first + k), turned[k], chosen)
        inside = distance < Q * (first + len(turned))
        if first:
            inside = inside & (distance >= Q * first)
        chosen = jnp.where(inside, chosen, 0.0)
        results.append(turn(chosen, -Q * place))
    return results


def pack_body(in_ref, out_ref, flat, scr0, scr1):
    lane = lane_ids((16, LANES))
    scratches = (scr0, scr1)
    tiles = COLUMNS * Q * LOCAL // LANES
    for qy in range(Q):
        for pair in range(Q):
            flat[pair, pl.ds(qy, 4, stride=16), :] = in_ref[0, qy * Q + pair]
    for ey in range(2):
        def read(tile):
            low = (tile % 2) * 32 + ey * 16
            return flat[tile // 2, low : low + 16, :]

        for j in range(LOCAL):
            for t in range(2):
                offset = j * COLUMNS * Q + NODES * t
                tile, shift = offset // LANES, offset % LANES
                first = read(tile)
                if shift and tile + 1 < tiles:
                    first = jnp.where(lane >= shift, first, read(tile + 1))
                scratches[t][ey, j * PITCH : j * PITCH + 16, :] = turn(first, -shift)
    for ey in range(2):
        for t in range(2):
            rows = [scratches[t][ey, pl.ds(qy, LOCAL, stride=PITCH), :] for qy in range(Q)]
            for place, value in enumerate(block_transpose(rows, range(Q if t == 0 else COLUMNS - Q))):
                out_ref[Q * t + place, 0, ey] = value


def pack(adjoint):
    return pl.pallas_call(
        pack_body,
        grid=(3,),
        in_specs=[pl.BlockSpec((1, NODES, 4, LANES), lambda i: (i, 0, 0, 0))],
        out_specs=pl.BlockSpec((PEERS, 1, 2, LOCAL, LANES), lambda i: (0, i, 0, 0, 0)),
        out_shape=jax.ShapeDtypeStruct((PEERS, 3, 2, LOCAL, LANES), F32),
        scratch_shapes=[
            pltpu.VMEM((Q, 64, LANES), F32),
            pltpu.VMEM((2, LOCAL * PITCH, LANES), F32),
            pltpu.VMEM((2, LOCAL * PITCH, LANES), F32),
        ],
        compiler_params=pltpu.CompilerParams(vmem_limit_bytes=24 * 2**20),
        name="pack",
    )(in_hbm(to_groups(adjoint)))


def base_body(ints, widths, heights, base_ref, table_ref, stack_ref, dzh_ref, dzl_ref,
              field_ref, fgh_ref, fgl_ref, fh_ref, fl_ref, scr):
    step = pl.program_id(0)

    @pl.when(step == 0)
    def _():
        scr[...] = jnp.zeros_like(scr)
        rows = pltpu.roll(table_ref[...], (PLANES - ints[1]) % PLANES, 0)
        for k in range(2):
            high, low = split(rows[:, k * PLANES : (k + 1) * PLANES])
            fgh_ref[k * PLANES : (k + 1) * PLANES, :] = high
            fgl_ref[k * PLANES : (k + 1) * PLANES, :] = low
        high, low = split(jnp.transpose(rows[:, :PLANES]))
        fh_ref[...] = high
        fl_ref[...] = low

    for qx in range(Q):
        part = base_ref[0, 0, :, qx * PLANES : (qx + 1) * PLANES]
        scr[qx * 16 : qx * 16 + Q, :] = part
        scr[176 + qx * 16 : 176 + qx * 16 + Q, :] = part
    mixed = lax.dot_general(
        scr[...], stack_ref[...], (((0,), (0,)), ((), ())), preferred_element_type=F32
    )
    plain = mixed[:, :LANES]
    field_ref[0, 0, 0] = plain
    field_ref[1, 0, 0] = mixed[:, LANES : 2 * LANES] * (2.0 / widths[ints[0]])
    field_ref[2, 0, 0] = mixed[:, 2 * LANES :] * (2.0 / heights[step % 2])
    exact = plain.astype(BF16)
    field_ref[3, 0, 0] = dot(dzh_ref[...], exact) + dot(dzl_ref[...], exact)


def base_stage(ints, widths, heights, base, table, stack, dz_high, dz_low):
    smem = pl.BlockSpec(memory_space=pltpu.SMEM)

    def whole(shape):
        return pl.BlockSpec(shape, lambda i: (0,) * len(shape))

    return pl.pallas_call(
        base_body,
        grid=(6,),
        in_specs=[
            smem, smem, smem,
            pl.BlockSpec((1, 1, Q, Q * PLANES), lambda i: (i // 2, i % 2, 0, 0)),
            whole(table.shape), whole(stack.shape), whole(dz_high.shape), whole(dz_low.shape),
        ],
        out_specs=[
            pl.BlockSpec((4, 1, 1, PLANES, LANES), lambda i: (0, i // 2, i % 2, 0, 0)),
            whole((2 * PLANES, PLANES)), whole((2 * PLANES, PLANES)),
            whole((PLANES, PLANES)), whole((PLANES, PLANES)),
        ],
        out_shape=[
            jax.ShapeDtypeStruct((4, 3, 2, PLANES, LANES), F32),
            jax.ShapeDtypeStruct((2 * PLANES, PLANES), BF16),
            jax.ShapeDtypeStruct((2 * PLANES, PLANES), BF16),
            jax.ShapeDtypeStruct((PLANES, PLANES), BF16),
            jax.ShapeDtypeStruct((PLANES, PLANES), BF16),
        ],
        scratch_shapes=[pltpu.VMEM((352, PLANES), BF16)],
        name="base_stage",
    )(ints, widths, heights, base, table, stack, dz_high, dz_low)


def lines_body(ints, widths, heights, in_ref, field_hbm, fgh_ref, fgl_ref, fh_ref, fl_ref,
               dh_ref, dl_ref, mass_ref, out_ref, fields, lines, slopes, packed, sems):
    copies = [
        pltpu.make_async_copy(field_hbm.at[k], fields.at[k], sems.at[k]) for k in range(4)
    ]
    for copy in copies:
        copy.start()
    width = widths[ints[0]]
    pairs = [((2 * p) // 2, (2 * p) % 2, (2 * p + 1) % 2) for p in range(3)]
    double_dh = jnp.concatenate([dh_ref[...], dh_ref[...]], axis=0)

    def coeffs(c, ey):
        return in_ref[:, c, ey].reshape(PLANES, LANES)

    for c, _, _ in pairs:
        high, low = split(jnp.concatenate([coeffs(c, 0), coeffs(c, 1)], axis=1))
        both = dot3(fgh_ref[...], fgl_ref[...], high, low)
        for ey in range(2):
            line = both[0][:, ey * LANES : (ey + 1) * LANES]
            lines[c, ey] = line
            slopes[2, c, ey] = both[1][:, ey * LANES : (ey + 1) * LANES]
            high_line, low_line = split(line)
            wide = jnp.concatenate([high_line, low_line], axis=1)
            parts = [slice(0, LANES), slice(LANES, PLANES)]
            planes = [dot(wide[p], double_dh) for p in parts]
            planes = [v + dot(high_line[p], dl_ref[...]) for v, p in zip(planes, parts)]
            for plane, p in zip(planes, parts):
                slopes[0, c, ey, p] = plane[:, :LANES] * (2.0 / width)
                slopes[1, c, ey, p] = plane[:, LANES:] * (2.0 / heights[ey])
    copies[0].wait()
    lane = lane_ids((PLANES, LANES))
    for c in range(3):
        copies[1 + c].wait()
        pieces = []
        for ey in range(2):
            total = fields[0, 0, ey] * slopes[0, c, ey]
            for d in range(1, 3):
                total = total + fields[0, d, ey] * slopes[d, c, ey]
            for d in range(3):
                total = total - lines[d, ey] * fields[1 + c, d, ey]
            pieces.append(total)
        high, low = split(jnp.concatenate(pieces, axis=1))
        hat = jnp.concatenate(dot3(fh_ref[...], fl_ref[...], high, low), axis=0)
        values = []
        for ey in range(2):
            mass = mass_ref[...] * (width * heights[ey] * 0.25)
            source = SIGMA * coeffs(c, ey) + hat[:, ey * LANES : (ey + 1) * LANES] * (1.0 / NU)
            values.append(mass * source)
        values[0] = values[0] + jnp.where(lane >= NODES - Q, turn(values[1], NODES - Q), 0.0)
        for ey in range(2):
            packed[c, ey] = values[ey]
    lane = lane_ids((PEERS, 8, LANES))
    pieces = []
    for half in range(2):
        for c in range(3):
            base = (half * 3 + c) * FACE
            for ey in range(2):
                value = packed[c, ey].reshape(PEERS, 2, 8, LANES)[:, half]
                pieces.append((base + NODES * ey, turn(value, base + (NODES - Q) * ey)))
    pieces.append((6 * FACE, jnp.full((PEERS, 8, LANES), width, F32)))
    starts = [start for start, _ in pieces] + [TILES * LANES]
    for tile in range(TILES):
        low, high = tile * LANES, (tile + 1) * LANES
        chosen = None
        for k, (start, value) in enumerate(pieces):
            if start < high and starts[k + 1] > low:
                chosen = value if chosen is None else jnp.where(lane >= start - low, value, chosen)
        out_ref[:, tile] = chosen


def lines_stage(ints, widths, heights, arrived, fields, tables, d_high, d_low, mass):
    smem = pl.BlockSpec(memory_space=pltpu.SMEM)

    def whole(array):
        return pl.BlockSpec(array.shape, lambda i: (0,) * array.ndim)

    return pl.pallas_call(
        lines_body,
        grid=(1,),
        in_specs=[smem, smem, smem, whole(arrived), pl.BlockSpec(memory_space=pl.ANY)]
        + [whole(a) for a in tables] + [whole(d_high), whole(d_low), whole(mass)],
        out_specs=pl.BlockSpec((PEERS, TILES, 8, LANES), lambda i: (0, 0, 0, 0)),
        out_shape=jax.ShapeDtypeStruct((PEERS, TILES, 8, LANES), F32),
        scratch_shapes=[
            pltpu.VMEM((4, 3, 2, PLANES, LANES), F32),
            pltpu.VMEM((3, 2, PLANES, LANES), F32),
            pltpu.VMEM((3, 3, 2, PLANES, LANES), F32),
            pltpu.VMEM((3, 2, PLANES, LANES), F32),
            pltpu.SemaphoreType.DMA((4,)),
        ],
        compiler_params=pltpu.CompilerParams(vmem_limit_bytes=24 * 2**20),
        name="lines_stage",
    )(*map(in_hbm, (ints, widths, heights)), arrived, in_hbm(fields), *map(in_hbm, tables), d_high, d_low, mass)


def join_columns(chunks, offset, partial=()):
    lane = (lane_ids(chunks[0].shape) - offset) & (LANES - 1)
    place = lane - Q * ((lane * 5958) >> 16)
    at_first = (place == 0) & (lane < NODES)
    at_last = (place == Q - 1) & (lane < NODES)
    results = []
    for k, chunk in enumerate(chunks):
        extra = 0.0
        if k > 0:
            extra = jnp.where(at_first, turn(chunks[k - 1], -(Q - 1)), extra)
        if k + 1 < len(chunks):
            extra = jnp.where(at_last, turn(chunks[k + 1], Q - 1), extra)
        results.append(extra if k in partial else chunk + extra)
    return results


def windows(refs, start):
    tile, offset = start // LANES, start % LANES
    chunks = [ref[tile] for ref in refs]
    if offset:
        lane = lane_ids((8, LANES))
        chunks = [
            jnp.where(lane >= offset, chunk, ref[tile + 1]) for chunk, ref in zip(chunks, refs)
        ]
    return chunks, offset


def face_parts():
    for comp in range(3):
        for half in range(2):
            for ey in range(2):
                start = (half * 3 + comp) * FACE + (NODES - Q) * ey
                yield comp, start, range(ey, Q), (Q - 1) * ey * LOCAL + half * 8


def place_body(own_ref, out_ref):
    refs = [own_ref.at[k] for k in range(COLUMNS)]
    cut = Q - GHOST
    for comp, start, places, base in face_parts():
        chunks, offset = windows(refs, start)
        chunks = join_columns(chunks, offset)
        sides = [
            block_transpose(chunks[:cut], places, offset, GHOST),
            block_transpose(chunks[cut:], places, offset),
        ]
        for t, values in enumerate(sides):
            for qy, value in zip(places, values):
                row = base + qy * LOCAL
                out_ref[comp, row : row + 8, t * LANES : (t + 1) * LANES] = value


def place_stage(own):
    return pl.pallas_call(
        place_body,
        grid=(1,),
        in_specs=[pl.BlockSpec(own.shape, lambda i: (0, 0, 0, 0))],
        out_specs=pl.BlockSpec((3, ROWS * LOCAL, 2 * LANES), lambda i: (0, 0, 0)),
        out_shape=jax.ShapeDtypeStruct((3, ROWS * LOCAL, 2 * LANES), F32),
        compiler_params=pltpu.CompilerParams(vmem_limit_bytes=24 * 2**20),
        name="place_stage",
    )(own)


def split3(value):
    high = value.astype(BF16)
    rest = value - high.astype(F32)
    mid = rest.astype(BF16)
    return high, mid, (rest - mid.astype(F32)).astype(BF16)


def dot_split(source, target, operator):
    cut = 176
    parts = [slice(0, cut), slice(cut, ROWS * LOCAL)]
    pieces = [split3(source[p, :]) for p in parts]
    totals = [None, None]
    for left, right in ((2, 0), (0, 2), (1, 1), (1, 0), (0, 1), (0, 0)):
        for k in range(2):
            value = dot(pieces[k][left], operator[right])
            totals[k] = value if totals[k] is None else totals[k] + value
    for k in range(2):
        target[parts[k], :] = totals[k]


def stiff_rows(stiff, values):
    middle = Q // 2
    even = [values[m] + values[Q - 1 - m] for m in range(middle)] + [values[middle]]
    odd = [values[m] - values[Q - 1 - m] for m in range(middle)]
    results = [None] * Q
    for row in range(middle + 1):
        total = None
        for m in range(middle + 1):
            factor = stiff[row][m] if m == middle or row == middle else (
                0.5 * (stiff[row][m] + stiff[row][Q - 1 - m])
            )
            term = factor * even[m]
            total = term if total is None else total + term
        if row == middle:
            results[row] = total
            continue
        other = None
        for m in range(middle):
            term = (0.5 * (stiff[row][m] - stiff[row][Q - 1 - m])) * odd[m]
            other = term if other is None else other + term
        results[row] = total + other
        results[Q - 1 - row] = total - other
    return results


def krylov_body(stiff_y, weights, ints, heights, placed_ref, own_ref, left_ref, right_ref, kb_ref, kn_ref, wx_ref,
                v0_ref, v1_ref, v2_ref, mom_ref, kxs, kbs, vec, prod, tmp):
    column_refs = (
        [left_ref.at[k] for k in range(GHOST)]
        + [own_ref.at[k] for k in range(COLUMNS)]
        + [right_ref.at[k] for k in range(GHOST)]
    )

    lane = lane_ids((8, LANES))
    widths = [ref[TILES - 1, :, LANES - 1 :] for ref in column_refs]
    zero = jnp.zeros((8, 1), F32)
    widths = [zero] + widths + [zero]
    for t in range(2):
        here = jnp.zeros((8, LANES), F32)
        near = here
        for place in range(Q):
            k = Q * t + place + 1
            low, high = Q * place, Q * place + Q - 1
            here = jnp.where((lane >= low) & (lane <= high), widths[k], here)
            near = jnp.where(lane == low, widths[k - 1], near)
            near = jnp.where(lane == high, widths[k + 1], near)
        vec[0, :, t * LANES : (t + 1) * LANES] = here
        vec[1, :, t * LANES : (t + 1) * LANES] = near
    here, near = vec[0], vec[1]
    line = lane_ids((8, 2 * LANES))
    own = ((line >= GHOST * Q) & (line < NODES)) | (
        (line >= LANES) & (line < LANES + (Q - GHOST) * Q)
    )
    own = own.astype(F32)
    mass_x = here * wx_ref[...]
    vec[2] = mass_x * own
    vec[1] = mass_x + near * wx_ref[...]
    vec[3] = own * jnp.where(near > 0.0, 0.5, 1.0)
    inverse, inverse_near = (
        jnp.where(value > 0.0, 1.0 / jnp.where(value > 0.0, value, 1.0), 0.0)[0:1]
        for value in (here, near)
    )
    scaled = kb_ref[...] * inverse
    for k, part in enumerate(split3(scaled + kn_ref[...] * inverse_near)):
        kxs[k] = part
    for k, part in enumerate(split3(scaled * own[0:1])):
        kbs[k] = part

    h0, h1 = heights[0], heights[1]
    inverse_y = (1.0 / h0, 1.0 / h1)
    mass_y = []
    for y in range(ROWS):
        if y < Q - 1:
            mass_y.append(h0 * weights[y])
        elif y == Q - 1:
            mass_y.append((h0 + h1) * weights[0])
        else:
            mass_y.append(h1 * weights[y - Q + 1])

    def apply(source, target, tmp, prod, mass_row, low_key):
        for half in range(2):
            plane = ints[0] * LOCAL + half * 8 + lax.broadcasted_iota(jnp.int32, (8, LANES), 0)
            kappa = jnp.where(plane == 1, PLANES // 2, plane >> 1).astype(F32)
            beta = kappa * (2.0 * np.pi / (PLANES / 64.0))
            lam = (beta * beta + SIGMA) * 0.25
            square = cross = None
            for t in range(2):
                lanes = slice(t * LANES, (t + 1) * LANES)
                mass_x = vec[mass_row, :, lanes]
                shift = lam * mass_x
                weight = vec[3, :, lanes]
                here_square = here_cross = None
                shared = None
                for ey in range(2):
                    rows = [
                        slice(y * LOCAL + half * 8, y * LOCAL + half * 8 + 8)
                        for y in range((Q - 1) * ey, (Q - 1) * ey + Q)
                    ]
                    values = [source[r, lanes] for r in rows]
                    scale = mass_x * inverse_y[ey]
                    stiff = [scale * value for value in stiff_rows(stiff_y, values)]
                    if ey == 0:
                        shared = stiff.pop()
                    else:
                        stiff[0] = stiff[0] + shared
                    for k, part in enumerate(stiff):
                        y, value = (Q - 1) * ey + k, values[k]
                        image = mass_y[y] * (tmp[rows[k], lanes] + shift * value) + part
                        if target is not None:
                            target[rows[k], lanes] = image
                        one, two = value * value, value * image
                        here_square = one if here_square is None else here_square + one
                        here_cross = two if here_cross is None else here_cross + two
                here_square = here_square * weight
                if target is not None:
                    here_cross = here_cross * weight
                square = here_square if square is None else square + here_square
                cross = here_cross if cross is None else cross + here_cross
            prod[low_key * LOCAL + half * 8 : low_key * LOCAL + half * 8 + 8, :] = square
            prod[(low_key + 1) * LOCAL + half * 8 : (low_key + 1) * LOCAL + half * 8 + 8, :] = cross

    cut = Q - GHOST - 1
    for comp, start, places, base in face_parts():
        left, offset = windows(column_refs[: GHOST + 1], start)
        right, _ = windows(column_refs[-GHOST - 1 :], start)
        sides = [
            block_transpose(join_columns(left, offset, (GHOST,)), places, offset),
            block_transpose(join_columns(right, offset, (0,)), places, offset, cut),
        ]
        for t, values in enumerate(sides):
            lanes = slice(t * LANES, (t + 1) * LANES)
            for qy, value in zip(places, values):
                rows = slice(base + qy * LOCAL, base + qy * LOCAL + 8)
                v0_ref[comp, rows, lanes] = placed_ref[comp, rows, lanes] + value
    vectors = (v0_ref, v1_ref, v2_ref)
    tasks = [(stage, comp) for stage in range(3) for comp in range(3)]

    def multiply(stage, comp):
        dot_split(vectors[stage].at[comp], tmp.at[comp], kxs if stage < 2 else kbs)

    multiply(*tasks[0])
    for k, (stage, comp) in enumerate(tasks):
        if k + 1 < len(tasks):
            multiply(*tasks[k + 1])
        target = vectors[stage + 1].at[comp] if stage < 2 else None
        mass_row = 1 if stage < 2 else 2
        apply(vectors[stage].at[comp], target, tmp.at[comp], prod.at[comp], mass_row, 2 * stage)
    for comp in range(3):
        prod[comp, 6 * LOCAL :, :] = jnp.zeros((LANES - 6 * LOCAL, LANES), F32)
        row = lax.dot_general(
            jnp.ones((8, LANES), F32), prod[comp], (((1,), (1,)), ((), ())),
            precision=HIGHEST, preferred_element_type=F32,
        )
        mom_ref[:, comp : comp + 1, :] = jnp.broadcast_to(
            row[0:1][None], (mom_ref.shape[0], 1, LANES)
        )


def krylov_stage(stiff_y, weights, ints, heights, placed, own, left, right, kb, near, wx, peers):
    smem = pl.BlockSpec(memory_space=pltpu.SMEM)

    def whole(array):
        return pl.BlockSpec(array.shape, lambda i: (0,) * array.ndim)

    def chunk(count):
        return pl.BlockSpec((count, TILES, 8, LANES), lambda i: (0, 0, 0, 0))

    vector = pl.BlockSpec((3, ROWS * LOCAL, 2 * LANES), lambda i: (0, 0, 0))
    shape = jax.ShapeDtypeStruct((3, ROWS * LOCAL, 2 * LANES), F32)

    def body(*refs):
        krylov_body(stiff_y, weights, *refs)

    return pl.pallas_call(
        body,
        grid=(1,),
        in_specs=[smem, smem, vector, chunk(COLUMNS), chunk(GHOST), chunk(GHOST), whole(kb), whole(near), whole(wx)],
        out_specs=[vector, vector, vector, pl.BlockSpec((peers, 8, LANES), lambda i: (0, 0, 0))],
        out_shape=[shape, shape, shape, jax.ShapeDtypeStruct((peers, 8, LANES), F32)],
        scratch_shapes=[
            pltpu.VMEM((3, 2 * LANES, 2 * LANES), BF16),
            pltpu.VMEM((3, 2 * LANES, 2 * LANES), BF16),
            pltpu.VMEM((4, 8, 2 * LANES), F32),
            pltpu.VMEM((3, LANES, LANES), F32),
            pltpu.VMEM((3, ROWS * LOCAL, 2 * LANES), F32),
        ],
        compiler_params=pltpu.CompilerParams(vmem_limit_bytes=24 * 2**20),
        name="krylov_stage",
    )(in_hbm(ints), in_hbm(heights), placed, own, left, right, kb, near, wx)


def unpack_body(v0_ref, v1_ref, v2_ref, out_ref, scr, flat):
    lane = lane_ids((16, LANES))
    run = COLUMNS * Q // 2
    for k, vector in enumerate((v0_ref, v1_ref, v2_ref)):
        for y in range(ROWS):
            rows = slice(y * LOCAL, (y + 1) * LOCAL)
            for t in range(2):
                value = vector[0, rows, t * LANES : (t + 1) * LANES]
                if y <= Q - 1:
                    scr[0, t, pl.ds(y, LOCAL, stride=PITCH), :] = value
                if y >= Q - 1:
                    scr[1, t, pl.ds(y - Q + 1, LOCAL, stride=PITCH), :] = value
        for ey in range(2):
            turned = []
            for r in range(2 * LOCAL):
                start = GHOST * Q if r % 2 == 0 else 0
                value = scr[ey, r % 2, (r // 2) * PITCH : (r // 2) * PITCH + 16, :]
                turned.append(turn(value, run * r - start))
            for tile in range(COLUMNS * Q * LOCAL // LANES):
                low, high = tile * LANES // run, (tile * LANES + LANES - 1) // run
                value = turned[low]
                for r in range(low + 1, high + 1):
                    value = jnp.where(lane >= run * r - LANES * tile, turned[r], value)
                place = (tile % 2) * 32 + ey * 16
                flat[tile // 2, place : place + 16, :] = value
        for qy in range(Q):
            for pair in range(Q):
                out_ref[0, k, qy * Q + pair] = flat[pair, pl.ds(qy, 4, stride=16), :]


def unpack(v0, v1, v2):
    vector = pl.BlockSpec((1, ROWS * LOCAL, 2 * LANES), lambda i: (i, 0, 0))
    target = pl.BlockSpec((1, 3, NODES, 4, LANES), lambda i: (i, 0, 0, 0, 0))
    shape = pltpu.HBM((3, 3, NODES, 4, LANES), F32)
    return pl.pallas_call(
        unpack_body,
        grid=(3,),
        in_specs=[vector] * 3,
        out_specs=target,
        out_shape=shape,
        scratch_shapes=[
            pltpu.VMEM((2, 2, LOCAL * PITCH, LANES), F32),
            pltpu.VMEM((Q, 64, LANES), F32),
        ],
        compiler_params=pltpu.CompilerParams(vmem_limit_bytes=24 * 2**20),
        name="unpack",
    )(v0, v1, v2)


def finish_body(mom_ref, u_ref, out_ref, coef):
    comp = pl.program_id(0)
    tiles = COLUMNS * Q * LOCAL // LANES

    @pl.when(comp == 0)
    def _():
        total = jnp.sum(mom_ref[...], axis=0)
        used = (lane_ids((8, LANES)) < LOCAL) & (
            lax.broadcasted_iota(jnp.int32, (8, LANES), 0) < 3
        )
        m = [jnp.where(used, turn(total, -LOCAL * k), 1.0) for k in range(6)]
        inv = 1.0 / m[0]
        m = [value * inv for value in m]
        d0, d1, d2 = (1.0 / jnp.sqrt(m[k]) for k in (1, 3, 5))
        g0, g1, g2 = d0, m[1] * d1, m[2] * d2
        l10 = m[2] * d0 * d1
        l20 = m[3] * d0 * d2
        k21 = m[4] * d1 * d2
        p1 = 1.0 - l10 * l10
        e = k21 - l20 * l10
        l21 = e / p1
        p2 = 1.0 - l20 * l20 - l21 * e
        y1 = g1 - l10 * g0
        y2 = g2 - l20 * g0 - l21 * y1
        z2 = y2 / p2
        z1 = y1 / p1 - l21 * z2
        z0 = g0 - l10 * z1 - l20 * z2
        lane = lane_ids((8, LANES))
        for k, value in enumerate((z0 * d0, z1 * d1, z2 * d2)):
            wide = [jnp.broadcast_to(value[:, j : j + 1], (8, LANES)) for j in range(LOCAL)]
            for tile in range(tiles):
                low = tile * LANES // (COLUMNS * Q)
                high = (tile * LANES + LANES - 1) // (COLUMNS * Q)
                chosen = wide[low]
                if high > low:
                    chosen = jnp.where(lane >= COLUMNS * Q * high - LANES * tile, wide[high], chosen)
                coef[k, tile] = chosen

    upper = lax.broadcasted_iota(jnp.int32, (4, LANES), 0) >= 2
    for pair in range(Q):
        factors = []
        for k in range(3):
            one, two = (
                jnp.broadcast_to(coef[k, 2 * pair + side, pl.ds(comp, 1), :], (4, LANES))
                for side in range(2)
            )
            factors.append(jnp.where(upper, two, one))
        for qy in range(Q):
            group = qy * Q + pair
            out_ref[0, group] = (
                factors[0] * u_ref[0, 0, group]
                + factors[1] * u_ref[0, 1, group]
                + factors[2] * u_ref[0, 2, group]
            )


def finish(moments, vectors):
    out = pl.pallas_call(
        finish_body,
        grid=(3,),
        in_specs=[
            pl.BlockSpec(moments.shape, lambda i: (0, 0, 0)),
            pl.BlockSpec((1, 3, NODES, 4, LANES), lambda i: (i, 0, 0, 0, 0)),
        ],
        out_specs=pl.BlockSpec((1, NODES, 4, LANES), lambda i: (i, 0, 0, 0)),
        out_shape=jax.ShapeDtypeStruct((3, NODES, 4, LANES), F32),
        scratch_shapes=[pltpu.VMEM((3, COLUMNS * Q * LOCAL // LANES, 8, LANES), F32)],
        compiler_params=pltpu.CompilerParams(vmem_limit_bytes=24 * 2**20),
        name="finish",
    )(moments, in_hbm(vectors))
    return from_groups(out)


def make_tables():
    derivative, weights = gll_tables(Q)
    basis, basis_slope, span_slope = fourier_table(PLANES)
    table = np.concatenate([basis.T, basis_slope.T], axis=1)
    table = table.astype(np.float32)
    eye = np.eye(Q)
    nodes = np.zeros((2, LANES, LANES))
    nodes[0, :NODES, :NODES] = np.kron(eye, derivative.T)
    nodes[1, :NODES, :NODES] = np.kron(derivative.T, eye)
    order = np.zeros((176, LANES))
    for qx in range(Q):
        for qy in range(Q):
            order[qx * 16 + qy, qy * Q + qx] = 1.0
    stack = np.concatenate([order, order @ nodes[0], order @ nodes[1]], axis=1)
    stack = np.concatenate(halves(stack), axis=0)
    plane = np.concatenate([nodes[0], nodes[1]], axis=1)
    mass = np.zeros((1, LANES), np.float32)
    mass[0, :NODES] = np.kron(weights, weights)
    stiff = (derivative.T * weights) @ derivative
    kb = np.zeros((2 * LANES, 2 * LANES))
    join = np.eye(2 * LANES)
    wx = np.zeros((1, 2 * LANES), np.float32)
    ends = []
    for t in range(2):
        for place in range(Q):
            low = t * LANES + place * Q
            kb[low : low + Q, low : low + Q] = stiff
            wx[0, low : low + Q] = weights
            ends.append(low)
    for left, right in zip(ends[:-1], ends[1:]):
        join[left + Q - 1, right] = 1.0
        join[right, left + Q - 1] = 1.0
    return dict(
        table=table, stack=stack, dz=halves(span_slope), plane=halves(plane), mass=mass,
        kb=kb.astype(np.float32), near=(kb @ join - kb).astype(np.float32), wx=wx,
        stiff=stiff.tolist(), weights=weights.tolist(),
    )


def local(adjoint_velocity, base_flow, column_widths, row_heights, base_phase):
    tables = make_tables()
    elem_count = lax.axis_size("elem")
    ints = jnp.stack([lax.axis_index("four").astype(jnp.int32), base_phase[0]])
    send = pack(adjoint_velocity)
    arrived = lax.all_to_all(send, "four", split_axis=0, concat_axis=0, tiled=True)
    fields, *turned = base_stage(
        ints, column_widths, row_heights, base_flow, jnp.asarray(tables["table"]),
        jnp.asarray(tables["stack"]), *(jnp.asarray(a) for a in tables["dz"]),
    )
    source = lines_stage(
        ints, column_widths, row_heights, arrived, fields, turned,
        *(jnp.asarray(a) for a in tables["plane"]), jnp.asarray(tables["mass"]),
    )
    own = lax.all_to_all(source, "four", split_axis=0, concat_axis=0, tiled=True)
    up = [(i, i + 1) for i in range(elem_count - 1)]
    left = lax.ppermute(own[COLUMNS - GHOST :], "elem", up)
    right = lax.ppermute(own[:GHOST], "elem", [(j, i) for i, j in up])
    v0, v1, v2, moments = krylov_stage(
        tables["stiff"], tables["weights"], ints, row_heights, place_stage(own), own, left, right,
        jnp.asarray(tables["kb"]), jnp.asarray(tables["near"]), jnp.asarray(tables["wx"]), elem_count,
    )
    moments = lax.all_to_all(moments, "elem", split_axis=0, concat_axis=0, tiled=True)
    return finish(moments, unpack(v0, v1, v2))


def solution(mesh):
    split_spec = P(None, None, None, ("elem", "four"))
    return jax.shard_map(
        local,
        mesh=mesh,
        in_specs=(split_spec, split_spec, P("elem"), P(), P()),
        out_specs=split_spec,
        check_vma=False,
    )
```

```python
import jax
import jax.numpy as jnp
import numpy as np
from jax import lax
from jax.experimental import pallas as pl
from jax.experimental.pallas import tpu as pltpu
from jax.sharding import PartitionSpec as P

Q = 11
PLANES = 256
PEERS = 16
LOCAL = 16
COLUMNS = 16
GHOST = 3
ROWS = 21
NODES = Q * Q
LANES = 128
PITCH = 17
FACE = ROWS * Q
TILES = 11
NU = 0.005
DT = 0.01
SIGMA = 1.0 / (NU * DT)
HIGHEST = lax.Precision.HIGHEST
F32 = jnp.float32
BF16 = jnp.bfloat16


def legendre_values(points, node_count):
    table_rows = np.zeros((points.shape[0], node_count))
    table_rows[:, 0] = 1.0
    table_rows[:, 1] = points
    for degree_now in range(2, node_count):
        table_rows[:, degree_now] = (
            (2 * degree_now - 1) * points * table_rows[:, degree_now - 1]
            - (degree_now - 1) * table_rows[:, degree_now - 2]
        ) / degree_now
    return table_rows


def gll_tables(node_count):
    degree = node_count - 1
    points = np.cos(np.pi * np.arange(node_count) / degree)
    for newton_step in range(60):
        legendre = legendre_values(points, node_count)
        points = points - (points * legendre[:, degree] - legendre[:, degree - 1]) / (
            node_count * legendre[:, degree]
        )
    legendre = legendre_values(points, node_count)
    weights = 2.0 / (degree * node_count * legendre[:, degree] ** 2)
    points = points[::-1]
    weights = weights[::-1]
    end_values = legendre[::-1, degree]
    derivative = np.zeros((node_count, node_count))
    for row_index in range(node_count):
        for column in range(node_count):
            if row_index != column:
                derivative[row_index, column] = end_values[row_index] / (
                    end_values[column] * (points[row_index] - points[column])
                )
    derivative[0, 0] = -degree * node_count / 4.0
    derivative[degree, degree] = degree * node_count / 4.0
    return derivative, weights


def fourier_table(plane_count):
    positions = np.arange(plane_count)
    basis_rows = np.zeros((plane_count, plane_count))
    basis_rows[0] = 1.0 / np.sqrt(plane_count)
    basis_rows[1] = np.cos(np.pi * positions) / np.sqrt(plane_count)
    for wave_index in range(1, plane_count // 2):
        angle = 2.0 * np.pi * wave_index * positions / plane_count
        basis_rows[2 * wave_index] = np.sqrt(2.0 / plane_count) * np.cos(angle)
        basis_rows[2 * wave_index + 1] = np.sqrt(2.0 / plane_count) * np.sin(angle)
    wave_counts = np.arange(plane_count) // 2
    wave_counts[1] = plane_count // 2
    wave_counts[0] = 0
    wavenumbers = 2.0 * np.pi * wave_counts / (plane_count / 64.0)
    rotate = np.zeros((plane_count, plane_count))
    for wave_index in range(1, plane_count // 2):
        rotate[2 * wave_index, 2 * wave_index + 1] = wavenumbers[2 * wave_index]
        rotate[2 * wave_index + 1, 2 * wave_index] = -wavenumbers[2 * wave_index]
    return basis_rows, rotate.T @ basis_rows, basis_rows.T @ rotate @ basis_rows


def halves(array):
    high = np.asarray(array, np.float32).astype(jnp.bfloat16)
    low = (np.asarray(array, np.float64) - high.astype(np.float64)).astype(jnp.bfloat16)
    return high, low


def split(value):
    high = value.astype(BF16)
    return high, (value - high.astype(F32)).astype(BF16)


def dot(left, right):
    return jnp.dot(left, right, preferred_element_type=F32)


def dot3(left_high, left_low, high, low):
    half = left_high.shape[0] // 2
    parts = [slice(0, half), slice(half, None)]
    totals = [dot(left_high[p], low) for p in parts]
    totals = [t + dot(left_low[p], high) for t, p in zip(totals, parts)]
    return [t + dot(left_high[p], high) for t, p in zip(totals, parts)]


def dot_full(left, right):
    return jnp.dot(left, right, precision=HIGHEST, preferred_element_type=F32)


def in_hbm(array):
    return pltpu.with_memory_space_constraint(array, pltpu.HBM)


def to_groups(array):
    array = jnp.transpose(array, (0, 2, 1, 3)).reshape(3, Q, 2, Q, 2, LANES)
    return jnp.transpose(array, (0, 1, 3, 4, 2, 5)).reshape(3, NODES, 4, LANES)


def from_groups(array):
    array = jnp.transpose(array.reshape(3, Q, Q, 2, 2, LANES), (0, 1, 4, 2, 3, 5))
    return jnp.transpose(array.reshape(3, Q, 2, COLUMNS * Q * LOCAL), (0, 2, 1, 3))


def lane_ids(shape):
    return lax.broadcasted_iota(jnp.int32, shape, len(shape) - 1)


def turn(value, shift):
    shift = shift % LANES
    return value if shift == 0 else pltpu.roll(value, shift, value.ndim - 1)


def block_transpose(arrays, places, offset=0, first=0):
    lane = lane_ids(arrays[0].shape)
    turned = [turn(array, Q * (first + k) - offset) for k, array in enumerate(arrays)]
    results = []
    for place in places:
        distance = (lane - Q * place) & (LANES - 1)
        chosen = turned[0]
        for k in range(1, len(turned)):
            chosen = jnp.where(distance >= Q * (first + k), turned[k], chosen)
        inside = distance < Q * (first + len(turned))
        if first:
            inside = inside & (distance >= Q * first)
        chosen = jnp.where(inside, chosen, 0.0)
        results.append(turn(chosen, -Q * place))
    return results


def pack_body(in_ref, out_ref, flat, scr0, scr1):
    lane = lane_ids((16, LANES))
    scratches = (scr0, scr1)
    tiles = COLUMNS * Q * LOCAL // LANES
    for qy in range(Q):
        for pair in range(Q):
            flat[pair, pl.ds(qy, 4, stride=16), :] = in_ref[0, qy * Q + pair]
    for ey in range(2):
        def read(tile):
            low = (tile % 2) * 32 + ey * 16
            return flat[tile // 2, low : low + 16, :]

        for j in range(LOCAL):
            for t in range(2):
                offset = j * COLUMNS * Q + NODES * t
                tile, shift = offset // LANES, offset % LANES
                first = read(tile)
                if shift and tile + 1 < tiles:
                    first = jnp.where(lane >= shift, first, read(tile + 1))
                scratches[t][ey, j * PITCH : j * PITCH + 16, :] = turn(first, -shift)
    for ey in range(2):
        for t in range(2):
            rows = [scratches[t][ey, pl.ds(qy, LOCAL, stride=PITCH), :] for qy in range(Q)]
            for place, value in enumerate(block_transpose(rows, range(Q if t == 0 else COLUMNS - Q))):
                out_ref[Q * t + place, 0, ey] = value


def pack(adjoint):
    return pl.pallas_call(
        pack_body,
        grid=(3,),
        in_specs=[pl.BlockSpec((1, NODES, 4, LANES), lambda i: (i, 0, 0, 0))],
        out_specs=pl.BlockSpec((PEERS, 1, 2, LOCAL, LANES), lambda i: (0, i, 0, 0, 0)),
        out_shape=jax.ShapeDtypeStruct((PEERS, 3, 2, LOCAL, LANES), F32),
        scratch_shapes=[
            pltpu.VMEM((Q, 64, LANES), F32),
            pltpu.VMEM((2, LOCAL * PITCH, LANES), F32),
            pltpu.VMEM((2, LOCAL * PITCH, LANES), F32),
        ],
        compiler_params=pltpu.CompilerParams(vmem_limit_bytes=24 * 2**20),
        name="pack",
    )(in_hbm(to_groups(adjoint)))


def base_body(ints, widths, heights, base_ref, table_ref, stack_ref, dzh_ref, dzl_ref,
              field_ref, fgh_ref, fgl_ref, fh_ref, fl_ref, scr):
    step = pl.program_id(0)

    @pl.when(step == 0)
    def _():
        scr[...] = jnp.zeros_like(scr)
        rows = pltpu.roll(table_ref[...], (PLANES - ints[1]) % PLANES, 0)
        for k in range(2):
            high, low = split(rows[:, k * PLANES : (k + 1) * PLANES])
            fgh_ref[k * PLANES : (k + 1) * PLANES, :] = high
            fgl_ref[k * PLANES : (k + 1) * PLANES, :] = low
        high, low = split(jnp.transpose(rows[:, :PLANES]))
        fh_ref[...] = high
        fl_ref[...] = low

    for qx in range(Q):
        part = base_ref[0, 0, :, qx * PLANES : (qx + 1) * PLANES]
        scr[qx * 16 : qx * 16 + Q, :] = part
        scr[176 + qx * 16 : 176 + qx * 16 + Q, :] = part
    mixed = lax.dot_general(
        scr[...], stack_ref[...], (((0,), (0,)), ((), ())), preferred_element_type=F32
    )
    plain = mixed[:, :LANES]
    field_ref[0, 0, 0] = plain
    field_ref[1, 0, 0] = mixed[:, LANES : 2 * LANES] * (2.0 / widths[ints[0]])
    field_ref[2, 0, 0] = mixed[:, 2 * LANES :] * (2.0 / heights[step % 2])
    exact = plain.astype(BF16)
    field_ref[3, 0, 0] = dot(dzh_ref[...], exact) + dot(dzl_ref[...], exact)


def base_stage(ints, widths, heights, base, table, stack, dz_high, dz_low):
    smem = pl.BlockSpec(memory_space=pltpu.SMEM)

    def whole(shape):
        return pl.BlockSpec(shape, lambda i: (0,) * len(shape))

    return pl.pallas_call(
        base_body,
        grid=(6,),
        in_specs=[
            smem, smem, smem,
            pl.BlockSpec((1, 1, Q, Q * PLANES), lambda i: (i // 2, i % 2, 0, 0)),
            whole(table.shape), whole(stack.shape), whole(dz_high.shape), whole(dz_low.shape),
        ],
        out_specs=[
            pl.BlockSpec((4, 1, 1, PLANES, LANES), lambda i: (0, i // 2, i % 2, 0, 0)),
            whole((2 * PLANES, PLANES)), whole((2 * PLANES, PLANES)),
            whole((PLANES, PLANES)), whole((PLANES, PLANES)),
        ],
        out_shape=[
            jax.ShapeDtypeStruct((4, 3, 2, PLANES, LANES), F32),
            jax.ShapeDtypeStruct((2 * PLANES, PLANES), BF16),
            jax.ShapeDtypeStruct((2 * PLANES, PLANES), BF16),
            jax.ShapeDtypeStruct((PLANES, PLANES), BF16),
            jax.ShapeDtypeStruct((PLANES, PLANES), BF16),
        ],
        scratch_shapes=[pltpu.VMEM((352, PLANES), BF16)],
        name="base_stage",
    )(ints, widths, heights, base, table, stack, dz_high, dz_low)


def lines_body(ints, widths, heights, in_ref, field_hbm, fgh_ref, fgl_ref, fh_ref, fl_ref,
               dh_ref, dl_ref, mass_ref, out_ref, fields, lines, slopes, packed, sems):
    copies = [
        pltpu.make_async_copy(field_hbm.at[k], fields.at[k], sems.at[k]) for k in range(4)
    ]
    for copy in copies:
        copy.start()
    width = widths[ints[0]]
    pairs = [((2 * p) // 2, (2 * p) % 2, (2 * p + 1) % 2) for p in range(3)]
    double_dh = jnp.concatenate([dh_ref[...], dh_ref[...]], axis=0)

    def coeffs(c, ey):
        return in_ref[:, c, ey].reshape(PLANES, LANES)

    for c, _, _ in pairs:
        high, low = split(jnp.concatenate([coeffs(c, 0), coeffs(c, 1)], axis=1))
        both = dot3(fgh_ref[...], fgl_ref[...], high, low)
        for ey in range(2):
            line = both[0][:, ey * LANES : (ey + 1) * LANES]
            lines[c, ey] = line
            slopes[2, c, ey] = both[1][:, ey * LANES : (ey + 1) * LANES]
            high_line, low_line = split(line)
            wide = jnp.concatenate([high_line, low_line], axis=1)
            parts = [slice(0, LANES), slice(LANES, PLANES)]
            planes = [dot(wide[p], double_dh) for p in parts]
            planes = [v + dot(high_line[p], dl_ref[...]) for v, p in zip(planes, parts)]
            for plane, p in zip(planes, parts):
                slopes[0, c, ey, p] = plane[:, :LANES] * (2.0 / width)
                slopes[1, c, ey, p] = plane[:, LANES:] * (2.0 / heights[ey])
    copies[0].wait()
    copies[1].wait()
    lane = lane_ids((PLANES, LANES))
    for c in range(3):
        if c == 1:
            copies[2].wait()
            copies[3].wait()
        pieces = []
        for ey in range(2):
            total = fields[0, 0, ey] * slopes[0, c, ey]
            for d in range(1, 3):
                total = total + fields[0, d, ey] * slopes[d, c, ey]
            for d in range(3):
                total = total - lines[d, ey] * fields[1 + c, d, ey]
            pieces.append(total)
        high, low = split(jnp.concatenate(pieces, axis=1))
        hat = jnp.concatenate(dot3(fh_ref[...], fl_ref[...], high, low), axis=0)
        values = []
        for ey in range(2):
            mass = mass_ref[...] * (width * heights[ey] * 0.25)
            source = SIGMA * coeffs(c, ey) + hat[:, ey * LANES : (ey + 1) * LANES] * (1.0 / NU)
            values.append(mass * source)
        values[0] = values[0] + jnp.where(lane >= NODES - Q, turn(values[1], NODES - Q), 0.0)
        for ey in range(2):
            packed[c, ey] = values[ey]
    lane = lane_ids((PEERS, 8, LANES))
    pieces = []
    for half in range(2):
        for c in range(3):
            base = (half * 3 + c) * FACE
            for ey in range(2):
                value = packed[c, ey].reshape(PEERS, 2, 8, LANES)[:, half]
                pieces.append((base + NODES * ey, turn(value, base + (NODES - Q) * ey)))
    pieces.append((6 * FACE, jnp.full((PEERS, 8, LANES), width, F32)))
    starts = [start for start, _ in pieces] + [TILES * LANES]
    for tile in range(TILES):
        low, high = tile * LANES, (tile + 1) * LANES
        chosen = None
        for k, (start, value) in enumerate(pieces):
            if start < high and starts[k + 1] > low:
                chosen = value if chosen is None else jnp.where(lane >= start - low, value, chosen)
        out_ref[:, tile] = chosen


def lines_stage(ints, widths, heights, arrived, fields, tables, d_high, d_low, mass):
    smem = pl.BlockSpec(memory_space=pltpu.SMEM)

    def whole(array):
        return pl.BlockSpec(array.shape, lambda i: (0,) * array.ndim)

    return pl.pallas_call(
        lines_body,
        grid=(1,),
        in_specs=[smem, smem, smem, whole(arrived), pl.BlockSpec(memory_space=pl.ANY)]
        + [whole(a) for a in tables] + [whole(d_high), whole(d_low), whole(mass)],
        out_specs=pl.BlockSpec((PEERS, TILES, 8, LANES), lambda i: (0, 0, 0, 0)),
        out_shape=jax.ShapeDtypeStruct((PEERS, TILES, 8, LANES), F32),
        scratch_shapes=[
            pltpu.VMEM((4, 3, 2, PLANES, LANES), F32),
            pltpu.VMEM((3, 2, PLANES, LANES), F32),
            pltpu.VMEM((3, 3, 2, PLANES, LANES), F32),
            pltpu.VMEM((3, 2, PLANES, LANES), F32),
            pltpu.SemaphoreType.DMA((4,)),
        ],
        compiler_params=pltpu.CompilerParams(vmem_limit_bytes=24 * 2**20),
        name="lines_stage",
    )(*map(in_hbm, (ints, widths, heights)), arrived, in_hbm(fields), *map(in_hbm, tables), d_high, d_low, mass)


def join_columns(chunks, offset, partial=()):
    lane = (lane_ids(chunks[0].shape) - offset) & (LANES - 1)
    place = lane - Q * ((lane * 5958) >> 16)
    at_first = (place == 0) & (lane < NODES)
    at_last = (place == Q - 1) & (lane < NODES)
    results = []
    for k, chunk in enumerate(chunks):
        extra = 0.0
        if k > 0:
            extra = jnp.where(at_first, turn(chunks[k - 1], -(Q - 1)), extra)
        if k + 1 < len(chunks):
            extra = jnp.where(at_last, turn(chunks[k + 1], Q - 1), extra)
        results.append(extra if k in partial else chunk + extra)
    return results


def windows(refs, start):
    tile, offset = start // LANES, start % LANES
    chunks = [ref[tile] for ref in refs]
    if offset:
        lane = lane_ids((8, LANES))
        chunks = [
            jnp.where(lane >= offset, chunk, ref[tile + 1]) for chunk, ref in zip(chunks, refs)
        ]
    return chunks, offset


def face_parts():
    for comp in range(3):
        for half in range(2):
            for ey in range(2):
                start = (half * 3 + comp) * FACE + (NODES - Q) * ey
                yield comp, start, range(ey, Q), (Q - 1) * ey * LOCAL + half * 8


def place_body(own_ref, out_ref):
    refs = [own_ref.at[k] for k in range(COLUMNS)]
    cut = Q - GHOST
    for comp, start, places, base in face_parts():
        chunks, offset = windows(refs, start)
        chunks = join_columns(chunks, offset)
        sides = [
            block_transpose(chunks[:cut], places, offset, GHOST),
            block_transpose(chunks[cut:], places, offset),
        ]
        for t, values in enumerate(sides):
            for qy, value in zip(places, values):
                row = base + qy * LOCAL
                out_ref[comp, row : row + 8, t * LANES : (t + 1) * LANES] = value


def place_stage(own):
    return pl.pallas_call(
        place_body,
        grid=(1,),
        in_specs=[pl.BlockSpec(own.shape, lambda i: (0, 0, 0, 0))],
        out_specs=pl.BlockSpec((3, ROWS * LOCAL, 2 * LANES), lambda i: (0, 0, 0)),
        out_shape=jax.ShapeDtypeStruct((3, ROWS * LOCAL, 2 * LANES), F32),
        compiler_params=pltpu.CompilerParams(vmem_limit_bytes=24 * 2**20),
        name="place_stage",
    )(own)


def split3(value):
    high = value.astype(BF16)
    rest = value - high.astype(F32)
    mid = rest.astype(BF16)
    return high, mid, (rest - mid.astype(F32)).astype(BF16)


def dot_split(source, target, operator):
    cut = 176
    parts = [slice(0, cut), slice(cut, ROWS * LOCAL)]
    pieces = [split3(source[p, :]) for p in parts]
    totals = [None, None]
    for left, right in ((2, 0), (0, 2), (1, 1), (1, 0), (0, 1), (0, 0)):
        for k in range(2):
            value = dot(pieces[k][left], operator[right])
            totals[k] = value if totals[k] is None else totals[k] + value
    for k in range(2):
        target[parts[k], :] = totals[k]


def stiff_rows(stiff, values):
    middle = Q // 2
    even = [values[m] + values[Q - 1 - m] for m in range(middle)] + [values[middle]]
    odd = [values[m] - values[Q - 1 - m] for m in range(middle)]
    results = [None] * Q
    for row in range(middle + 1):
        total = None
        for m in range(middle + 1):
            factor = stiff[row][m] if m == middle or row == middle else (
                0.5 * (stiff[row][m] + stiff[row][Q - 1 - m])
            )
            term = factor * even[m]
            total = term if total is None else total + term
        if row == middle:
            results[row] = total
            continue
        other = None
        for m in range(middle):
            term = (0.5 * (stiff[row][m] - stiff[row][Q - 1 - m])) * odd[m]
            other = term if other is None else other + term
        results[row] = total + other
        results[Q - 1 - row] = total - other
    return results


def krylov_body(stiff_y, weights, ints, heights, placed_ref, own_ref, left_ref, right_ref, kb_ref, kn_ref, wx_ref,
                v0_ref, v1_ref, v2_ref, mom_ref, kxs, kbs, vec, prod, tmp):
    column_refs = (
        [left_ref.at[k] for k in range(GHOST)]
        + [own_ref.at[k] for k in range(COLUMNS)]
        + [right_ref.at[k] for k in range(GHOST)]
    )

    lane = lane_ids((8, LANES))
    widths = [ref[TILES - 1, :, LANES - 1 :] for ref in column_refs]
    zero = jnp.zeros((8, 1), F32)
    widths = [zero] + widths + [zero]
    for t in range(2):
        here = jnp.zeros((8, LANES), F32)
        near = here
        for place in range(Q):
            k = Q * t + place + 1
            low, high = Q * place, Q * place + Q - 1
            here = jnp.where((lane >= low) & (lane <= high), widths[k], here)
            near = jnp.where(lane == low, widths[k - 1], near)
            near = jnp.where(lane == high, widths[k + 1], near)
        vec[0, :, t * LANES : (t + 1) * LANES] = here
        vec[1, :, t * LANES : (t + 1) * LANES] = near
    here, near = vec[0], vec[1]
    line = lane_ids((8, 2 * LANES))
    own = ((line >= GHOST * Q) & (line < NODES)) | (
        (line >= LANES) & (line < LANES + (Q - GHOST) * Q)
    )
    own = own.astype(F32)
    mass_x = here * wx_ref[...]
    vec[2] = mass_x * own
    vec[1] = mass_x + near * wx_ref[...]
    vec[3] = own * jnp.where(near > 0.0, 0.5, 1.0)
    inverse, inverse_near = (
        jnp.where(value > 0.0, 1.0 / jnp.where(value > 0.0, value, 1.0), 0.0)[0:1]
        for value in (here, near)
    )
    scaled = kb_ref[...] * inverse
    for k, part in enumerate(split3(scaled + kn_ref[...] * inverse_near)):
        kxs[k] = part
    for k, part in enumerate(split3(scaled * own[0:1])):
        kbs[k] = part

    h0, h1 = heights[0], heights[1]
    inverse_y = (1.0 / h0, 1.0 / h1)
    mass_y = []
    for y in range(ROWS):
        if y < Q - 1:
            mass_y.append(h0 * weights[y])
        elif y == Q - 1:
            mass_y.append((h0 + h1) * weights[0])
        else:
            mass_y.append(h1 * weights[y - Q + 1])

    def apply(source, target, tmp, prod, mass_row, low_key):
        for half in range(2):
            plane = ints[0] * LOCAL + half * 8 + lax.broadcasted_iota(jnp.int32, (8, LANES), 0)
            kappa = jnp.where(plane == 1, PLANES // 2, plane >> 1).astype(F32)
            beta = kappa * (2.0 * np.pi / (PLANES / 64.0))
            lam = (beta * beta + SIGMA) * 0.25
            square = cross = None
            for t in range(2):
                lanes = slice(t * LANES, (t + 1) * LANES)
                mass_x = vec[mass_row, :, lanes]
                shift = lam * mass_x
                weight = vec[3, :, lanes]
                here_square = here_cross = None
                shared = None
                for ey in range(2):
                    rows = [
                        slice(y * LOCAL + half * 8, y * LOCAL + half * 8 + 8)
                        for y in range((Q - 1) * ey, (Q - 1) * ey + Q)
                    ]
                    values = [source[r, lanes] for r in rows]
                    scale = mass_x * inverse_y[ey]
                    stiff = [scale * value for value in stiff_rows(stiff_y, values)]
                    if ey == 0:
                        shared = stiff.pop()
                    else:
                        stiff[0] = stiff[0] + shared
                    for k, part in enumerate(stiff):
                        y, value = (Q - 1) * ey + k, values[k]
                        image = mass_y[y] * (tmp[rows[k], lanes] + shift * value) + part
                        if target is not None:
                            target[rows[k], lanes] = image
                        one, two = value * value, value * image
                        here_square = one if here_square is None else here_square + one
                        here_cross = two if here_cross is None else here_cross + two
                here_square = here_square * weight
                if target is not None:
                    here_cross = here_cross * weight
                square = here_square if square is None else square + here_square
                cross = here_cross if cross is None else cross + here_cross
            prod[low_key * LOCAL + half * 8 : low_key * LOCAL + half * 8 + 8, :] = square
            prod[(low_key + 1) * LOCAL + half * 8 : (low_key + 1) * LOCAL + half * 8 + 8, :] = cross

    cut = Q - GHOST - 1
    for comp, start, places, base in face_parts():
        left, offset = windows(column_refs[: GHOST + 1], start)
        right, _ = windows(column_refs[-GHOST - 1 :], start)
        sides = [
            block_transpose(join_columns(left, offset, (GHOST,)), places, offset),
            block_transpose(join_columns(right, offset, (0,)), places, offset, cut),
        ]
        for t, values in enumerate(sides):
            lanes = slice(t * LANES, (t + 1) * LANES)
            for qy, value in zip(places, values):
                rows = slice(base + qy * LOCAL, base + qy * LOCAL + 8)
                v0_ref[comp, rows, lanes] = placed_ref[comp, rows, lanes] + value
    vectors = (v0_ref, v1_ref, v2_ref)
    tasks = [(stage, comp) for stage in range(3) for comp in range(3)]

    def multiply(stage, comp):
        dot_split(vectors[stage].at[comp], tmp.at[comp], kxs if stage < 2 else kbs)

    multiply(*tasks[0])
    for k, (stage, comp) in enumerate(tasks):
        if k + 1 < len(tasks):
            multiply(*tasks[k + 1])
        target = vectors[stage + 1].at[comp] if stage < 2 else None
        mass_row = 1 if stage < 2 else 2
        apply(vectors[stage].at[comp], target, tmp.at[comp], prod.at[comp], mass_row, 2 * stage)
    for comp in range(3):
        prod[comp, 6 * LOCAL :, :] = jnp.zeros((LANES - 6 * LOCAL, LANES), F32)
        row = lax.dot_general(
            jnp.ones((8, LANES), F32), prod[comp], (((1,), (1,)), ((), ())),
            precision=HIGHEST, preferred_element_type=F32,
        )
        mom_ref[:, comp : comp + 1, :] = jnp.broadcast_to(
            row[0:1][None], (mom_ref.shape[0], 1, LANES)
        )


def krylov_stage(stiff_y, weights, ints, heights, placed, own, left, right, kb, near, wx, peers):
    smem = pl.BlockSpec(memory_space=pltpu.SMEM)

    def whole(array):
        return pl.BlockSpec(array.shape, lambda i: (0,) * array.ndim)

    def chunk(count):
        return pl.BlockSpec((count, TILES, 8, LANES), lambda i: (0, 0, 0, 0))

    vector = pl.BlockSpec((3, ROWS * LOCAL, 2 * LANES), lambda i: (0, 0, 0))
    shape = jax.ShapeDtypeStruct((3, ROWS * LOCAL, 2 * LANES), F32)

    def body(*refs):
        krylov_body(stiff_y, weights, *refs)

    return pl.pallas_call(
        body,
        grid=(1,),
        in_specs=[smem, smem, vector, chunk(COLUMNS), chunk(GHOST), chunk(GHOST), whole(kb), whole(near), whole(wx)],
        out_specs=[vector, vector, vector, pl.BlockSpec((peers, 8, LANES), lambda i: (0, 0, 0))],
        out_shape=[shape, shape, shape, jax.ShapeDtypeStruct((peers, 8, LANES), F32)],
        scratch_shapes=[
            pltpu.VMEM((3, 2 * LANES, 2 * LANES), BF16),
            pltpu.VMEM((3, 2 * LANES, 2 * LANES), BF16),
            pltpu.VMEM((4, 8, 2 * LANES), F32),
            pltpu.VMEM((3, LANES, LANES), F32),
            pltpu.VMEM((3, ROWS * LOCAL, 2 * LANES), F32),
        ],
        compiler_params=pltpu.CompilerParams(vmem_limit_bytes=24 * 2**20),
        name="krylov_stage",
    )(in_hbm(ints), in_hbm(heights), placed, own, left, right, kb, near, wx)


def unpack_body(v0_ref, v1_ref, v2_ref, out_ref, scr, flat):
    lane = lane_ids((16, LANES))
    run = COLUMNS * Q // 2
    for k, vector in enumerate((v0_ref, v1_ref, v2_ref)):
        for y in range(ROWS):
            rows = slice(y * LOCAL, (y + 1) * LOCAL)
            for t in range(2):
                value = vector[0, rows, t * LANES : (t + 1) * LANES]
                if y <= Q - 1:
                    scr[0, t, pl.ds(y, LOCAL, stride=PITCH), :] = value
                if y >= Q - 1:
                    scr[1, t, pl.ds(y - Q + 1, LOCAL, stride=PITCH), :] = value
        for ey in range(2):
            turned = []
            for r in range(2 * LOCAL):
                start = GHOST * Q if r % 2 == 0 else 0
                value = scr[ey, r % 2, (r // 2) * PITCH : (r // 2) * PITCH + 16, :]
                turned.append(turn(value, run * r - start))
            for tile in range(COLUMNS * Q * LOCAL // LANES):
                low, high = tile * LANES // run, (tile * LANES + LANES - 1) // run
                value = turned[low]
                for r in range(low + 1, high + 1):
                    value = jnp.where(lane >= run * r - LANES * tile, turned[r], value)
                place = (tile % 2) * 32 + ey * 16
                flat[tile // 2, place : place + 16, :] = value
        for qy in range(Q):
            for pair in range(Q):
                out_ref[0, k, qy * Q + pair] = flat[pair, pl.ds(qy, 4, stride=16), :]


def unpack(v0, v1, v2):
    vector = pl.BlockSpec((1, ROWS * LOCAL, 2 * LANES), lambda i: (i, 0, 0))
    target = pl.BlockSpec((1, 3, NODES, 4, LANES), lambda i: (i, 0, 0, 0, 0))
    shape = pltpu.HBM((3, 3, NODES, 4, LANES), F32)
    return pl.pallas_call(
        unpack_body,
        grid=(3,),
        in_specs=[vector] * 3,
        out_specs=target,
        out_shape=shape,
        scratch_shapes=[
            pltpu.VMEM((2, 2, LOCAL * PITCH, LANES), F32),
            pltpu.VMEM((Q, 64, LANES), F32),
        ],
        compiler_params=pltpu.CompilerParams(vmem_limit_bytes=24 * 2**20),
        name="unpack",
    )(v0, v1, v2)


def finish_body(mom_ref, u_ref, out_ref, coef):
    comp = pl.program_id(0)
    tiles = COLUMNS * Q * LOCAL // LANES

    @pl.when(comp == 0)
    def _():
        total = jnp.sum(mom_ref[...], axis=0)
        used = (lane_ids((8, LANES)) < LOCAL) & (
            lax.broadcasted_iota(jnp.int32, (8, LANES), 0) < 3
        )
        m = [jnp.where(used, turn(total, -LOCAL * k), 1.0) for k in range(6)]
        inv = 1.0 / m[0]
        m = [value * inv for value in m]
        d0, d1, d2 = (1.0 / jnp.sqrt(m[k]) for k in (1, 3, 5))
        g0, g1, g2 = d0, m[1] * d1, m[2] * d2
        l10 = m[2] * d0 * d1
        l20 = m[3] * d0 * d2
        k21 = m[4] * d1 * d2
        p1 = 1.0 - l10 * l10
        e = k21 - l20 * l10
        l21 = e / p1
        p2 = 1.0 - l20 * l20 - l21 * e
        y1 = g1 - l10 * g0
        y2 = g2 - l20 * g0 - l21 * y1
        z2 = y2 / p2
        z1 = y1 / p1 - l21 * z2
        z0 = g0 - l10 * z1 - l20 * z2
        lane = lane_ids((8, LANES))
        for k, value in enumerate((z0 * d0, z1 * d1, z2 * d2)):
            wide = [jnp.broadcast_to(value[:, j : j + 1], (8, LANES)) for j in range(LOCAL)]
            for tile in range(tiles):
                low = tile * LANES // (COLUMNS * Q)
                high = (tile * LANES + LANES - 1) // (COLUMNS * Q)
                chosen = wide[low]
                if high > low:
                    chosen = jnp.where(lane >= COLUMNS * Q * high - LANES * tile, wide[high], chosen)
                coef[k, tile] = chosen

    upper = lax.broadcasted_iota(jnp.int32, (4, LANES), 0) >= 2
    for pair in range(Q):
        factors = []
        for k in range(3):
            one, two = (
                jnp.broadcast_to(coef[k, 2 * pair + side, pl.ds(comp, 1), :], (4, LANES))
                for side in range(2)
            )
            factors.append(jnp.where(upper, two, one))
        for qy in range(Q):
            group = qy * Q + pair
            out_ref[0, group] = (
                factors[0] * u_ref[0, 0, group]
                + factors[1] * u_ref[0, 1, group]
                + factors[2] * u_ref[0, 2, group]
            )


def finish(moments, vectors):
    out = pl.pallas_call(
        finish_body,
        grid=(3,),
        in_specs=[
            pl.BlockSpec(moments.shape, lambda i: (0, 0, 0)),
            pl.BlockSpec((1, 3, NODES, 4, LANES), lambda i: (i, 0, 0, 0, 0)),
        ],
        out_specs=pl.BlockSpec((1, NODES, 4, LANES), lambda i: (i, 0, 0, 0)),
        out_shape=jax.ShapeDtypeStruct((3, NODES, 4, LANES), F32),
        scratch_shapes=[pltpu.VMEM((3, COLUMNS * Q * LOCAL // LANES, 8, LANES), F32)],
        compiler_params=pltpu.CompilerParams(vmem_limit_bytes=24 * 2**20),
        name="finish",
    )(moments, in_hbm(vectors))
    return from_groups(out)


def make_tables():
    derivative, weights = gll_tables(Q)
    basis, basis_slope, span_slope = fourier_table(PLANES)
    table = np.concatenate([basis.T, basis_slope.T], axis=1)
    table = table.astype(np.float32)
    eye = np.eye(Q)
    nodes = np.zeros((2, LANES, LANES))
    nodes[0, :NODES, :NODES] = np.kron(eye, derivative.T)
    nodes[1, :NODES, :NODES] = np.kron(derivative.T, eye)
    order = np.zeros((176, LANES))
    for qx in range(Q):
        for qy in range(Q):
            order[qx * 16 + qy, qy * Q + qx] = 1.0
    stack = np.concatenate([order, order @ nodes[0], order @ nodes[1]], axis=1)
    stack = np.concatenate(halves(stack), axis=0)
    plane = np.concatenate([nodes[0], nodes[1]], axis=1)
    mass = np.zeros((1, LANES), np.float32)
    mass[0, :NODES] = np.kron(weights, weights)
    stiff = (derivative.T * weights) @ derivative
    kb = np.zeros((2 * LANES, 2 * LANES))
    join = np.eye(2 * LANES)
    wx = np.zeros((1, 2 * LANES), np.float32)
    ends = []
    for t in range(2):
        for place in range(Q):
            low = t * LANES + place * Q
            kb[low : low + Q, low : low + Q] = stiff
            wx[0, low : low + Q] = weights
            ends.append(low)
    for left, right in zip(ends[:-1], ends[1:]):
        join[left + Q - 1, right] = 1.0
        join[right, left + Q - 1] = 1.0
    return dict(
        table=table, stack=stack, dz=halves(span_slope), plane=halves(plane), mass=mass,
        kb=kb.astype(np.float32), near=(kb @ join - kb).astype(np.float32), wx=wx,
        stiff=stiff.tolist(), weights=weights.tolist(),
    )


def local(adjoint_velocity, base_flow, column_widths, row_heights, base_phase):
    tables = make_tables()
    elem_count = lax.axis_size("elem")
    ints = jnp.stack([lax.axis_index("four").astype(jnp.int32), base_phase[0]])
    send = pack(adjoint_velocity)
    arrived = lax.all_to_all(send, "four", split_axis=0, concat_axis=0, tiled=True)
    fields, *turned = base_stage(
        ints, column_widths, row_heights, base_flow, jnp.asarray(tables["table"]),
        jnp.asarray(tables["stack"]), *(jnp.asarray(a) for a in tables["dz"]),
    )
    source = lines_stage(
        ints, column_widths, row_heights, arrived, fields, turned,
        *(jnp.asarray(a) for a in tables["plane"]), jnp.asarray(tables["mass"]),
    )
    own = lax.all_to_all(source, "four", split_axis=0, concat_axis=0, tiled=True)
    up = [(i, i + 1) for i in range(elem_count - 1)]
    left = lax.ppermute(own[COLUMNS - GHOST :], "elem", up)
    right = lax.ppermute(own[:GHOST], "elem", [(j, i) for i, j in up])
    v0, v1, v2, moments = krylov_stage(
        tables["stiff"], tables["weights"], ints, row_heights, place_stage(own), own, left, right,
        jnp.asarray(tables["kb"]), jnp.asarray(tables["near"]), jnp.asarray(tables["wx"]), elem_count,
    )
    moments = lax.all_to_all(moments, "elem", split_axis=0, concat_axis=0, tiled=True)
    return finish(moments, unpack(v0, v1, v2))


def solution(mesh):
    split_spec = P(None, None, None, ("elem", "four"))
    return jax.shard_map(
        local,
        mesh=mesh,
        in_specs=(split_spec, split_spec, P("elem"), P(), P()),
        out_specs=split_spec,
        check_vma=False,
    )
```
